32 devices in a mesh: tgt: 8 (over z, core), src: 4 (over y, x).
Axes of the slice: x: 2, y: 2, z: 4, core: 2. Of those that a mesh axis runs over, the one named last changes fastest.
Arguments:
- right_side: float32 [8192], P(('tgt', 'src')), may hold values from -50 to 50
- targets: float32 [3, 8192], P(None, ('tgt', 'src')), may hold values from -1 to 1
- source_nodes: float32 [3, 16, 8192], P(None, None, ('tgt', 'src')), may hold values from -1 to 1
- node_weights: float32 [16, 8192], P(None, ('tgt', 'src')), may hold values from -0.02734375 to 0.02734375
- near_list: int32 [2, 384], P(None, ('tgt', 'src')), may hold values from 0 to 31, as said below
- near_count: int32 [32], P(('tgt', 'src')), may hold values from 1 to 12, as said below
- row_basis: float32 [32, 32, 256], P(('tgt', 'src')), may hold values from -1 to 1
- column_basis: float32 [32, 32, 256], P(('tgt', 'src')), may hold values from -0.375 to 0.375
- coupling: float32 [8, 4, 8, 4, 1024], P('tgt', None, None, 'src'), may hold values from -0.109375 to 0.109375
Outputs:
- solution: float32 [8192], P(('tgt', 'src'))
The draws below stay inside these ranges and needn't reach their ends.
Inputs may be any that keep to these rules, and one draw needn't show every extreme that they name: `near_list`: for the device with tgt index i and src index j (slots j + i * 4 times 12 onward), every slot names a target cluster c with c // 4 = i and a source cluster d with d % 4 = j; the slots of one device name distinct pairs. `near_count`: some device has all 12 slots live.
All inputs are finite; a program needn't handle non-finite values.
Results may differ from the reference program's by a relative error of at most 0.0003.
Values sent between devices are 32-bit elements; how exact they have to be, the bound alone decides.
No kernel may reach another device: no remote copies, remote signals or barrier semaphores. Data moves between devices by JAX's collectives and lax.ppermute only.
A program may use at most 64 MiB of HBM per device.

```python
import jax
import jax.numpy as jnp
from jax import lax

LEAF = 256
Q = 16
R = 32
NEAR_MAX = 12
POINTS = 8192
N_TGT = 8
N_SRC = 4
DEVICES = 32


def near_layout(key):
    layout_key = jax.random.fold_in(key, 17)
    pair_key, light_key, heavy_key, pick_key = jax.random.split(layout_key, 4)
    device_ids = jnp.arange(DEVICES, dtype=jnp.int32)

    def device_pairs(device):
        return jax.random.permutation(jax.random.fold_in(pair_key, device), DEVICES)[:NEAR_MAX]
    chosen = jax.vmap(device_pairs)(device_ids).astype(jnp.int32)
    tgt_pos = device_ids // N_SRC
    src_pos = device_ids % N_SRC
    row_part = chosen // N_TGT
    column_part = chosen % N_TGT
    target_ids = tgt_pos[:, None] * N_SRC + row_part
    source_ids = column_part * N_SRC + src_pos[:, None]
    light_load = jax.random.randint(light_key, (DEVICES,), 1, NEAR_MAX // 3 + 1)
    heavy_slot = jax.random.randint(heavy_key, (DEVICES,), 0, 8) == 0
    counts = jnp.where(heavy_slot, NEAR_MAX, light_load)
    forced = jax.random.randint(pick_key, (), 0, DEVICES)
    counts = jnp.where(device_ids == forced, NEAR_MAX, counts)
    listing = jnp.stack([target_ids.reshape(-1), source_ids.reshape(-1)]).astype(jnp.int32)
    return (listing, counts.astype(jnp.int32))


def draw_near_list(key, part):
    return near_layout(key)[0]


def draw_near_count(key, part):
    return near_layout(key)[1]


def draw_right_side(key, part):
    first_key, second_key = jax.random.split(jax.random.fold_in(key, 5), 2)
    total_points = LEAF * DEVICES
    position = jnp.arange(total_points, dtype=jnp.float32) / (total_points - 1)
    rising = 0.1 * jnp.exp(jnp.log(3.0) * position)
    rough = jnp.exp(jax.random.uniform(second_key, (total_points,), jnp.float32, 0.0, jnp.log(10.0)))
    values = jax.random.truncated_normal(first_key, -4.0, 4.0, (total_points,), jnp.float32) * rising * rough
    return values


def strengthened(values, rng, source, target, blocks, factor):
    owner, partner = [(jnp.arange(values.shape[dim]) // (values.shape[dim] // blocks)).reshape([-1 if axis == dim else 1 for axis in range(values.ndim)]) for dim in (source, target)]
    chosen = jax.random.permutation(rng, blocks)[partner]
    strong = (owner == chosen) | (owner == (partner + blocks // 2) % blocks)
    return jnp.where(strong, factor * values, values)


def levels(stream_key, dims, shards, smallest, largest):
    loudness, own = 1.0, jax.random.fold_in(stream_key, 6)
    for dim, parts in shards:
        steps = jnp.exp(jax.random.uniform(jax.random.fold_in(own, dim), (parts,), jnp.float32, smallest / len(shards), largest / len(shards)))
        loudness = loudness * jnp.repeat(steps, dims[dim] // parts).reshape([-1 if axis == dim else 1 for axis in range(len(dims))])
    return loudness


def scatter_about(rng, shape, scale, most, shards=(), kind=jnp.bfloat16):
    values = jax.random.normal(rng, shape, jnp.float32) * scale
    if len(shards) > 0:
        values = levels(rng, shape, shards, -0.22, 0.18) * values
    return jnp.clip(values, min=-most, max=most).astype(kind)


def noise_with(stream_key, dims, spread, most, shards, heavy, kind=jnp.bfloat16):
    result = spread * jax.random.normal(stream_key, dims, jnp.float32)
    if shards:
        result = result * levels(stream_key, dims, shards, -0.22, 0.18)
    return jnp.clip(strengthened(result, jax.random.fold_in(stream_key, 3), *heavy), -most, most).astype(kind)


def setup_inputs(seed: int = 0) -> dict:
    arg_keys = jax.random.split(jax.random.key(seed), 10)
    return {
        "right_side": draw_right_side(jax.random.fold_in(arg_keys[9], 71), 0),
        "targets": jnp.clip(jax.random.uniform(arg_keys[1], (3, POINTS), jnp.float32, -1.0, 1.0) * levels(arg_keys[1], (3, POINTS), ((1, 32),), -0.4, 0.0), -1.0, 1.0),
        "source_nodes": jnp.clip(jax.random.uniform(arg_keys[2], (3, Q, POINTS), jnp.float32, -1.0, 1.0) * levels(arg_keys[2], (3, Q, POINTS), ((2, 32),), -0.4, 0.0), -1.0, 1.0),
        "node_weights": scatter_about(arg_keys[3], (Q, POINTS), (0.3 / (Q * LEAF) ** 0.5), 0.02734375, ((1, 32),), jnp.float32),
        "near_list": draw_near_list(jax.random.fold_in(arg_keys[9], 71), 0),
        "near_count": draw_near_count(jax.random.fold_in(arg_keys[9], 71), 0),
        "row_basis": scatter_about(arg_keys[6], (DEVICES, R, LEAF), R ** -0.5, 1.0, ((0, 32),), jnp.float32),
        "column_basis": scatter_about(arg_keys[7], (DEVICES, R, LEAF), LEAF ** -0.5, 0.375, ((0, 32),), jnp.float32),
        "coupling": noise_with(arg_keys[8], (N_TGT, N_SRC, N_TGT, N_SRC, R * R), (0.4 / (R * DEVICES) ** 0.5), 0.109375, ((0, 8), (3, 4)), (3, 1, 4, 2.0), jnp.float32),
    }


spread_sq = 0.0004
norm_floor = 1e-06
highest = lax.Precision.HIGHEST

def tile_values(points, src_nodes, src_weights):
    summed = jnp.zeros((points.shape[1], src_nodes.shape[2]), jnp.float32)
    for node_index in range(src_nodes.shape[1]):
        offset_first = points[0][:, None] - src_nodes[0, node_index][None, :]
        offset_second = points[1][:, None] - src_nodes[1, node_index][None, :]
        offset_third = points[2][:, None] - src_nodes[2, node_index][None, :]
        distance = jnp.sqrt(offset_first * offset_first + offset_second * offset_second + offset_third * offset_third + spread_sq)
        summed = summed + src_weights[node_index][None, :] / distance
    return summed

def reference(right_side, targets, source_nodes, node_weights, near_list, near_count, row_basis, column_basis, coupling):
    slot_total = DEVICES * NEAR_MAX
    slot_ids = jnp.arange(slot_total, dtype=jnp.int32)
    live_slot = slot_ids % NEAR_MAX < near_count[slot_ids // NEAR_MAX]
    target_ids = near_list[0]
    source_ids = near_list[1]
    point_blocks = targets.reshape(3, DEVICES, LEAF)
    node_blocks = source_nodes.reshape(3, Q, DEVICES, LEAF)
    weight_blocks = node_weights.reshape(Q, DEVICES, LEAF)
    near_mask = jnp.zeros((DEVICES, DEVICES), jnp.float32).at[target_ids, source_ids].max(live_slot.astype(jnp.float32))
    keep_far = 1.0 - near_mask
    coupled = coupling.reshape(DEVICES, DEVICES, R, R)

    def operate(vector):
        blocks = vector.reshape(DEVICES, LEAF)

        def one_tile(slot_number):
            target = target_ids[slot_number]
            source = source_ids[slot_number]

            def compute(unused):
                tile_block = tile_values(point_blocks[:, target], node_blocks[:, :, source], weight_blocks[:, source])
                return jnp.dot(tile_block, blocks[source], precision=highest)

            def nothing(unused):
                return jnp.zeros((LEAF,), jnp.float32)
            return lax.cond(live_slot[slot_number], compute, nothing, 0)
        contrib = lax.map(one_tile, slot_ids)
        near_part = jnp.zeros((DEVICES, LEAF), jnp.float32).at[target_ids].add(contrib)
        coeffs = jnp.einsum('crp,cp->cr', column_basis, blocks, precision=highest)

        def one_row(row_index):
            return jnp.einsum('bst,bt->s', coupled[row_index] * keep_far[row_index][:, None, None], coeffs, precision=highest)
        far_coeffs = lax.map(one_row, jnp.arange(DEVICES, dtype=jnp.int32))
        far_part = jnp.einsum('cr,crp->cp', far_coeffs, row_basis, precision=highest)
        return (0.5 * blocks + near_part + far_part).reshape(DEVICES * LEAF)
    rhs_norm = jnp.sqrt(jnp.sum(right_side * right_side) + norm_floor)
    basis_one = right_side / rhs_norm
    image_one = operate(basis_one)
    proj_first = jnp.sum(basis_one * image_one)
    rest_one = image_one - proj_first * basis_one
    height_first = jnp.sqrt(jnp.sum(rest_one * rest_one) + norm_floor)
    basis_two = rest_one / height_first
    image_two = operate(basis_two)
    proj_cross = jnp.sum(basis_one * image_two)
    proj_second = jnp.sum(basis_two * image_two)
    rest_two = image_two - proj_cross * basis_one - proj_second * basis_two
    height_second = jnp.sqrt(jnp.sum(rest_two * rest_two) + norm_floor)
    radius_first = jnp.sqrt(proj_first * proj_first + height_first * height_first)
    cos_first = proj_first / radius_first
    sin_first = height_first / radius_first
    rotated_top = cos_first * proj_cross + sin_first * proj_second
    rotated_low = cos_first * proj_second - sin_first * proj_cross
    radius_second = jnp.sqrt(rotated_low * rotated_low + height_second * height_second)
    coeff_second = -sin_first * rhs_norm * (rotated_low / radius_second) / radius_second
    coeff_first = (cos_first * rhs_norm - rotated_top * coeff_second) / radius_first
    return coeff_first * basis_one + coeff_second * basis_two
```

```python
import functools

import jax
import jax.numpy as jnp
from jax import lax
from jax.experimental import pallas as pl
from jax.experimental.pallas import tpu as pltpu
from jax.sharding import PartitionSpec as P

spread_sq = 0.0004
norm_floor = 1e-06
highest = lax.Precision.HIGHEST
both_axes = ("tgt", "src")
lane_contract = (((1,), (1,)), ((), ()))
plain_contract = (((1,), (0,)), ((), ()))
vmem_space = pl.BlockSpec(memory_space=pltpu.VMEM)
smem_space = pl.BlockSpec(memory_space=pltpu.SMEM)
any_space = pl.BlockSpec(memory_space=pl.ANY)


def in_three(value):
    top = value.astype(jnp.bfloat16)
    rest = value - top.astype(jnp.float32)
    middle = rest.astype(jnp.bfloat16)
    low = (rest - middle.astype(jnp.float32)).astype(jnp.bfloat16)
    return top, middle, low


def exact_dot(value, flags, contract):
    parts = [
        lax.dot_general(part, flags, contract, preferred_element_type=jnp.float32)
        for part in in_three(value)
    ]
    return parts[0] + (parts[1] + parts[2])


def exact_pick(flags, value):
    parts = [
        lax.dot_general(flags, part, plain_contract, preferred_element_type=jnp.float32)
        for part in in_three(value)
    ]
    return parts[0] + (parts[1] + parts[2])


def iota(shape, dim):
    return lax.broadcasted_iota(jnp.int32, shape, dim)


def rows_of(src_count):
    return max(8, src_count)


def pack_kernel(nodes, weights, values, column_basis, packed, *, node_rows):
    packed[...] = jnp.zeros_like(packed)
    for coord in range(3):
        packed[pl.ds(coord * node_rows, node_rows), :] = nodes[coord]
    packed[pl.ds(3 * node_rows, node_rows), :] = weights[...]
    vector = values[...]
    packed[pl.ds(4 * node_rows, 1), :] = vector
    tall = jnp.broadcast_to(vector, (8, vector.shape[1]))
    coeffs = lax.dot_general(
        tall, column_basis[0], lane_contract, precision=highest, preferred_element_type=jnp.float32
    )
    packed[pl.ds(4 * node_rows + 1, 1), pl.ds(0, coeffs.shape[1])] = coeffs[0:1]


def far_rows(coeffs, coupling, keep, row_bases, src_count, tgt_count, rank):
    rows = rows_of(src_count)
    width = coeffs.shape[1]
    spread_flags = (
        (iota((width, rank * rank), 0) % rank) == (iota((width, rank * rank), 1) % rank)
    ).astype(jnp.bfloat16)
    tiled = exact_dot(coeffs, spread_flags, plain_contract)
    row_id = iota((rows, rank * rank), 0) % src_count
    summed = jnp.zeros((rows, rank * rank), jnp.float32)
    for target in range(src_count):
        block = coupling[pl.ds(target * tgt_count, tgt_count), :]
        kept = keep[pl.ds(target * tgt_count, tgt_count), :]
        block = block * jnp.concatenate([kept] * (rank * rank // 128), axis=1)
        total = jnp.sum(block * tiled, axis=0, keepdims=True)
        summed = jnp.where(row_id == target, total, summed)
    stacked = src_count * rank
    group_flags = (
        (iota((stacked, rank * rank), 1) // rank) == (iota((stacked, rank * rank), 0) % rank)
    ).astype(jnp.bfloat16)
    far = exact_dot(summed, group_flags, lane_contract)
    own = (iota((rows, stacked), 1) // rank) == (iota((rows, stacked), 0) % src_count)
    far = jnp.where(own, far, 0.0)
    return lax.dot_general(
        far, row_bases[...], plain_contract, precision=highest, preferred_element_type=jnp.float32
    )


def near_rows(partial, src_count, leaf):
    rows = rows_of(src_count)
    ones = jnp.ones((8, 128), jnp.bfloat16)
    row_id = iota((rows, leaf), 0) % src_count
    result = jnp.zeros((rows, leaf), jnp.float32)
    for target in range(src_count):
        block = partial[target]
        parts = [
            lax.dot_general(ones, part, lane_contract, preferred_element_type=jnp.float32)
            for part in in_three(block)
        ]
        total = (parts[0] + (parts[1] + parts[2]))[0:1]
        result = jnp.where(row_id == target, total, result)
    return result


def clear_partials(partial, keep, src_count):
    keep[...] = jnp.ones_like(keep)
    for target in range(src_count):
        partial[target] = jnp.zeros(partial.shape[1:], jnp.float32)


def add_product(partial, target, start, size, tile, vector):
    half = vector * tile
    total = half[:, 0:128]
    for lane in range(128, tile.shape[1], 128):
        total = total + half[:, lane : lane + 128]
    here = pl.ds(start, size)
    partial[target, here, :] = partial[target, here, :] + total


def first_kernel(
    near_list, near_count, coupling, *refs, src_count, tgt_count, node_rows, rank, leaf
):
    columns = refs[:tgt_count]
    refs = refs[tgt_count:]
    points, refs = refs[:src_count], refs[src_count:]
    rows_in, refs = refs[:src_count], refs[src_count:]
    cols_in, refs = refs[:src_count], refs[src_count:]
    message, tiles_out = refs[:2]
    (held, flat_points, row_bases, col_bases, spread, partial, keep, tiles, far_values) = refs[2:11]
    held_sems, point_sems, row_sems, col_sems, tile_sems = refs[11:]
    tgt_index = lax.axis_index("tgt")
    src_index = lax.axis_index("src")
    copies = []
    for shift in range(src_count):
        there = lax.rem(src_index - shift + src_count, src_count)
        copies.append(
            pltpu.make_async_copy(points[shift], flat_points.at[there], point_sems.at[shift])
        )
    column_copies = []
    for spot in range(tgt_count):
        there = column_place(tgt_index, spot, tgt_count)
        column_copies.append(
            pltpu.make_async_copy(columns[spot], held.at[there], held_sems.at[spot])
        )
    base_copies = []
    for shift in range(src_count):
        there = lax.rem(src_index - shift + src_count, src_count)
        here = pl.ds(pl.multiple_of(there * rank, rank), rank)
        base_copies.append(
            pltpu.make_async_copy(rows_in[shift].at[0], row_bases.at[here, :], row_sems.at[shift])
        )
        base_copies.append(
            pltpu.make_async_copy(cols_in[shift].at[0], col_bases.at[here, :], col_sems.at[shift])
        )
    for copy in copies + column_copies + base_copies:
        copy.start()
    clear_partials(partial, keep, src_count)
    for copy in copies:
        copy.wait()
    for target in range(src_count):
        upright = jnp.transpose(
            jnp.concatenate([flat_points[target], jnp.zeros((5, leaf), jnp.float32)], axis=0)
        )
        for coord in range(3):
            spread[target * 3 + coord] = jnp.broadcast_to(upright[:, coord : coord + 1], (leaf, 128))
    for copy in column_copies:
        copy.wait()
    live = near_count[0]
    block = 32

    def one_slot(slot, carry):
        target = near_list[0, slot] - tgt_index * src_count
        source = near_list[1, slot] // src_count
        keep[pl.ds(target * tgt_count + source, 1), :] = jnp.zeros((1, 128), jnp.float32)

        def one_block(number, inner):
            start = pl.multiple_of(number * block, block)
            here = pl.ds(start, block)
            near = [spread[target * 3 + coord, here, :] for coord in range(3)]
            halves = []
            for lane in range(0, leaf, 128):
                lanes = pl.ds(lane, 128)
                total = None
                for node in range(node_rows):
                    gaps = [
                        near[coord] - held[source, pl.ds(coord * node_rows + node, 1), lanes]
                        for coord in range(3)
                    ]
                    square = gaps[0] * gaps[0] + gaps[1] * gaps[1] + gaps[2] * gaps[2] + spread_sq
                    term = held[source, pl.ds(3 * node_rows + node, 1), lanes] * lax.rsqrt(square)
                    total = term if total is None else total + term
                halves.append(total)
            tile = jnp.concatenate(halves, axis=1)
            tiles[slot, here, :] = tile
            vector = held[source, pl.ds(4 * node_rows, 1), :]
            add_product(partial, target, start, block, tile, vector)
            return inner

        lax.fori_loop(0, leaf // block, one_block, 0)
        pltpu.make_async_copy(tiles.at[slot], tiles_out.at[slot], tile_sems.at[slot]).start()
        return carry

    lax.fori_loop(0, live, one_slot, 0)
    for spot in range(tgt_count):
        far_values[pl.ds(spot, 1), :] = held[spot, pl.ds(4 * node_rows + 1, 1), pl.ds(0, 128)]
    for copy in base_copies:
        copy.wait()
    near = near_rows(partial, src_count, leaf)
    far = far_rows(far_values[...], coupling, keep, row_bases, src_count, tgt_count, rank)
    total = near + far
    rows = rows_of(src_count)
    stacked = src_count * rank
    coeffs = lax.dot_general(
        total, col_bases[...], lane_contract, precision=highest, preferred_element_type=jnp.float32
    )
    own = (iota((rows, stacked), 1) // rank) == (iota((rows, stacked), 0) % src_count)
    coeffs = jnp.where(own, coeffs, 0.0)
    for start in range(0, src_count * tgt_count, rows):
        message[pl.ds(start, rows), pl.ds(0, leaf)] = total
        message[pl.ds(start, rows), pl.ds(leaf, stacked)] = coeffs

    def finish(slot, carry):
        pltpu.make_async_copy(tiles.at[slot], tiles_out.at[slot], tile_sems.at[slot]).wait()
        return carry

    lax.fori_loop(0, live, finish, 0)


def column_place(tgt_index, spot, tgt_count):
    group = 2 if tgt_count % 2 == 0 else 1
    lines = tgt_count // group
    shift, flip = spot % lines, spot // lines
    line = lax.rem(tgt_index // group - shift + lines, lines)
    return line * group + lax.rem(tgt_index % group + flip, group)


def second_kernel(
    near_list, near_count, coupling, received, values, tiles_in, *refs, src_count, tgt_count, rank, leaf
):
    rows_in, refs = refs[:src_count], refs[src_count:]
    message = refs[0]
    (row_bases, partial, keep, tiles, image, row_sems, tile_sems) = refs[1:]
    tgt_index = lax.axis_index("tgt")
    src_index = lax.axis_index("src")
    live = near_count[0]

    def fetch(slot, carry):
        pltpu.make_async_copy(tiles_in.at[slot], tiles.at[slot], tile_sems.at[slot]).start()
        return carry

    lax.fori_loop(0, live, fetch, 0)
    base_copies = []
    for shift in range(src_count):
        there = lax.rem(src_index - shift + src_count, src_count)
        here = pl.ds(pl.multiple_of(there * rank, rank), rank)
        base_copies.append(
            pltpu.make_async_copy(rows_in[shift].at[0], row_bases.at[here, :], row_sems.at[shift])
        )
    for copy in base_copies:
        copy.start()
    clear_partials(partial, keep, src_count)
    stacked = src_count * rank
    groups = (tgt_count, src_count * tgt_count)
    flags = ((iota(groups, 1) // src_count) == iota(groups, 0)).astype(jnp.bfloat16)
    image[...] = exact_pick(flags, received[...])
    block = 64

    def one_slot(slot, carry):
        target = near_list[0, slot] - tgt_index * src_count
        source = near_list[1, slot] // src_count
        keep[pl.ds(target * tgt_count + source, 1), :] = jnp.zeros((1, 128), jnp.float32)
        pltpu.make_async_copy(tiles_in.at[slot], tiles.at[slot], tile_sems.at[slot]).wait()
        vector = image[pl.ds(source, 1), pl.ds(0, leaf)]
        for start in range(0, leaf, block):
            add_product(partial, target, start, block, tiles[slot, pl.ds(start, block), :], vector)
        return carry

    lax.fori_loop(0, live, one_slot, 0)
    for copy in base_copies:
        copy.wait()
    near = near_rows(partial, src_count, leaf)
    far = far_rows(
        image[:, pl.ds(leaf, stacked)], coupling, keep, row_bases, src_count, tgt_count, rank
    )
    total = near + far
    pieces = [total[target : target + 1] for target in range(src_count)]
    pieces.append(image[pl.ds(tgt_index, 1), pl.ds(0, leaf)])
    pieces.append(values[...])
    for number, piece in enumerate(pieces):
        message[:, pl.ds(number * leaf, leaf)] = jnp.broadcast_to(piece, (message.shape[0], leaf))


def third_kernel(received, result, *, src_count, tgt_count, leaf):
    def inner(left, right):
        return jnp.sum(left * right, axis=0, keepdims=True)

    devices = src_count * tgt_count
    groups = (tgt_count, devices)
    flags = ((iota(groups, 1) // src_count) == iota(groups, 0)).astype(jnp.bfloat16)
    images = exact_pick(flags, received[:, pl.ds(0, src_count * leaf)])
    square = (devices, devices)
    place = (iota(square, 0) % tgt_count) * src_count + iota(square, 0) // tgt_count
    flags = (iota(square, 1) == place).astype(jnp.bfloat16)
    others = exact_pick(flags, received[:, pl.ds(src_count * leaf, 2 * leaf)])
    sums = None
    for target in range(src_count):
        twice = images[:, target * leaf : (target + 1) * leaf]
        mine = slice(target * tgt_count, (target + 1) * tgt_count)
        once = others[mine, :leaf]
        start = others[mine, leaf:]
        pairs = [
            (start, start),
            (start, once),
            (once, once),
            (start, twice),
            (once, twice),
            (twice, twice),
        ]
        products = [inner(left, right) for left, right in pairs]
        sums = products if sums is None else [old + new for old, new in zip(sums, products)]
    g00, g01, g11, g02, g12, g22 = [jnp.sum(value, axis=1, keepdims=True) for value in sums]
    rhs_norm = jnp.sqrt(g00 + norm_floor)
    scale = 1.0 / rhs_norm
    proj_first = scale * scale * (0.5 * g00 + g01)
    left = 0.5 - proj_first
    rest_sq = scale * scale * (left * left * g00 + 2.0 * left * g01 + g11)
    height_first = jnp.sqrt(jnp.maximum(rest_sq, 0.0) + norm_floor)
    c1 = scale / height_first
    c0 = left * c1
    i0 = 0.5 * c0
    i1 = 0.5 * c1 + c0
    i2 = c1
    to_start = i0 * g00 + i1 * g01 + i2 * g02
    to_once = i0 * g01 + i1 * g11 + i2 * g12
    proj_cross = scale * to_start
    proj_second = c0 * to_start + c1 * to_once
    r0 = i0 - proj_cross * scale - proj_second * c0
    r1 = i1 - proj_second * c1
    r2 = i2
    last_sq = (
        r0 * (r0 * g00 + 2.0 * (r1 * g01 + r2 * g02))
        + r1 * (r1 * g11 + 2.0 * r2 * g12)
        + r2 * r2 * g22
    )
    height_second = jnp.sqrt(jnp.maximum(last_sq, 0.0) + norm_floor)
    radius_first = jnp.sqrt(proj_first * proj_first + height_first * height_first)
    cos_first = proj_first / radius_first
    sin_first = height_first / radius_first
    rotated_top = cos_first * proj_cross + sin_first * proj_second
    rotated_low = cos_first * proj_second - sin_first * proj_cross
    radius_second = jnp.sqrt(rotated_low * rotated_low + height_second * height_second)
    coeff_second = -sin_first * rhs_norm * (rotated_low / radius_second) / radius_second
    coeff_first = (cos_first * rhs_norm - rotated_top * coeff_second) / radius_first
    me = lax.axis_index("tgt") * src_count + lax.axis_index("src")
    once = received[pl.ds(me, 1), pl.ds(src_count * leaf, leaf)]
    start = received[pl.ds(me, 1), pl.ds((src_count + 1) * leaf, leaf)]
    result[...] = (coeff_first * scale + coeff_second * c0) * start + (coeff_second * c1) * once


def per_device(
    right_side,
    targets,
    source_nodes,
    node_weights,
    near_list,
    near_count,
    row_basis,
    column_basis,
    coupling,
):
    src_count = lax.axis_size("src")
    tgt_count = lax.axis_size("tgt")
    leaf = right_side.shape[0]
    node_rows = node_weights.shape[0]
    rank = row_basis.shape[1]
    slots = near_list.shape[1]
    stacked = src_count * rank
    device_count = src_count * tgt_count
    values = right_side.reshape(1, leaf)
    couplings = coupling.reshape(src_count * tgt_count, rank * rank)
    packed_rows = -(-(4 * node_rows + 2) // 8) * 8

    packed = pl.pallas_call(
        functools.partial(pack_kernel, node_rows=node_rows),
        out_shape=jax.ShapeDtypeStruct((packed_rows, leaf), jnp.float32),
        in_specs=[vmem_space] * 4,
        out_specs=vmem_space,
        name="pack",
    )(source_nodes, node_weights, values, column_basis)

    group = 2 if tgt_count % 2 == 0 else 1
    lines = tgt_count // group

    def from_line(value, shift):
        pairs = [
            (tgt, ((tgt // group + shift) % lines) * group + tgt % group) for tgt in range(tgt_count)
        ]
        return lax.ppermute(value, "tgt", pairs)

    def from_flip(value):
        return lax.ppermute(value, "tgt", [(tgt, tgt ^ 1) for tgt in range(tgt_count)])

    def from_source(value, shift):
        return lax.ppermute(value, "src", [(src, (src + shift) % src_count) for src in range(src_count)])

    columns = [packed] + [from_line(packed, shift) for shift in range(1, lines)]
    if group == 2:
        columns = columns + [from_flip(value) for value in columns]
    points = [targets] + [from_source(targets, shift) for shift in range(1, src_count)]
    rows_in = [row_basis] + [from_source(row_basis, shift) for shift in range(1, src_count)]
    cols_in = [column_basis] + [from_source(column_basis, shift) for shift in range(1, src_count)]

    sizes = dict(src_count=src_count, tgt_count=tgt_count, rank=rank, leaf=leaf)
    message, tiles = pl.pallas_call(
        functools.partial(first_kernel, node_rows=node_rows, **sizes),
        out_shape=(
            jax.ShapeDtypeStruct((device_count, leaf + stacked), jnp.float32),
            jax.ShapeDtypeStruct((slots, leaf, leaf), jnp.float32),
        ),
        in_specs=[smem_space, smem_space, vmem_space]
        + [any_space] * (tgt_count + 3 * src_count),
        out_specs=(vmem_space, any_space),
        scratch_shapes=[
            pltpu.VMEM((tgt_count, packed_rows, leaf), jnp.float32),
            pltpu.VMEM((src_count, 3, leaf), jnp.float32),
            pltpu.VMEM((stacked, leaf), jnp.float32),
            pltpu.VMEM((stacked, leaf), jnp.float32),
            pltpu.VMEM((src_count * 3, leaf, 128), jnp.float32),
            pltpu.VMEM((src_count, leaf, 128), jnp.float32),
            pltpu.VMEM((src_count * tgt_count, 128), jnp.float32),
            pltpu.VMEM((slots, leaf, leaf), jnp.float32),
            pltpu.VMEM((tgt_count, 128), jnp.float32),
            pltpu.SemaphoreType.DMA((tgt_count,)),
            pltpu.SemaphoreType.DMA((src_count,)),
            pltpu.SemaphoreType.DMA((src_count,)),
            pltpu.SemaphoreType.DMA((src_count,)),
            pltpu.SemaphoreType.DMA((slots,)),
        ],
        name="first",
    )(near_list, near_count, couplings, *columns, *points, *rows_in, *cols_in)

    received = lax.all_to_all(message, both_axes, 0, 0, tiled=True)

    message = pl.pallas_call(
        functools.partial(second_kernel, **sizes),
        out_shape=jax.ShapeDtypeStruct((device_count, (src_count + 2) * leaf), jnp.float32),
        in_specs=[smem_space, smem_space, vmem_space, vmem_space, vmem_space]
        + [any_space] * (1 + src_count),
        out_specs=vmem_space,
        scratch_shapes=[
            pltpu.VMEM((stacked, leaf), jnp.float32),
            pltpu.VMEM((src_count, leaf, 128), jnp.float32),
            pltpu.VMEM((src_count * tgt_count, 128), jnp.float32),
            pltpu.VMEM((slots, leaf, leaf), jnp.float32),
            pltpu.VMEM((tgt_count, leaf + stacked), jnp.float32),
            pltpu.SemaphoreType.DMA((src_count,)),
            pltpu.SemaphoreType.DMA((slots,)),
        ],
        name="second",
    )(near_list, near_count, couplings, received, values, tiles, *rows_in)

    received = lax.all_to_all(message, both_axes, 0, 0, tiled=True)

    result = pl.pallas_call(
        functools.partial(third_kernel, src_count=src_count, tgt_count=tgt_count, leaf=leaf),
        out_shape=jax.ShapeDtypeStruct((1, leaf), jnp.float32),
        in_specs=[vmem_space],
        out_specs=vmem_space,
        name="third",
    )(received)
    return result.reshape(leaf)


def solution(mesh):
    return jax.shard_map(
        per_device,
        mesh=mesh,
        in_specs=(
            P(("tgt", "src")),
            P(None, ("tgt", "src")),
            P(None, None, ("tgt", "src")),
            P(None, ("tgt", "src")),
            P(None, ("tgt", "src")),
            P(("tgt", "src")),
            P(("tgt", "src"), None, None),
            P(("tgt", "src"), None, None),
            P("tgt", None, None, "src", None),
        ),
        out_specs=P(("tgt", "src")),
        check_vma=False,
    )
```

```python
import functools

import jax
import jax.numpy as jnp
from jax import lax
from jax.experimental import pallas as pl
from jax.experimental.pallas import tpu as pltpu
from jax.sharding import PartitionSpec as P

spread_sq = 0.0004
norm_floor = 1e-06
highest = lax.Precision.HIGHEST
both_axes = ("tgt", "src")
lane_contract = (((1,), (1,)), ((), ()))
plain_contract = (((1,), (0,)), ((), ()))
vmem_space = pl.BlockSpec(memory_space=pltpu.VMEM)
smem_space = pl.BlockSpec(memory_space=pltpu.SMEM)
kernel_params = pltpu.CompilerParams(vmem_limit_bytes=32 * 1024 * 1024)


def in_three(value):
    top = value.astype(jnp.bfloat16)
    rest = value - top.astype(jnp.float32)
    middle = rest.astype(jnp.bfloat16)
    low = (rest - middle.astype(jnp.float32)).astype(jnp.bfloat16)
    return top, middle, low


def exact_dot(value, flags, contract):
    parts = [
        lax.dot_general(part, flags, contract, preferred_element_type=jnp.float32)
        for part in in_three(value)
    ]
    return parts[0] + (parts[1] + parts[2])


def exact_pick(flags, value):
    parts = [
        lax.dot_general(flags, part, plain_contract, preferred_element_type=jnp.float32)
        for part in in_three(value)
    ]
    return parts[0] + (parts[1] + parts[2])


def iota(shape, dim):
    return lax.broadcasted_iota(jnp.int32, shape, dim)


def rows_of(src_count):
    return max(8, src_count)


def pack_kernel(
    nodes, weights, values, targets, row_basis, column_basis, packed, basis, *, node_rows, rank
):
    for coord in range(3):
        packed[pl.ds(coord * node_rows, node_rows), :] = nodes[coord]
    packed[pl.ds(3 * node_rows, node_rows), :] = weights[...]
    vector = values[...]
    leaf = vector.shape[1]
    packed[pl.ds(4 * node_rows, 8), :] = jnp.zeros((8, leaf), jnp.float32)
    packed[pl.ds(4 * node_rows, 1), :] = vector
    tall = jnp.broadcast_to(vector, (8, leaf))
    coeffs = lax.dot_general(
        tall, column_basis[0], lane_contract, precision=highest, preferred_element_type=jnp.float32
    )
    packed[pl.ds(4 * node_rows + 1, 1), pl.ds(0, rank)] = coeffs[0:1]
    basis[pl.ds(0, rank), :] = row_basis[0]
    basis[pl.ds(rank, rank), :] = column_basis[0]
    basis[pl.ds(2 * rank, 8), :] = jnp.zeros((8, leaf), jnp.float32)
    basis[pl.ds(2 * rank, 3), :] = targets[...]


def far_rows(coeffs, coupling, keep, row_bases, src_count, tgt_count, rank):
    rows = rows_of(src_count)
    width = coeffs.shape[1]
    spread_flags = (
        (iota((width, rank * rank), 0) % rank) == (iota((width, rank * rank), 1) % rank)
    ).astype(jnp.bfloat16)
    tiled = exact_dot(coeffs, spread_flags, plain_contract)
    row_id = iota((rows, rank * rank), 0) % src_count
    summed = jnp.zeros((rows, rank * rank), jnp.float32)
    for target in range(src_count):
        block = coupling[pl.ds(target * tgt_count, tgt_count), :]
        kept = keep[pl.ds(target * tgt_count, tgt_count), :]
        block = block * jnp.concatenate([kept] * (rank * rank // 128), axis=1)
        total = jnp.sum(block * tiled, axis=0, keepdims=True)
        summed = jnp.where(row_id == target, total, summed)
    stacked = src_count * rank
    group_flags = (
        (iota((stacked, rank * rank), 1) // rank) == (iota((stacked, rank * rank), 0) % rank)
    ).astype(jnp.bfloat16)
    far = exact_dot(summed, group_flags, lane_contract)
    own = (iota((rows, stacked), 1) // rank) == (iota((rows, stacked), 0) % src_count)
    far = jnp.where(own, far, 0.0)
    return lax.dot_general(
        far, row_bases[...], plain_contract, precision=highest, preferred_element_type=jnp.float32
    )


def near_rows(partial, src_count, leaf):
    rows = rows_of(src_count)
    ones = jnp.ones((8, 128), jnp.bfloat16)
    row_id = iota((rows, leaf), 0) % src_count
    result = jnp.zeros((rows, leaf), jnp.float32)
    for target in range(src_count):
        block = partial[target]
        parts = [
            lax.dot_general(ones, part, lane_contract, preferred_element_type=jnp.float32)
            for part in in_three(block)
        ]
        total = (parts[0] + (parts[1] + parts[2]))[0:1]
        result = jnp.where(row_id == target, total, result)
    return result


def clear_partials(partial, keep, src_count):
    keep[...] = jnp.ones_like(keep)
    for target in range(src_count):
        partial[target] = jnp.zeros(partial.shape[1:], jnp.float32)


def add_product(partial, target, start, size, tile, vector):
    half = vector * tile
    total = half[:, 0:128]
    for lane in range(128, tile.shape[1], 128):
        total = total + half[:, lane : lane + 128]
    here = pl.ds(start, size)
    partial[target, here, :] = partial[target, here, :] + total


def first_kernel(
    near_list, near_count, coupling, *refs, src_count, tgt_count, node_rows, rank, leaf
):
    columns, refs = refs[:tgt_count], refs[tgt_count:]
    bases, refs = refs[:src_count], refs[src_count:]
    message, tiles, row_bases = refs[:3]
    held, col_bases, spread, partial, keep, far_values = refs[3:]
    tgt_index = lax.axis_index("tgt")
    src_index = lax.axis_index("src")
    clear_partials(partial, keep, src_count)
    for spot in range(tgt_count):
        there = column_place(tgt_index, spot, tgt_count)
        held[there] = columns[spot][...]
        far_values[pl.ds(there, 1), :] = columns[spot][pl.ds(4 * node_rows + 1, 1), pl.ds(0, 128)]
    for shift in range(src_count):
        there = lax.rem(src_index - shift + src_count, src_count)
        here = pl.ds(pl.multiple_of(there * rank, rank), rank)
        row_bases[here, :] = bases[shift][pl.ds(0, rank), :]
        col_bases[here, :] = bases[shift][pl.ds(rank, rank), :]
        upright = jnp.transpose(bases[shift][pl.ds(2 * rank, 8), :])
        for coord in range(3):
            spread[there * 3 + coord] = jnp.broadcast_to(upright[:, coord : coord + 1], (leaf, 128))
    live = near_count[0]
    block = 32

    def one_slot(slot, carry):
        target = near_list[0, slot] - tgt_index * src_count
        source = near_list[1, slot] // src_count
        keep[pl.ds(target * tgt_count + source, 1), :] = jnp.zeros((1, 128), jnp.float32)

        def one_block(number, inner):
            start = pl.multiple_of(number * block, block)
            here = pl.ds(start, block)
            near = [spread[target * 3 + coord, here, :] for coord in range(3)]
            halves = []
            for lane in range(0, leaf, 128):
                lanes = pl.ds(lane, 128)
                total = None
                for node in range(node_rows):
                    gaps = [
                        near[coord] - held[source, pl.ds(coord * node_rows + node, 1), lanes]
                        for coord in range(3)
                    ]
                    square = gaps[0] * gaps[0] + gaps[1] * gaps[1] + gaps[2] * gaps[2] + spread_sq
                    term = held[source, pl.ds(3 * node_rows + node, 1), lanes] * lax.rsqrt(square)
                    total = term if total is None else total + term
                halves.append(total)
            tile = jnp.concatenate(halves, axis=1)
            tiles[slot, here, :] = tile
            vector = held[source, pl.ds(4 * node_rows, 1), :]
            add_product(partial, target, start, block, tile, vector)
            return inner

        lax.fori_loop(0, leaf // block, one_block, 0)
        return carry

    lax.fori_loop(0, live, one_slot, 0)
    near = near_rows(partial, src_count, leaf)
    far = far_rows(far_values[...], coupling, keep, row_bases, src_count, tgt_count, rank)
    total = near + far
    rows = rows_of(src_count)
    stacked = src_count * rank
    coeffs = lax.dot_general(
        total, col_bases[...], lane_contract, precision=highest, preferred_element_type=jnp.float32
    )
    own = (iota((rows, stacked), 1) // rank) == (iota((rows, stacked), 0) % src_count)
    coeffs = jnp.where(own, coeffs, 0.0)
    for start in range(0, src_count * tgt_count, rows):
        message[pl.ds(start, rows), 0, pl.ds(0, leaf)] = total
        message[pl.ds(start, rows), 0, pl.ds(leaf, stacked)] = coeffs


def column_place(tgt_index, spot, tgt_count):
    group = 2 if tgt_count % 2 == 0 else 1
    lines = tgt_count // group
    shift, flip = spot % lines, spot // lines
    line = lax.rem(tgt_index // group - shift + lines, lines)
    return line * group + lax.rem(tgt_index % group + flip, group)


def second_kernel(
    near_list,
    near_count,
    coupling,
    received,
    values,
    row_bases,
    tiles,
    message,
    partial,
    keep,
    image,
    *,
    src_count,
    tgt_count,
    rank,
    leaf,
):
    tgt_index = lax.axis_index("tgt")
    live = near_count[0]
    clear_partials(partial, keep, src_count)
    stacked = src_count * rank
    groups = (tgt_count, src_count * tgt_count)
    flags = ((iota(groups, 1) // src_count) == iota(groups, 0)).astype(jnp.bfloat16)
    image[...] = exact_pick(flags, received[:, 0, :])
    block = 64

    def one_slot(slot, carry):
        target = near_list[0, slot] - tgt_index * src_count
        source = near_list[1, slot] // src_count
        keep[pl.ds(target * tgt_count + source, 1), :] = jnp.zeros((1, 128), jnp.float32)
        vector = image[pl.ds(source, 1), pl.ds(0, leaf)]
        for start in range(0, leaf, block):
            add_product(partial, target, start, block, tiles[slot, pl.ds(start, block), :], vector)
        return carry

    lax.fori_loop(0, live, one_slot, 0)
    near = near_rows(partial, src_count, leaf)
    far = far_rows(
        image[:, pl.ds(leaf, stacked)], coupling, keep, row_bases, src_count, tgt_count, rank
    )
    total = near + far
    pieces = [total[target : target + 1] for target in range(src_count)]
    pieces.append(image[pl.ds(tgt_index, 1), pl.ds(0, leaf)])
    pieces.append(values[...])
    for number, piece in enumerate(pieces):
        message[:, 0, pl.ds(number * leaf, leaf)] = jnp.broadcast_to(piece, (message.shape[0], leaf))


def third_kernel(received, result, *, src_count, tgt_count, leaf):
    def inner(left, right):
        return jnp.sum(left * right, axis=0, keepdims=True)

    devices = src_count * tgt_count
    groups = (tgt_count, devices)
    flags = ((iota(groups, 1) // src_count) == iota(groups, 0)).astype(jnp.bfloat16)
    batch = 4 if src_count % 4 == 0 else 1
    picked = []
    for first in range(0, src_count, batch):
        images = exact_pick(flags, received[:, 0, pl.ds(first * leaf, batch * leaf)])
        shape = (batch * tgt_count, devices)
        place = (iota(shape, 0) % tgt_count) * src_count + iota(shape, 0) // tgt_count + first
        own_flags = (iota(shape, 1) == place).astype(jnp.bfloat16)
        others = exact_pick(own_flags, received[:, 0, pl.ds(src_count * leaf, 2 * leaf)])
        for number in range(batch):
            mine = slice(number * tgt_count, (number + 1) * tgt_count)
            twice = images[:, number * leaf : (number + 1) * leaf]
            picked.append((others[mine, leaf:], others[mine, :leaf], twice))
    sums = None
    for start, once, twice in picked:
        pairs = [
            (start, start),
            (start, once),
            (once, once),
            (start, twice),
            (once, twice),
            (twice, twice),
        ]
        products = [inner(left, right) for left, right in pairs]
        sums = products if sums is None else [old + new for old, new in zip(sums, products)]
    g00, g01, g11, g02, g12, g22 = [jnp.sum(value, axis=1, keepdims=True) for value in sums]
    rhs_norm = jnp.sqrt(g00 + norm_floor)
    scale = 1.0 / rhs_norm
    proj_first = scale * scale * (0.5 * g00 + g01)
    left = 0.5 - proj_first
    rest_sq = scale * scale * (left * left * g00 + 2.0 * left * g01 + g11)
    height_first = jnp.sqrt(jnp.maximum(rest_sq, 0.0) + norm_floor)
    c1 = scale / height_first
    c0 = left * c1
    i0 = 0.5 * c0
    i1 = 0.5 * c1 + c0
    i2 = c1
    to_start = i0 * g00 + i1 * g01 + i2 * g02
    to_once = i0 * g01 + i1 * g11 + i2 * g12
    proj_cross = scale * to_start
    proj_second = c0 * to_start + c1 * to_once
    r0 = i0 - proj_cross * scale - proj_second * c0
    r1 = i1 - proj_second * c1
    r2 = i2
    last_sq = (
        r0 * (r0 * g00 + 2.0 * (r1 * g01 + r2 * g02))
        + r1 * (r1 * g11 + 2.0 * r2 * g12)
        + r2 * r2 * g22
    )
    height_second = jnp.sqrt(jnp.maximum(last_sq, 0.0) + norm_floor)
    radius_first = jnp.sqrt(proj_first * proj_first + height_first * height_first)
    cos_first = proj_first / radius_first
    sin_first = height_first / radius_first
    rotated_top = cos_first * proj_cross + sin_first * proj_second
    rotated_low = cos_first * proj_second - sin_first * proj_cross
    radius_second = jnp.sqrt(rotated_low * rotated_low + height_second * height_second)
    coeff_second = -sin_first * rhs_norm * (rotated_low / radius_second) / radius_second
    coeff_first = (cos_first * rhs_norm - rotated_top * coeff_second) / radius_first
    me = lax.axis_index("tgt") * src_count + lax.axis_index("src")
    once = received[me, :, pl.ds(src_count * leaf, leaf)]
    start = received[me, :, pl.ds((src_count + 1) * leaf, leaf)]
    result[...] = (coeff_first * scale + coeff_second * c0) * start + (coeff_second * c1) * once


def per_device(
    right_side,
    targets,
    source_nodes,
    node_weights,
    near_list,
    near_count,
    row_basis,
    column_basis,
    coupling,
):
    src_count = lax.axis_size("src")
    tgt_count = lax.axis_size("tgt")
    leaf = right_side.shape[0]
    node_rows = node_weights.shape[0]
    rank = row_basis.shape[1]
    slots = near_list.shape[1]
    stacked = src_count * rank
    device_count = src_count * tgt_count
    values = right_side.reshape(1, leaf)
    couplings = coupling.reshape(src_count * tgt_count, rank * rank)
    packed_rows = 4 * node_rows + 8

    basis_rows = 2 * rank + 8
    packed, basis = pl.pallas_call(
        functools.partial(pack_kernel, node_rows=node_rows, rank=rank),
        out_shape=(
            jax.ShapeDtypeStruct((packed_rows, leaf), jnp.float32),
            jax.ShapeDtypeStruct((basis_rows, leaf), jnp.float32),
        ),
        in_specs=[vmem_space] * 6,
        out_specs=(vmem_space, vmem_space),
        compiler_params=kernel_params,
        name="pack",
    )(source_nodes, node_weights, values, targets, row_basis, column_basis)

    group = 2 if tgt_count % 2 == 0 else 1
    lines = tgt_count // group

    def from_line(value, shift):
        pairs = [
            (tgt, ((tgt // group + shift) % lines) * group + tgt % group) for tgt in range(tgt_count)
        ]
        return lax.ppermute(value, "tgt", pairs)

    def from_flip(value):
        return lax.ppermute(value, "tgt", [(tgt, tgt ^ 1) for tgt in range(tgt_count)])

    def from_source(value, shift):
        return lax.ppermute(value, "src", [(src, (src + shift) % src_count) for src in range(src_count)])

    columns = [packed] + [from_line(packed, shift) for shift in range(1, lines)]
    if group == 2:
        columns = columns + [from_flip(value) for value in columns]
    bases = [basis] + [from_source(basis, shift) for shift in range(1, src_count)]

    sizes = dict(src_count=src_count, tgt_count=tgt_count, rank=rank, leaf=leaf)
    message, tiles, row_bases = pl.pallas_call(
        functools.partial(first_kernel, node_rows=node_rows, **sizes),
        out_shape=(
            jax.ShapeDtypeStruct((device_count, 1, leaf + stacked), jnp.float32),
            jax.ShapeDtypeStruct((slots, leaf, leaf), jnp.float32),
            jax.ShapeDtypeStruct((stacked, leaf), jnp.float32),
        ),
        in_specs=[smem_space, smem_space] + [vmem_space] * (1 + tgt_count + src_count),
        out_specs=(vmem_space, vmem_space, vmem_space),
        scratch_shapes=[
            pltpu.VMEM((tgt_count, packed_rows, leaf), jnp.float32),
            pltpu.VMEM((stacked, leaf), jnp.float32),
            pltpu.VMEM((src_count * 3, leaf, 128), jnp.float32),
            pltpu.VMEM((src_count, leaf, 128), jnp.float32),
            pltpu.VMEM((src_count * tgt_count, 128), jnp.float32),
            pltpu.VMEM((tgt_count, 128), jnp.float32),
        ],
        compiler_params=kernel_params,
        name="first",
    )(near_list, near_count, couplings, *columns, *bases)

    received = lax.all_to_all(message, both_axes, 0, 0, tiled=True)

    message = pl.pallas_call(
        functools.partial(second_kernel, **sizes),
        out_shape=jax.ShapeDtypeStruct((device_count, 1, (src_count + 2) * leaf), jnp.float32),
        in_specs=[smem_space, smem_space] + [vmem_space] * 5,
        out_specs=vmem_space,
        scratch_shapes=[
            pltpu.VMEM((src_count, leaf, 128), jnp.float32),
            pltpu.VMEM((src_count * tgt_count, 128), jnp.float32),
            pltpu.VMEM((tgt_count, leaf + stacked), jnp.float32),
        ],
        compiler_params=kernel_params,
        name="second",
    )(near_list, near_count, couplings, received, values, row_bases, tiles)

    received = lax.all_to_all(message, both_axes, 0, 0, tiled=True)

    result = pl.pallas_call(
        functools.partial(third_kernel, src_count=src_count, tgt_count=tgt_count, leaf=leaf),
        out_shape=jax.ShapeDtypeStruct((1, leaf), jnp.float32),
        in_specs=[vmem_space],
        out_specs=vmem_space,
        compiler_params=kernel_params,
        name="third",
    )(received)
    return result.reshape(leaf)


def solution(mesh):
    return jax.shard_map(
        per_device,
        mesh=mesh,
        in_specs=(
            P(("tgt", "src")),
            P(None, ("tgt", "src")),
            P(None, None, ("tgt", "src")),
            P(None, ("tgt", "src")),
            P(None, ("tgt", "src")),
            P(("tgt", "src")),
            P(("tgt", "src"), None, None),
            P(("tgt", "src"), None, None),
            P("tgt", None, None, "src", None),
        ),
        out_specs=P(("tgt", "src")),
        check_vma=False,
    )
```

```python
import functools

import jax
import jax.numpy as jnp
from jax import lax
from jax.experimental import pallas as pl
from jax.experimental.pallas import tpu as pltpu
from jax.sharding import PartitionSpec as P

spread_sq = 0.0004
norm_floor = 1e-06
highest = lax.Precision.HIGHEST
both_axes = ("tgt", "src")
lane_contract = (((1,), (1,)), ((), ()))
plain_contract = (((1,), (0,)), ((), ()))
term_count = 48
vmem_space = pl.BlockSpec(memory_space=pltpu.VMEM)
smem_space = pl.BlockSpec(memory_space=pltpu.SMEM)
kernel_params = pltpu.CompilerParams(vmem_limit_bytes=32 * 1024 * 1024)


def in_three(value):
    top = value.astype(jnp.bfloat16)
    rest = value - top.astype(jnp.float32)
    middle = rest.astype(jnp.bfloat16)
    low = (rest - middle.astype(jnp.float32)).astype(jnp.bfloat16)
    return top, middle, low


def exact_dot(value, flags, contract):
    parts = [
        lax.dot_general(part, flags, contract, preferred_element_type=jnp.float32)
        for part in in_three(value)
    ]
    return parts[0] + (parts[1] + parts[2])


def exact_pick(flags, value):
    parts = [
        lax.dot_general(flags, part, plain_contract, preferred_element_type=jnp.float32)
        for part in in_three(value)
    ]
    return parts[0] + (parts[1] + parts[2])


def iota(shape, dim):
    return lax.broadcasted_iota(jnp.int32, shape, dim)


def rows_of(src_count):
    return max(8, src_count)


def on_grid(value, steps):
    return lax.round(value * steps, lax.RoundingMethod.TO_NEAREST_EVEN) * (1.0 / steps)


def as_bfloat16(value):
    return value.astype(jnp.bfloat16).astype(jnp.float32)


def coordinate_parts(coords):
    parts = []
    for value in coords:
        high = on_grid(value, 128.0)
        rest = value - high
        mid = on_grid(rest, 32768.0)
        parts.append((high, mid, as_bfloat16(rest - mid)))
    return parts


def distance_terms(coords, shift, factor):
    parts = coordinate_parts(coords)
    high_sum = sum(high * high for high, mid, low in parts)
    top = as_bfloat16(high_sum)
    rest_sum = sum((mid + low) * (2.0 * high + (mid + low)) for high, mid, low in parts) + shift
    first = as_bfloat16(rest_sum)
    second = as_bfloat16(rest_sum - first)
    third = rest_sum - first - second
    squares = [top, high_sum - top]
    rests = [first, second, third]
    ones = [jnp.ones_like(top)]
    crosses = [tuple(factor * piece for piece in part) for part in parts]
    terms = {}
    if factor == 1.0:
        terms.update(zip(range(0, 4), ones * 2 + squares))
        terms.update(zip(range(16, 22), ones * 3 + rests))
        order = (1, 2, 0, 0, 1, 2, 1)
    else:
        terms.update(zip(range(0, 4), squares + ones * 2))
        terms.update(zip(range(16, 22), rests + ones * 3))
        order = (0, 0, 1, 2, 1, 1, 2)
    for coord in range(3):
        terms[4 + coord] = crosses[coord][0]
        for number, piece in enumerate(order):
            terms[22 + 7 * coord + number] = crosses[coord][piece]
    return terms


def store_terms(staged, terms, rows):
    for number, value in terms.items():
        for half in range(staged.shape[0]):
            staged[half, pl.ds(number * rows, rows), :] = value[:, half * 128 : (half + 1) * 128]


def pack_kernel(
    nodes, weights, values, targets, row_basis, column_basis, packed, basis, *, node_rows, rank
):
    for coord in range(3):
        packed[pl.ds(coord * node_rows, node_rows), :] = nodes[coord]
    packed[pl.ds(3 * node_rows, node_rows), :] = weights[...]
    vector = values[...]
    leaf = vector.shape[1]
    packed[pl.ds(4 * node_rows, 8), :] = jnp.zeros((8, leaf), jnp.float32)
    packed[pl.ds(4 * node_rows, 1), :] = vector
    tall = jnp.broadcast_to(vector, (8, leaf))
    coeffs = lax.dot_general(
        tall, column_basis[0], lane_contract, precision=highest, preferred_element_type=jnp.float32
    )
    packed[pl.ds(4 * node_rows + 1, 1), pl.ds(0, rank)] = coeffs[0:1]
    basis[pl.ds(0, rank), :] = row_basis[0]
    basis[pl.ds(rank, rank), :] = column_basis[0]
    basis[pl.ds(2 * rank, 8), :] = jnp.zeros((8, leaf), jnp.float32)
    basis[pl.ds(2 * rank, 3), :] = targets[...]


def far_rows(coeffs, coupling, keep, row_bases, src_count, tgt_count, rank):
    rows = rows_of(src_count)
    width = coeffs.shape[1]
    spread_flags = (
        (iota((width, rank * rank), 0) % rank) == (iota((width, rank * rank), 1) % rank)
    ).astype(jnp.bfloat16)
    tiled = exact_dot(coeffs, spread_flags, plain_contract)
    row_id = iota((rows, rank * rank), 0) % src_count
    summed = jnp.zeros((rows, rank * rank), jnp.float32)
    for target in range(src_count):
        block = coupling[pl.ds(target * tgt_count, tgt_count), :]
        kept = keep[pl.ds(target * tgt_count, tgt_count), :]
        block = block * jnp.concatenate([kept] * (rank * rank // 128), axis=1)
        total = jnp.sum(block * tiled, axis=0, keepdims=True)
        summed = jnp.where(row_id == target, total, summed)
    stacked = src_count * rank
    group_flags = (
        (iota((stacked, rank * rank), 1) // rank) == (iota((stacked, rank * rank), 0) % rank)
    ).astype(jnp.bfloat16)
    far = exact_dot(summed, group_flags, lane_contract)
    own = (iota((rows, stacked), 1) // rank) == (iota((rows, stacked), 0) % src_count)
    far = jnp.where(own, far, 0.0)
    return lax.dot_general(
        far, row_bases[...], plain_contract, precision=highest, preferred_element_type=jnp.float32
    )


def near_rows(partial, src_count, leaf):
    rows = rows_of(src_count)
    ones = jnp.ones((8, 128), jnp.bfloat16)
    row_id = iota((rows, leaf), 0) % src_count
    result = jnp.zeros((rows, leaf), jnp.float32)
    for target in range(src_count):
        block = partial[target]
        parts = [
            lax.dot_general(ones, part, lane_contract, preferred_element_type=jnp.float32)
            for part in in_three(block)
        ]
        total = (parts[0] + (parts[1] + parts[2]))[0:1]
        result = jnp.where(row_id == target, total, result)
    return result


def clear_partials(partial, keep, src_count):
    keep[...] = jnp.ones_like(keep)
    for target in range(src_count):
        partial[target] = jnp.zeros(partial.shape[1:], jnp.float32)


def add_product(partial, target, start, size, tile, vector):
    half = vector * tile
    total = half[:, 0:128]
    for lane in range(128, tile.shape[1], 128):
        total = total + half[:, lane : lane + 128]
    here = pl.ds(start, size)
    partial[target, here, :] = partial[target, here, :] + total


def first_kernel(
    near_list, near_count, coupling, *refs, src_count, tgt_count, node_rows, rank, leaf
):
    columns, refs = refs[:tgt_count], refs[tgt_count:]
    bases, refs = refs[:src_count], refs[src_count:]
    message, tiles, row_bases = refs[:3]
    held, col_bases, point_rows, point_staged, point_terms = refs[3:8]
    node_staged, node_terms, built, partial, keep, far_values = refs[8:]
    tgt_index = lax.axis_index("tgt")
    src_index = lax.axis_index("src")
    clear_partials(partial, keep, src_count)
    for spot in range(tgt_count):
        there = column_place(tgt_index, spot, tgt_count)
        held[there] = columns[spot][...]
        far_values[pl.ds(there, 1), :] = columns[spot][pl.ds(4 * node_rows + 1, 1), pl.ds(0, 128)]
    for shift in range(src_count):
        there = lax.rem(src_index - shift + src_count, src_count)
        here = pl.ds(pl.multiple_of(there * rank, rank), rank)
        row_bases[here, :] = bases[shift][pl.ds(0, rank), :]
        col_bases[here, :] = bases[shift][pl.ds(rank, rank), :]
        for coord in range(3):
            point_rows[coord, pl.ds(there, 1), :] = bases[shift][pl.ds(2 * rank + coord, 1), :]
    for spot in range(tgt_count):
        built[spot] = 0
    node_staged[...] = jnp.zeros_like(node_staged)
    point_staged[...] = jnp.zeros_like(point_staged)
    rows = rows_of(src_count)
    halves = leaf // 128
    coords = [point_rows[coord] for coord in range(3)]
    store_terms(point_staged, distance_terms(coords, spread_sq, -2.0), rows)
    for target in range(src_count):
        for half in range(halves):
            across = point_staged[half, pl.ds(target, term_count, stride=rows), :]
            point_terms[target, pl.ds(half * 128, 128), :] = jnp.transpose(across).astype(
                jnp.bfloat16
            )
    live = near_count[0]
    block = 128

    def one_slot(slot, carry):
        target = near_list[0, slot] - tgt_index * src_count
        source = near_list[1, slot] // src_count
        keep[pl.ds(target * tgt_count + source, 1), :] = jnp.zeros((1, 128), jnp.float32)

        @pl.when(built[source] == 0)
        def _():
            built[source] = 1
            coords = [held[source, pl.ds(coord * node_rows, node_rows), :] for coord in range(3)]
            store_terms(node_staged, distance_terms(coords, 0.0, 1.0), node_rows)
            for node in range(node_rows):
                for half in range(halves):
                    across = node_staged[half, pl.ds(node, term_count, stride=node_rows), :]
                    node_terms[source, node, :, pl.ds(half * 128, 128)] = across.astype(jnp.bfloat16)

        vector = held[source, pl.ds(4 * node_rows, 1), :]

        def one_block(number, inner):
            start = pl.multiple_of(number * block, block)
            here = pl.ds(start, block)
            lhs = point_terms[target, here, :]
            tile = None
            for node in range(node_rows):
                square = lax.dot_general(
                    lhs,
                    node_terms[source, node],
                    plain_contract,
                    preferred_element_type=jnp.float32,
                )
                term = held[source, pl.ds(3 * node_rows + node, 1), :] * lax.rsqrt(square)
                tile = term if tile is None else tile + term
            tiles[slot, here, :] = tile
            add_product(partial, target, start, block, tile, vector)
            return inner

        lax.fori_loop(0, leaf // block, one_block, 0)
        return carry

    lax.fori_loop(0, live, one_slot, 0)
    near = near_rows(partial, src_count, leaf)
    far = far_rows(far_values[...], coupling, keep, row_bases, src_count, tgt_count, rank)
    total = near + far
    stacked = src_count * rank
    coeffs = lax.dot_general(
        total, col_bases[...], lane_contract, precision=highest, preferred_element_type=jnp.float32
    )
    own = (iota((rows, stacked), 1) // rank) == (iota((rows, stacked), 0) % src_count)
    coeffs = jnp.where(own, coeffs, 0.0)
    for start in range(0, src_count * tgt_count, rows):
        message[pl.ds(start, rows), 0, pl.ds(0, leaf)] = total
        message[pl.ds(start, rows), 0, pl.ds(leaf, stacked)] = coeffs


def column_place(tgt_index, spot, tgt_count):
    group = 2 if tgt_count % 2 == 0 else 1
    lines = tgt_count // group
    shift, flip = spot % lines, spot // lines
    line = lax.rem(tgt_index // group - shift + lines, lines)
    return line * group + lax.rem(tgt_index % group + flip, group)


def second_kernel(
    near_list,
    near_count,
    coupling,
    received,
    values,
    row_bases,
    tiles,
    message,
    partial,
    keep,
    image,
    *,
    src_count,
    tgt_count,
    rank,
    leaf,
):
    tgt_index = lax.axis_index("tgt")
    live = near_count[0]
    clear_partials(partial, keep, src_count)
    stacked = src_count * rank
    groups = (tgt_count, src_count * tgt_count)
    flags = ((iota(groups, 1) // src_count) == iota(groups, 0)).astype(jnp.bfloat16)
    image[...] = exact_pick(flags, received[:, 0, :])
    block = 64

    def one_slot(slot, carry):
        target = near_list[0, slot] - tgt_index * src_count
        source = near_list[1, slot] // src_count
        keep[pl.ds(target * tgt_count + source, 1), :] = jnp.zeros((1, 128), jnp.float32)
        vector = image[pl.ds(source, 1), pl.ds(0, leaf)]
        for start in range(0, leaf, block):
            add_product(partial, target, start, block, tiles[slot, pl.ds(start, block), :], vector)
        return carry

    lax.fori_loop(0, live, one_slot, 0)
    near = near_rows(partial, src_count, leaf)
    far = far_rows(
        image[:, pl.ds(leaf, stacked)], coupling, keep, row_bases, src_count, tgt_count, rank
    )
    total = near + far
    pieces = [total[target : target + 1] for target in range(src_count)]
    pieces.append(image[pl.ds(tgt_index, 1), pl.ds(0, leaf)])
    pieces.append(values[...])
    for number, piece in enumerate(pieces):
        message[:, 0, pl.ds(number * leaf, leaf)] = jnp.broadcast_to(piece, (message.shape[0], leaf))


def third_kernel(received, result, *, src_count, tgt_count, leaf):
    def inner(left, right):
        return jnp.sum(left * right, axis=0, keepdims=True)

    devices = src_count * tgt_count
    groups = (tgt_count, devices)
    flags = ((iota(groups, 1) // src_count) == iota(groups, 0)).astype(jnp.bfloat16)
    batch = 4 if src_count % 4 == 0 else 1
    picked = []
    for first in range(0, src_count, batch):
        images = exact_pick(flags, received[:, 0, pl.ds(first * leaf, batch * leaf)])
        shape = (batch * tgt_count, devices)
        place = (iota(shape, 0) % tgt_count) * src_count + iota(shape, 0) // tgt_count + first
        own_flags = (iota(shape, 1) == place).astype(jnp.bfloat16)
        others = exact_pick(own_flags, received[:, 0, pl.ds(src_count * leaf, 2 * leaf)])
        for number in range(batch):
            mine = slice(number * tgt_count, (number + 1) * tgt_count)
            twice = images[:, number * leaf : (number + 1) * leaf]
            picked.append((others[mine, leaf:], others[mine, :leaf], twice))
    sums = None
    for start, once, twice in picked:
        pairs = [
            (start, start),
            (start, once),
            (once, once),
            (start, twice),
            (once, twice),
            (twice, twice),
        ]
        products = [inner(left, right) for left, right in pairs]
        sums = products if sums is None else [old + new for old, new in zip(sums, products)]
    g00, g01, g11, g02, g12, g22 = [jnp.sum(value, axis=1, keepdims=True) for value in sums]
    rhs_norm = jnp.sqrt(g00 + norm_floor)
    scale = 1.0 / rhs_norm
    proj_first = scale * scale * (0.5 * g00 + g01)
    left = 0.5 - proj_first
    rest_sq = scale * scale * (left * left * g00 + 2.0 * left * g01 + g11)
    height_first = jnp.sqrt(jnp.maximum(rest_sq, 0.0) + norm_floor)
    c1 = scale / height_first
    c0 = left * c1
    i0 = 0.5 * c0
    i1 = 0.5 * c1 + c0
    i2 = c1
    to_start = i0 * g00 + i1 * g01 + i2 * g02
    to_once = i0 * g01 + i1 * g11 + i2 * g12
    proj_cross = scale * to_start
    proj_second = c0 * to_start + c1 * to_once
    r0 = i0 - proj_cross * scale - proj_second * c0
    r1 = i1 - proj_second * c1
    r2 = i2
    last_sq = (
        r0 * (r0 * g00 + 2.0 * (r1 * g01 + r2 * g02))
        + r1 * (r1 * g11 + 2.0 * r2 * g12)
        + r2 * r2 * g22
    )
    height_second = jnp.sqrt(jnp.maximum(last_sq, 0.0) + norm_floor)
    radius_first = jnp.sqrt(proj_first * proj_first + height_first * height_first)
    cos_first = proj_first / radius_first
    sin_first = height_first / radius_first
    rotated_top = cos_first * proj_cross + sin_first * proj_second
    rotated_low = cos_first * proj_second - sin_first * proj_cross
    radius_second = jnp.sqrt(rotated_low * rotated_low + height_second * height_second)
    coeff_second = -sin_first * rhs_norm * (rotated_low / radius_second) / radius_second
    coeff_first = (cos_first * rhs_norm - rotated_top * coeff_second) / radius_first
    me = lax.axis_index("tgt") * src_count + lax.axis_index("src")
    once = received[me, :, pl.ds(src_count * leaf, leaf)]
    start = received[me, :, pl.ds((src_count + 1) * leaf, leaf)]
    result[...] = (coeff_first * scale + coeff_second * c0) * start + (coeff_second * c1) * once


def per_device(
    right_side,
    targets,
    source_nodes,
    node_weights,
    near_list,
    near_count,
    row_basis,
    column_basis,
    coupling,
):
    src_count = lax.axis_size("src")
    tgt_count = lax.axis_size("tgt")
    leaf = right_side.shape[0]
    node_rows = node_weights.shape[0]
    rank = row_basis.shape[1]
    slots = near_list.shape[1]
    stacked = src_count * rank
    device_count = src_count * tgt_count
    values = right_side.reshape(1, leaf)
    couplings = coupling.reshape(src_count * tgt_count, rank * rank)
    packed_rows = 4 * node_rows + 8

    basis_rows = 2 * rank + 8
    packed, basis = pl.pallas_call(
        functools.partial(pack_kernel, node_rows=node_rows, rank=rank),
        out_shape=(
            jax.ShapeDtypeStruct((packed_rows, leaf), jnp.float32),
            jax.ShapeDtypeStruct((basis_rows, leaf), jnp.float32),
        ),
        in_specs=[vmem_space] * 6,
        out_specs=(vmem_space, vmem_space),
        compiler_params=kernel_params,
        name="pack",
    )(source_nodes, node_weights, values, targets, row_basis, column_basis)

    group = 2 if tgt_count % 2 == 0 else 1
    lines = tgt_count // group

    def from_line(value, shift):
        pairs = [
            (tgt, ((tgt // group + shift) % lines) * group + tgt % group) for tgt in range(tgt_count)
        ]
        return lax.ppermute(value, "tgt", pairs)

    def from_flip(value):
        return lax.ppermute(value, "tgt", [(tgt, tgt ^ 1) for tgt in range(tgt_count)])

    def from_source(value, shift):
        return lax.ppermute(value, "src", [(src, (src + shift) % src_count) for src in range(src_count)])

    columns = [packed] + [from_line(packed, shift) for shift in range(1, lines)]
    if group == 2:
        columns = columns + [from_flip(value) for value in columns]
    bases = [basis] + [from_source(basis, shift) for shift in range(1, src_count)]

    sizes = dict(src_count=src_count, tgt_count=tgt_count, rank=rank, leaf=leaf)
    message, tiles, row_bases = pl.pallas_call(
        functools.partial(first_kernel, node_rows=node_rows, **sizes),
        out_shape=(
            jax.ShapeDtypeStruct((device_count, 1, leaf + stacked), jnp.float32),
            jax.ShapeDtypeStruct((slots, leaf, leaf), jnp.float32),
            jax.ShapeDtypeStruct((stacked, leaf), jnp.float32),
        ),
        in_specs=[smem_space, smem_space] + [vmem_space] * (1 + tgt_count + src_count),
        out_specs=(vmem_space, vmem_space, vmem_space),
        scratch_shapes=[
            pltpu.VMEM((tgt_count, packed_rows, leaf), jnp.float32),
            pltpu.VMEM((stacked, leaf), jnp.float32),
            pltpu.VMEM((3, rows_of(src_count), leaf), jnp.float32),
            pltpu.VMEM((leaf // 128, term_count * rows_of(src_count), 128), jnp.float32),
            pltpu.VMEM((src_count, leaf, term_count), jnp.bfloat16),
            pltpu.VMEM((leaf // 128, term_count * node_rows, 128), jnp.float32),
            pltpu.VMEM((tgt_count, node_rows, term_count, leaf), jnp.bfloat16),
            pltpu.SMEM((tgt_count,), jnp.int32),
            pltpu.VMEM((src_count, leaf, 128), jnp.float32),
            pltpu.VMEM((src_count * tgt_count, 128), jnp.float32),
            pltpu.VMEM((tgt_count, 128), jnp.float32),
        ],
        compiler_params=kernel_params,
        name="first",
    )(near_list, near_count, couplings, *columns, *bases)

    received = lax.all_to_all(message, both_axes, 0, 0, tiled=True)

    message = pl.pallas_call(
        functools.partial(second_kernel, **sizes),
        out_shape=jax.ShapeDtypeStruct((device_count, 1, (src_count + 2) * leaf), jnp.float32),
        in_specs=[smem_space, smem_space] + [vmem_space] * 5,
        out_specs=vmem_space,
        scratch_shapes=[
            pltpu.VMEM((src_count, leaf, 128), jnp.float32),
            pltpu.VMEM((src_count * tgt_count, 128), jnp.float32),
            pltpu.VMEM((tgt_count, leaf + stacked), jnp.float32),
        ],
        compiler_params=kernel_params,
        name="second",
    )(near_list, near_count, couplings, received, values, row_bases, tiles)

    received = lax.all_to_all(message, both_axes, 0, 0, tiled=True)

    result = pl.pallas_call(
        functools.partial(third_kernel, src_count=src_count, tgt_count=tgt_count, leaf=leaf),
        out_shape=jax.ShapeDtypeStruct((1, leaf), jnp.float32),
        in_specs=[vmem_space],
        out_specs=vmem_space,
        compiler_params=kernel_params,
        name="third",
    )(received)
    return result.reshape(leaf)


def solution(mesh):
    return jax.shard_map(
        per_device,
        mesh=mesh,
        in_specs=(
            P(("tgt", "src")),
            P(None, ("tgt", "src")),
            P(None, None, ("tgt", "src")),
            P(None, ("tgt", "src")),
            P(None, ("tgt", "src")),
            P(("tgt", "src")),
            P(("tgt", "src"), None, None),
            P(("tgt", "src"), None, None),
            P("tgt", None, None, "src", None),
        ),
        out_specs=P(("tgt", "src")),
        check_vma=False,
    )
```

```python
import functools

import jax
import jax.numpy as jnp
from jax import lax
from jax.experimental import pallas as pl
from jax.experimental.pallas import tpu as pltpu
from jax.sharding import PartitionSpec as P

spread_sq = 0.0004
norm_floor = 1e-06
highest = lax.Precision.HIGHEST
both_axes = ("tgt", "src")
lane_contract = (((1,), (1,)), ((), ()))
plain_contract = (((1,), (0,)), ((), ()))
term_count = 48
vmem_space = pl.BlockSpec(memory_space=pltpu.VMEM)
smem_space = pl.BlockSpec(memory_space=pltpu.SMEM)
hbm_space = pl.BlockSpec(memory_space=pltpu.HBM)
kernel_params = pltpu.CompilerParams(vmem_limit_bytes=32 * 1024 * 1024)


def in_three(value):
    top = value.astype(jnp.bfloat16)
    rest = value - top.astype(jnp.float32)
    middle = rest.astype(jnp.bfloat16)
    low = (rest - middle.astype(jnp.float32)).astype(jnp.bfloat16)
    return top, middle, low


def exact_dot(value, flags, contract):
    parts = [
        lax.dot_general(part, flags, contract, preferred_element_type=jnp.float32)
        for part in in_three(value)
    ]
    return parts[0] + (parts[1] + parts[2])


def exact_pick(flags, value):
    parts = [
        lax.dot_general(flags, part, plain_contract, preferred_element_type=jnp.float32)
        for part in in_three(value)
    ]
    return parts[0] + (parts[1] + parts[2])


def iota(shape, dim):
    return lax.broadcasted_iota(jnp.int32, shape, dim)


def rows_of(src_count):
    return max(8, src_count)


def on_grid(value, steps):
    return lax.round(value * steps, lax.RoundingMethod.TO_NEAREST_EVEN) * (1.0 / steps)


def as_bfloat16(value):
    return value.astype(jnp.bfloat16).astype(jnp.float32)


def coordinate_parts(coords):
    parts = []
    for value in coords:
        high = on_grid(value, 128.0)
        rest = value - high
        mid = on_grid(rest, 32768.0)
        parts.append((high, mid, as_bfloat16(rest - mid)))
    return parts


def distance_terms(coords, shift, factor):
    parts = coordinate_parts(coords)
    high_sum = sum(high * high for high, mid, low in parts)
    top = as_bfloat16(high_sum)
    rest_sum = sum((mid + low) * (2.0 * high + (mid + low)) for high, mid, low in parts) + shift
    first = as_bfloat16(rest_sum)
    second = as_bfloat16(rest_sum - first)
    third = rest_sum - first - second
    squares = [top, high_sum - top]
    rests = [first, second, third]
    ones = [jnp.ones_like(top)]
    crosses = [tuple(factor * piece for piece in part) for part in parts]
    terms = {}
    if factor == 1.0:
        terms.update(zip(range(0, 4), ones * 2 + squares))
        terms.update(zip(range(16, 22), ones * 3 + rests))
        order = (1, 2, 0, 0, 1, 2, 1)
    else:
        terms.update(zip(range(0, 4), squares + ones * 2))
        terms.update(zip(range(16, 22), rests + ones * 3))
        order = (0, 0, 1, 2, 1, 1, 2)
    for coord in range(3):
        terms[4 + coord] = crosses[coord][0]
        for number, piece in enumerate(order):
            terms[22 + 7 * coord + number] = crosses[coord][piece]
    return terms


def store_terms(staged, terms, rows):
    for number, value in terms.items():
        for half in range(staged.shape[0]):
            staged[half, pl.ds(number * rows, rows), :] = value[:, half * 128 : (half + 1) * 128]


def pack_kernel(
    nodes,
    weights,
    values_in,
    targets,
    row_basis,
    column_basis,
    near_in,
    coupling_in,
    packed,
    basis,
    near,
    coupling,
    values,
    points,
    sems,
    *,
    node_rows,
    rank,
):
    pieces = [
        (column_basis.at[0], basis.at[pl.ds(rank, rank), :]),
        (values_in, values),
        (targets, points),
        (row_basis.at[0], basis.at[pl.ds(0, rank), :]),
        (weights, packed.at[pl.ds(3 * node_rows, node_rows), :]),
        (near_in, near),
        (coupling_in, coupling),
    ]
    for coord in range(3):
        pieces.append((nodes.at[coord], packed.at[pl.ds(coord * node_rows, node_rows), :]))
    copies = [
        pltpu.make_async_copy(source, place, sems.at[number])
        for number, (source, place) in enumerate(pieces)
    ]
    for copy in copies:
        copy.start()
    leaf = values.shape[1]
    packed[pl.ds(4 * node_rows, 8), :] = jnp.zeros((8, leaf), jnp.float32)
    basis[pl.ds(2 * rank, 8), :] = jnp.zeros((8, leaf), jnp.float32)
    for copy in copies[:3]:
        copy.wait()
    vector = values[...]
    packed[pl.ds(4 * node_rows, 1), :] = vector
    tall = jnp.broadcast_to(vector, (8, leaf))
    coeffs = lax.dot_general(
        tall,
        basis[pl.ds(rank, rank), :],
        lane_contract,
        precision=highest,
        preferred_element_type=jnp.float32,
    )
    packed[pl.ds(4 * node_rows + 1, 1), pl.ds(0, rank)] = coeffs[0:1]
    basis[pl.ds(2 * rank, 3), :] = points[...]
    for copy in copies[3:]:
        copy.wait()


def far_rows(coeffs, coupling, keep, row_bases, src_count, tgt_count, rank):
    rows = rows_of(src_count)
    width = coeffs.shape[1]
    spread_flags = (
        (iota((width, rank * rank), 0) % rank) == (iota((width, rank * rank), 1) % rank)
    ).astype(jnp.bfloat16)
    tiled = exact_dot(coeffs, spread_flags, plain_contract)
    row_id = iota((rows, rank * rank), 0) % src_count
    summed = jnp.zeros((rows, rank * rank), jnp.float32)
    for target in range(src_count):
        block = coupling[pl.ds(target * tgt_count, tgt_count), 0, :]
        kept = keep[pl.ds(target * tgt_count, tgt_count), :]
        block = block * jnp.concatenate([kept] * (rank * rank // 128), axis=1)
        total = jnp.sum(block * tiled, axis=0, keepdims=True)
        summed = jnp.where(row_id == target, total, summed)
    stacked = src_count * rank
    group_flags = (
        (iota((stacked, rank * rank), 1) // rank) == (iota((stacked, rank * rank), 0) % rank)
    ).astype(jnp.bfloat16)
    far = exact_dot(summed, group_flags, lane_contract)
    own = (iota((rows, stacked), 1) // rank) == (iota((rows, stacked), 0) % src_count)
    far = jnp.where(own, far, 0.0)
    return lax.dot_general(
        far, row_bases[...], plain_contract, precision=highest, preferred_element_type=jnp.float32
    )


def near_rows(partial, src_count, leaf):
    rows = rows_of(src_count)
    ones = jnp.ones((8, 128), jnp.bfloat16)
    row_id = iota((rows, leaf), 0) % src_count
    result = jnp.zeros((rows, leaf), jnp.float32)
    for target in range(src_count):
        block = partial[target]
        parts = [
            lax.dot_general(ones, part, lane_contract, preferred_element_type=jnp.float32)
            for part in in_three(block)
        ]
        total = (parts[0] + (parts[1] + parts[2]))[0:1]
        result = jnp.where(row_id == target, total, result)
    return result


def clear_partials(partial, keep, src_count):
    keep[...] = jnp.ones_like(keep)
    for target in range(src_count):
        partial[target] = jnp.zeros(partial.shape[1:], jnp.float32)


def add_product(partial, target, start, size, tile, vector):
    half = vector * tile
    total = half[:, 0:128]
    for lane in range(128, tile.shape[1], 128):
        total = total + half[:, lane : lane + 128]
    here = pl.ds(start, size)
    partial[target, here, :] = partial[target, here, :] + total


def first_kernel(
    near_list, near_count, coupling, *refs, src_count, tgt_count, node_rows, rank, leaf
):
    columns, refs = refs[:tgt_count], refs[tgt_count:]
    bases, refs = refs[:src_count], refs[src_count:]
    message, tiles, row_bases = refs[:3]
    held, col_bases, point_rows, point_staged, point_terms = refs[3:8]
    node_staged, node_terms, built, partial, keep, far_values = refs[8:]
    tgt_index = lax.axis_index("tgt")
    src_index = lax.axis_index("src")
    clear_partials(partial, keep, src_count)
    for spot in range(tgt_count):
        there = column_place(tgt_index, spot, tgt_count)
        held[there] = columns[spot][...]
        far_values[pl.ds(there, 1), :] = columns[spot][pl.ds(4 * node_rows + 1, 1), pl.ds(0, 128)]
    for shift in range(src_count):
        there = lax.rem(src_index - shift + src_count, src_count)
        here = pl.ds(pl.multiple_of(there * rank, rank), rank)
        row_bases[here, :] = bases[shift][pl.ds(0, rank), :]
        col_bases[here, :] = bases[shift][pl.ds(rank, rank), :]
        for coord in range(3):
            point_rows[coord, pl.ds(there, 1), :] = bases[shift][pl.ds(2 * rank + coord, 1), :]
    for spot in range(tgt_count):
        built[spot] = 0
    node_staged[...] = jnp.zeros_like(node_staged)
    point_staged[...] = jnp.zeros_like(point_staged)
    rows = rows_of(src_count)
    halves = leaf // 128
    coords = [point_rows[coord] for coord in range(3)]
    store_terms(point_staged, distance_terms(coords, spread_sq, -2.0), rows)
    for target in range(src_count):
        for half in range(halves):
            across = point_staged[half, pl.ds(target, term_count, stride=rows), :]
            point_terms[target, pl.ds(half * 128, 128), :] = jnp.transpose(across).astype(
                jnp.bfloat16
            )
    live = near_count[0]
    block = 128

    def one_slot(slot, carry):
        target = near_list[0, slot] - tgt_index * src_count
        source = near_list[1, slot] // src_count
        keep[pl.ds(target * tgt_count + source, 1), :] = jnp.zeros((1, 128), jnp.float32)

        @pl.when(built[source] == 0)
        def _():
            built[source] = 1
            coords = [held[source, pl.ds(coord * node_rows, node_rows), :] for coord in range(3)]
            store_terms(node_staged, distance_terms(coords, 0.0, 1.0), node_rows)
            for node in range(node_rows):
                for half in range(halves):
                    across = node_staged[half, pl.ds(node, term_count, stride=node_rows), :]
                    node_terms[source, node, :, pl.ds(half * 128, 128)] = across.astype(jnp.bfloat16)

        vector = held[source, pl.ds(4 * node_rows, 1), :]

        def one_block(number, inner):
            start = pl.multiple_of(number * block, block)
            here = pl.ds(start, block)
            lhs = point_terms[target, here, :]
            tile = None
            for node in range(node_rows):
                square = lax.dot_general(
                    lhs,
                    node_terms[source, node],
                    plain_contract,
                    preferred_element_type=jnp.float32,
                )
                term = held[source, pl.ds(3 * node_rows + node, 1), :] * lax.rsqrt(square)
                tile = term if tile is None else tile + term
            tiles[slot, here, :] = tile
            add_product(partial, target, start, block, tile, vector)
            return inner

        lax.fori_loop(0, leaf // block, one_block, 0)
        return carry

    lax.fori_loop(0, live, one_slot, 0)
    near = near_rows(partial, src_count, leaf)
    far = far_rows(far_values[...], coupling, keep, row_bases, src_count, tgt_count, rank)
    total = near + far
    stacked = src_count * rank
    coeffs = lax.dot_general(
        total, col_bases[...], lane_contract, precision=highest, preferred_element_type=jnp.float32
    )
    own = (iota((rows, stacked), 1) // rank) == (iota((rows, stacked), 0) % src_count)
    coeffs = jnp.where(own, coeffs, 0.0)
    for start in range(0, src_count * tgt_count, rows):
        message[pl.ds(start, rows), 0, pl.ds(0, leaf)] = total
        message[pl.ds(start, rows), 0, pl.ds(leaf, stacked)] = coeffs


def column_place(tgt_index, spot, tgt_count):
    group = 2 if tgt_count % 2 == 0 else 1
    lines = tgt_count // group
    shift, flip = spot % lines, spot // lines
    line = lax.rem(tgt_index // group - shift + lines, lines)
    return line * group + lax.rem(tgt_index % group + flip, group)


def second_kernel(
    near_list,
    near_count,
    coupling,
    received,
    values,
    row_bases,
    tiles,
    message,
    partial,
    keep,
    image,
    *,
    src_count,
    tgt_count,
    rank,
    leaf,
):
    tgt_index = lax.axis_index("tgt")
    live = near_count[0]
    clear_partials(partial, keep, src_count)
    stacked = src_count * rank
    groups = (tgt_count, src_count * tgt_count)
    flags = ((iota(groups, 1) // src_count) == iota(groups, 0)).astype(jnp.bfloat16)
    image[...] = exact_pick(flags, received[:, 0, :])
    block = 64

    def one_slot(slot, carry):
        target = near_list[0, slot] - tgt_index * src_count
        source = near_list[1, slot] // src_count
        keep[pl.ds(target * tgt_count + source, 1), :] = jnp.zeros((1, 128), jnp.float32)
        vector = image[pl.ds(source, 1), pl.ds(0, leaf)]
        for start in range(0, leaf, block):
            add_product(partial, target, start, block, tiles[slot, pl.ds(start, block), :], vector)
        return carry

    lax.fori_loop(0, live, one_slot, 0)
    near = near_rows(partial, src_count, leaf)
    far = far_rows(
        image[:, pl.ds(leaf, stacked)], coupling, keep, row_bases, src_count, tgt_count, rank
    )
    total = near + far
    pieces = [total[target : target + 1] for target in range(src_count)]
    pieces.append(image[pl.ds(tgt_index, 1), pl.ds(0, leaf)])
    pieces.append(values[...])
    for number, piece in enumerate(pieces):
        message[:, 0, pl.ds(number * leaf, leaf)] = jnp.broadcast_to(piece, (message.shape[0], leaf))


def third_kernel(received, result, *, src_count, tgt_count, leaf):
    def inner(left, right):
        return jnp.sum(left * right, axis=0, keepdims=True)

    devices = src_count * tgt_count
    groups = (tgt_count, devices)
    flags = ((iota(groups, 1) // src_count) == iota(groups, 0)).astype(jnp.bfloat16)
    batch = 4 if src_count % 4 == 0 else 1
    picked = []
    for first in range(0, src_count, batch):
        images = exact_pick(flags, received[:, 0, pl.ds(first * leaf, batch * leaf)])
        shape = (batch * tgt_count, devices)
        place = (iota(shape, 0) % tgt_count) * src_count + iota(shape, 0) // tgt_count + first
        own_flags = (iota(shape, 1) == place).astype(jnp.bfloat16)
        others = exact_pick(own_flags, received[:, 0, pl.ds(src_count * leaf, 2 * leaf)])
        for number in range(batch):
            mine = slice(number * tgt_count, (number + 1) * tgt_count)
            twice = images[:, number * leaf : (number + 1) * leaf]
            picked.append((others[mine, leaf:], others[mine, :leaf], twice))
    sums = None
    for start, once, twice in picked:
        pairs = [
            (start, start),
            (start, once),
            (once, once),
            (start, twice),
            (once, twice),
            (twice, twice),
        ]
        products = [inner(left, right) for left, right in pairs]
        sums = products if sums is None else [old + new for old, new in zip(sums, products)]
    g00, g01, g11, g02, g12, g22 = [jnp.sum(value, axis=1, keepdims=True) for value in sums]
    rhs_norm = jnp.sqrt(g00 + norm_floor)
    scale = 1.0 / rhs_norm
    proj_first = scale * scale * (0.5 * g00 + g01)
    left = 0.5 - proj_first
    rest_sq = scale * scale * (left * left * g00 + 2.0 * left * g01 + g11)
    height_first = jnp.sqrt(jnp.maximum(rest_sq, 0.0) + norm_floor)
    c1 = scale / height_first
    c0 = left * c1
    i0 = 0.5 * c0
    i1 = 0.5 * c1 + c0
    i2 = c1
    to_start = i0 * g00 + i1 * g01 + i2 * g02
    to_once = i0 * g01 + i1 * g11 + i2 * g12
    proj_cross = scale * to_start
    proj_second = c0 * to_start + c1 * to_once
    r0 = i0 - proj_cross * scale - proj_second * c0
    r1 = i1 - proj_second * c1
    r2 = i2
    last_sq = (
        r0 * (r0 * g00 + 2.0 * (r1 * g01 + r2 * g02))
        + r1 * (r1 * g11 + 2.0 * r2 * g12)
        + r2 * r2 * g22
    )
    height_second = jnp.sqrt(jnp.maximum(last_sq, 0.0) + norm_floor)
    radius_first = jnp.sqrt(proj_first * proj_first + height_first * height_first)
    cos_first = proj_first / radius_first
    sin_first = height_first / radius_first
    rotated_top = cos_first * proj_cross + sin_first * proj_second
    rotated_low = cos_first * proj_second - sin_first * proj_cross
    radius_second = jnp.sqrt(rotated_low * rotated_low + height_second * height_second)
    coeff_second = -sin_first * rhs_norm * (rotated_low / radius_second) / radius_second
    coeff_first = (cos_first * rhs_norm - rotated_top * coeff_second) / radius_first
    me = lax.axis_index("tgt") * src_count + lax.axis_index("src")
    once = received[me, :, pl.ds(src_count * leaf, leaf)]
    start = received[me, :, pl.ds((src_count + 1) * leaf, leaf)]
    result[...] = (coeff_first * scale + coeff_second * c0) * start + (coeff_second * c1) * once


def per_device(
    right_side,
    targets,
    source_nodes,
    node_weights,
    near_list,
    near_count,
    row_basis,
    column_basis,
    coupling,
):
    src_count = lax.axis_size("src")
    tgt_count = lax.axis_size("tgt")
    leaf = right_side.shape[0]
    node_rows = node_weights.shape[0]
    rank = row_basis.shape[1]
    slots = near_list.shape[1]
    stacked = src_count * rank
    device_count = src_count * tgt_count
    values = right_side.reshape(1, leaf)
    couplings = coupling.reshape(src_count * tgt_count, 1, rank * rank)
    packed_rows = 4 * node_rows + 8

    basis_rows = 2 * rank + 8
    packed, basis, near_list, couplings, values = pl.pallas_call(
        functools.partial(pack_kernel, node_rows=node_rows, rank=rank),
        out_shape=(
            jax.ShapeDtypeStruct((packed_rows, leaf), jnp.float32),
            jax.ShapeDtypeStruct((basis_rows, leaf), jnp.float32),
            jax.ShapeDtypeStruct(near_list.shape, jnp.int32),
            jax.ShapeDtypeStruct(couplings.shape, jnp.float32),
            jax.ShapeDtypeStruct(values.shape, jnp.float32),
        ),
        in_specs=[hbm_space] * 8,
        out_specs=(vmem_space,) * 5,
        scratch_shapes=[
            pltpu.VMEM(targets.shape, jnp.float32),
            pltpu.SemaphoreType.DMA((10,)),
        ],
        compiler_params=kernel_params,
        name="pack",
    )(
        *[
            pltpu.with_memory_space_constraint(value, pltpu.HBM)
            for value in (
                source_nodes,
                node_weights,
                values,
                targets,
                row_basis,
                column_basis,
                near_list,
                couplings,
            )
        ]
    )

    group = 2 if tgt_count % 2 == 0 else 1
    lines = tgt_count // group

    def from_line(value, shift):
        pairs = [
            (tgt, ((tgt // group + shift) % lines) * group + tgt % group) for tgt in range(tgt_count)
        ]
        return lax.ppermute(value, "tgt", pairs)

    def from_flip(value):
        return lax.ppermute(value, "tgt", [(tgt, tgt ^ 1) for tgt in range(tgt_count)])

    def from_source(value, shift):
        return lax.ppermute(value, "src", [(src, (src + shift) % src_count) for src in range(src_count)])

    columns = [packed] + [from_line(packed, shift) for shift in range(1, lines)]
    if group == 2:
        columns = columns + [from_flip(value) for value in columns]
    bases = [basis] + [from_source(basis, shift) for shift in range(1, src_count)]

    sizes = dict(src_count=src_count, tgt_count=tgt_count, rank=rank, leaf=leaf)
    message, tiles, row_bases = pl.pallas_call(
        functools.partial(first_kernel, node_rows=node_rows, **sizes),
        out_shape=(
            jax.ShapeDtypeStruct((device_count, 1, leaf + stacked), jnp.float32),
            jax.ShapeDtypeStruct((slots, leaf, leaf), jnp.float32),
            jax.ShapeDtypeStruct((stacked, leaf), jnp.float32),
        ),
        in_specs=[smem_space, smem_space] + [vmem_space] * (1 + tgt_count + src_count),
        out_specs=(vmem_space, vmem_space, vmem_space),
        scratch_shapes=[
            pltpu.VMEM((tgt_count, packed_rows, leaf), jnp.float32),
            pltpu.VMEM((stacked, leaf), jnp.float32),
            pltpu.VMEM((3, rows_of(src_count), leaf), jnp.float32),
            pltpu.VMEM((leaf // 128, term_count * rows_of(src_count), 128), jnp.float32),
            pltpu.VMEM((src_count, leaf, term_count), jnp.bfloat16),
            pltpu.VMEM((leaf // 128, term_count * node_rows, 128), jnp.float32),
            pltpu.VMEM((tgt_count, node_rows, term_count, leaf), jnp.bfloat16),
            pltpu.SMEM((tgt_count,), jnp.int32),
            pltpu.VMEM((src_count, leaf, 128), jnp.float32),
            pltpu.VMEM((src_count * tgt_count, 128), jnp.float32),
            pltpu.VMEM((tgt_count, 128), jnp.float32),
        ],
        compiler_params=kernel_params,
        name="first",
    )(near_list, near_count, couplings, *columns, *bases)

    received = lax.all_to_all(message, both_axes, 0, 0, tiled=True)

    message = pl.pallas_call(
        functools.partial(second_kernel, **sizes),
        out_shape=jax.ShapeDtypeStruct((device_count, 1, (src_count + 2) * leaf), jnp.float32),
        in_specs=[smem_space, smem_space] + [vmem_space] * 5,
        out_specs=vmem_space,
        scratch_shapes=[
            pltpu.VMEM((src_count, leaf, 128), jnp.float32),
            pltpu.VMEM((src_count * tgt_count, 128), jnp.float32),
            pltpu.VMEM((tgt_count, leaf + stacked), jnp.float32),
        ],
        compiler_params=kernel_params,
        name="second",
    )(near_list, near_count, couplings, received, values, row_bases, tiles)

    received = lax.all_to_all(message, both_axes, 0, 0, tiled=True)

    result = pl.pallas_call(
        functools.partial(third_kernel, src_count=src_count, tgt_count=tgt_count, leaf=leaf),
        out_shape=jax.ShapeDtypeStruct((1, leaf), jnp.float32),
        in_specs=[vmem_space],
        out_specs=vmem_space,
        compiler_params=kernel_params,
        name="third",
    )(received)
    return result.reshape(leaf)


def solution(mesh):
    return jax.shard_map(
        per_device,
        mesh=mesh,
        in_specs=(
            P(("tgt", "src")),
            P(None, ("tgt", "src")),
            P(None, None, ("tgt", "src")),
            P(None, ("tgt", "src")),
            P(None, ("tgt", "src")),
            P(("tgt", "src")),
            P(("tgt", "src"), None, None),
            P(("tgt", "src"), None, None),
            P("tgt", None, None, "src", None),
        ),
        out_specs=P(("tgt", "src")),
        check_vma=False,
    )
```

```python
import functools

import jax
import jax.numpy as jnp
from jax import lax
from jax.experimental import pallas as pl
from jax.experimental.pallas import tpu as pltpu
from jax.sharding import PartitionSpec as P

spread_sq = 0.0004
norm_floor = 1e-06
highest = lax.Precision.HIGHEST
both_axes = ("tgt", "src")
lane_contract = (((1,), (1,)), ((), ()))
plain_contract = (((1,), (0,)), ((), ()))
unique_terms = 16
term_repeats = 4
term_count = unique_terms * term_repeats
vmem_space = pl.BlockSpec(memory_space=pltpu.VMEM)
smem_space = pl.BlockSpec(memory_space=pltpu.SMEM)
hbm_space = pl.BlockSpec(memory_space=pltpu.HBM)
kernel_params = pltpu.CompilerParams(vmem_limit_bytes=32 * 1024 * 1024)


def in_three(value):
    top = value.astype(jnp.bfloat16)
    rest = value - top.astype(jnp.float32)
    middle = rest.astype(jnp.bfloat16)
    low = (rest - middle.astype(jnp.float32)).astype(jnp.bfloat16)
    return top, middle, low


def exact_dot(value, flags, contract):
    parts = [
        lax.dot_general(part, flags, contract, preferred_element_type=jnp.float32)
        for part in in_three(value)
    ]
    return parts[0] + (parts[1] + parts[2])


def iota(shape, dim):
    return lax.broadcasted_iota(jnp.int32, shape, dim)


def stack_rows(src_count, leaf):
    return max(8, src_count * (leaf // 128))


def partner(index, shift, count):
    if count & (count - 1) == 0:
        return index ^ shift
    return lax.rem(index - shift + count, count)


def partner_pairs(shift, count):
    if count & (count - 1) == 0:
        return [(place, place ^ shift) for place in range(count)]
    return [(place, (place + shift) % count) for place in range(count)]


def on_grid(value, steps):
    return lax.round(value * steps, lax.RoundingMethod.TO_NEAREST_EVEN) * (1.0 / steps)


def as_bfloat16(value):
    return value.astype(jnp.bfloat16).astype(jnp.float32)


def coordinate_parts(coords):
    parts = []
    for value in coords:
        high = on_grid(value, 128.0)
        rest = value - high
        mid = on_grid(rest, 32768.0)
        parts.append((high, mid, as_bfloat16(rest - mid)))
    return parts


def split_terms(coords, shift):
    parts = coordinate_parts(coords)
    high_sum = sum(high * high for high, mid, low in parts)
    top = as_bfloat16(high_sum)
    rest_sum = sum((mid + low) * (2.0 * high + (mid + low)) for high, mid, low in parts) + shift
    first = as_bfloat16(rest_sum)
    second = as_bfloat16(rest_sum - first)
    return parts, [top, high_sum - top], [first, second, rest_sum - first - second]


def node_side(coords):
    parts, squares, rests = split_terms(coords, 0.0)
    terms = [piece for part in parts for piece in part] + squares + rests
    return dict(enumerate(terms))


def target_side(coords, shift):
    parts, squares, rests = split_terms(coords, shift)
    one = jnp.ones_like(squares[0])
    terms = {}
    for coord, part in enumerate(parts):
        high, mid, low = [-2.0 * piece for piece in part]
        spot = 3 * coord
        terms[spot] = high
        terms[unique_terms + spot] = mid
        terms[2 * unique_terms + spot] = low
        for piece in (1, 2):
            terms[unique_terms + spot + piece] = high
            terms[2 * unique_terms + spot + piece] = mid
            terms[3 * unique_terms + spot + piece] = low
    terms[9] = one
    terms[10] = one
    terms[14] = squares[0]
    terms[15] = squares[1]
    for piece in range(3):
        terms[unique_terms + 11 + piece] = one
    terms[unique_terms + 14] = rests[0]
    terms[unique_terms + 15] = rests[1]
    terms[2 * unique_terms + 14] = rests[2]
    return terms


def store_terms(staged, terms, rows):
    for number, value in terms.items():
        for half in range(staged.shape[0]):
            staged[half, pl.ds(number * rows, rows), :] = value[:, half * 128 : (half + 1) * 128]


def pack_kernel(
    nodes,
    weights,
    values_in,
    targets,
    row_basis,
    column_basis,
    near_in,
    coupling_in,
    packed,
    basis,
    near,
    coupling,
    values,
    points,
    sems,
    *,
    node_rows,
    rank,
):
    pieces = [
        (column_basis.at[0], basis.at[pl.ds(rank, rank), :]),
        (values_in, values),
        (targets, points),
        (row_basis.at[0], basis.at[pl.ds(0, rank), :]),
        (weights, packed.at[pl.ds(3 * node_rows, node_rows), :]),
        (near_in, near),
        (coupling_in, coupling),
    ]
    for coord in range(3):
        pieces.append((nodes.at[coord], packed.at[pl.ds(coord * node_rows, node_rows), :]))
    copies = [
        pltpu.make_async_copy(source, place, sems.at[number])
        for number, (source, place) in enumerate(pieces)
    ]
    for copy in copies:
        copy.start()
    leaf = values.shape[1]
    packed[pl.ds(4 * node_rows, 8), :] = jnp.zeros((8, leaf), jnp.float32)
    basis[pl.ds(2 * rank, 8), :] = jnp.zeros((8, leaf), jnp.float32)
    for copy in copies[:3]:
        copy.wait()
    vector = values[...]
    packed[pl.ds(4 * node_rows, 1), :] = vector
    tall = jnp.broadcast_to(vector, (8, leaf))
    coeffs = lax.dot_general(
        tall,
        basis[pl.ds(rank, rank), :],
        lane_contract,
        precision=highest,
        preferred_element_type=jnp.float32,
    )
    packed[pl.ds(4 * node_rows + 1, 1), pl.ds(0, rank)] = coeffs[0:1]
    basis[pl.ds(2 * rank, 3), :] = points[...]
    basis[pl.ds(2 * rank + 3, 1), :] = vector
    for copy in copies[3:]:
        copy.wait()


def prepare_kernel(near_list, near_count, coupling, kept, spread_flags, group_flags, *, counts):
    src_count, tgt_count, rank = counts
    tgt_index = lax.axis_index("tgt")
    kept[...] = coupling[:, 0, :]
    width = kept.shape[1]

    def one_slot(slot, carry):
        target = near_list[0, slot] - tgt_index * src_count
        source = near_list[1, slot] // src_count
        kept[pl.ds(target * tgt_count + source, 1), :] = jnp.zeros((1, width), jnp.float32)
        return carry

    lax.fori_loop(0, near_count[0], one_slot, 0)
    shape = spread_flags.shape
    row, lane = iota(shape, 0), iota(shape, 1)
    spread_flags[...] = ((row % rank) == (lane % rank)).astype(jnp.bfloat16)
    group_flags[...] = ((row % rank) == (lane // rank)).astype(jnp.bfloat16)


def far_stack(coeffs, kept, spread_flags, group_flags, row_bases, src_count, tgt_count, rank):
    stacked, leaf = row_bases.shape
    halves = leaf // 128
    rows = stack_rows(src_count, leaf)
    tiled = exact_dot(coeffs, spread_flags[pl.ds(0, coeffs.shape[1]), :], plain_contract)
    row_id = iota((rows, rank * rank), 0) // halves
    summed = jnp.zeros((rows, rank * rank), jnp.float32)
    for target in range(src_count):
        block = kept[pl.ds(target * tgt_count, tgt_count), :]
        total = jnp.sum(block * tiled, axis=0, keepdims=True)
        summed = jnp.where(row_id == target, total, summed)
    far = exact_dot(summed, group_flags[...], lane_contract)
    own = (iota((rows, stacked), 1) // rank) == (iota((rows, stacked), 0) // halves)
    far = jnp.where(own, far, 0.0)
    wide = lax.dot_general(
        far, row_bases[...], plain_contract, precision=highest, preferred_element_type=jnp.float32
    )
    return fold_halves([wide[:, half * 128 : (half + 1) * 128] for half in range(halves)])


def fold_halves(pieces):
    half_id = iota(pieces[0].shape, 0) % len(pieces)
    result = pieces[0]
    for half in range(1, len(pieces)):
        result = jnp.where(half_id == half, pieces[half], result)
    return result


def near_stack(partial, src_count, leaf):
    rows = stack_rows(src_count, leaf)
    halves = leaf // 128
    ones = jnp.ones((8, 128), jnp.bfloat16)
    row_id = iota((rows, 128), 0)
    result = jnp.zeros((rows, 128), jnp.float32)
    for target in range(src_count):
        parts = [
            lax.dot_general(ones, part, lane_contract, preferred_element_type=jnp.float32)
            for part in in_three(partial[target])
        ]
        total = (parts[0] + (parts[1] + parts[2]))[0:1]
        for half in range(halves):
            piece = total[:, half * 128 : (half + 1) * 128]
            result = jnp.where(row_id == target * halves + half, piece, result)
    return result


def clear_partials(partial, src_count):
    for target in range(src_count):
        partial[target] = jnp.zeros(partial.shape[1:], jnp.float32)


def add_product(partial, target, start, size, pieces, vectors):
    total = None
    for piece, vector in zip(pieces, vectors):
        total = piece * vector if total is None else total + piece * vector
    here = pl.ds(start, size)
    partial[target, here, :] = partial[target, here, :] + total


def first_kernel(
    near_list,
    near_count,
    kept,
    spread_flags,
    group_flags,
    *refs,
    src_count,
    tgt_count,
    node_rows,
    rank,
    leaf,
):
    columns, refs = refs[:tgt_count], refs[tgt_count:]
    bases, refs = refs[:src_count], refs[src_count:]
    message, tiles, row_bases, row_values = refs[:4]
    held, col_bases, point_rows, point_staged, point_terms = refs[4:9]
    node_staged, node_terms, built, partial, far_values = refs[9:]
    tgt_index = lax.axis_index("tgt")
    src_index = lax.axis_index("src")
    halves = leaf // 128
    stacked = src_count * rank
    rows = stack_rows(src_count, leaf)
    clear_partials(partial, src_count)
    for spot in range(tgt_count):
        there = column_place(tgt_index, spot, tgt_count)
        held[there] = columns[spot][...]
        far_values[pl.ds(there, 1), :] = columns[spot][pl.ds(4 * node_rows + 1, 1), pl.ds(0, 128)]
        built[spot] = 0
    for shift in range(src_count):
        there = partner(src_index, shift, src_count)
        here = pl.ds(pl.multiple_of(there * rank, rank), rank)
        row_bases[here, :] = bases[shift][pl.ds(0, rank), :]
        col_bases[here, :] = bases[shift][pl.ds(rank, rank), :]
        for coord in range(3):
            point_rows[coord, pl.ds(there, 1), :] = bases[shift][pl.ds(2 * rank + coord, 1), :]
        for half in range(halves):
            row_values[pl.ds(there * halves + half, 1), :] = bases[shift][
                pl.ds(2 * rank + 3, 1), pl.ds(half * 128, 128)
            ]
    node_staged[...] = jnp.ones_like(node_staged)
    point_staged[...] = jnp.zeros_like(point_staged)
    coords = [point_rows[coord] for coord in range(3)]
    target_rows = point_rows.shape[1]
    store_terms(point_staged, target_side(coords, spread_sq), target_rows)
    for target in range(src_count):
        for half in range(halves):
            across = point_staged[half, pl.ds(target, term_count, stride=target_rows), :]
            point_terms[target, pl.ds(half * 128, 128), :] = jnp.transpose(across).astype(
                jnp.bfloat16
            )
    block = 128

    def one_slot(slot, carry):
        target = near_list[0, slot] - tgt_index * src_count
        source = near_list[1, slot] // src_count

        @pl.when(built[source] == 0)
        def _():
            built[source] = 1
            coords = [held[source, pl.ds(coord * node_rows, node_rows), :] for coord in range(3)]
            store_terms(node_staged, node_side(coords), node_rows)
            for node in range(node_rows):
                for half in range(halves):
                    across = node_staged[half, pl.ds(node, unique_terms, stride=node_rows), :]
                    node_terms[source, node, :, pl.ds(half * 128, 128)] = across.astype(jnp.bfloat16)

        vectors = [
            held[source, pl.ds(4 * node_rows, 1), pl.ds(half * 128, 128)] for half in range(halves)
        ]
        for start in range(0, leaf, block):
            here = pl.ds(start, block)
            lhs = point_terms[target, here, :]
            tile = None
            for node in range(node_rows):
                rhs = jnp.concatenate([node_terms[source, node]] * term_repeats, axis=0)
                square = lax.dot_general(
                    lhs, rhs, plain_contract, preferred_element_type=jnp.float32
                )
                term = held[source, pl.ds(3 * node_rows + node, 1), :] * lax.rsqrt(square)
                tile = term if tile is None else tile + term
            tiles[slot, here, :] = tile
            pieces = [tile[:, half * 128 : (half + 1) * 128] for half in range(halves)]
            add_product(partial, target, start, block, pieces, vectors)
        return carry

    lax.fori_loop(0, near_count[0], one_slot, 0)
    total = near_stack(partial, src_count, leaf) + far_stack(
        far_values[...], kept, spread_flags, group_flags, row_bases, src_count, tgt_count, rank
    )
    coeffs = fold_halves(
        [
            lax.dot_general(
                total,
                col_bases[:, pl.ds(half * 128, 128)],
                lane_contract,
                precision=highest,
                preferred_element_type=jnp.float32,
            )
            for half in range(halves)
        ]
    )
    own = (iota((rows, stacked), 1) // rank) == (iota((rows, stacked), 0) // halves)
    coeffs = jnp.sum(jnp.where(own, coeffs, 0.0), axis=0, keepdims=True)
    shape = message.shape[1:]
    row_id = iota(shape, 0)
    for target in range(src_count):
        lines = [total[target * halves + half : target * halves + half + 1] for half in range(halves)]
        lines += [coeffs[:, lane : lane + 128] for lane in range(0, stacked, 128)]
        body = jnp.zeros(shape, jnp.float32)
        for number, line in enumerate(lines):
            body = jnp.where(row_id == number, line, body)
        for there in range(tgt_count):
            message[there * src_count + target] = body


def column_place(tgt_index, spot, tgt_count):
    group = 2 if tgt_count % 2 == 0 else 1
    lines = tgt_count // group
    shift, flip = spot % lines, spot // lines
    return partner(tgt_index // group, shift, lines) * group + lax.rem(
        tgt_index % group + flip, group
    )


def second_kernel(
    near_list,
    near_count,
    kept,
    spread_flags,
    group_flags,
    received,
    values,
    row_bases,
    row_values,
    tiles,
    message,
    once_out,
    partial,
    image,
    *,
    src_count,
    tgt_count,
    rank,
    leaf,
):
    tgt_index = lax.axis_index("tgt")
    src_index = lax.axis_index("src")
    halves = leaf // 128
    stacked = src_count * rank
    rows = stack_rows(src_count, leaf)
    lines = received.shape[1]
    clear_partials(partial, src_count)
    for there in range(tgt_count):
        total = received[there * src_count]
        for source in range(1, src_count):
            total = total + received[there * src_count + source]
        image[pl.ds(there * lines, lines), :] = total

    def one_slot(slot, carry):
        target = near_list[0, slot] - tgt_index * src_count
        source = near_list[1, slot] // src_count
        vectors = [image[pl.ds(source * lines + half, 1), :] for half in range(halves)]
        block = 64
        for start in range(0, leaf, block):
            here = pl.ds(start, block)
            pieces = [tiles[slot, here, pl.ds(half * 128, 128)] for half in range(halves)]
            add_product(partial, target, start, block, pieces, vectors)
        return carry

    lax.fori_loop(0, near_count[0], one_slot, 0)
    coeffs = jnp.concatenate(
        [
            image[pl.ds(halves + piece, tgt_count, stride=lines), :]
            for piece in range(stacked // 128)
        ],
        axis=1,
    )
    mine = (iota((tgt_count, stacked), 1) // rank) == src_index
    coeffs = jnp.where(mine, coeffs, 0.0)
    twice = near_stack(partial, src_count, leaf) + far_stack(
        coeffs, kept, spread_flags, group_flags, row_bases, src_count, tgt_count, rank
    )
    once = [image[pl.ds(tgt_index * lines + half, 1), :] for half in range(halves)]
    start = [values[:, pl.ds(half * 128, 128)] for half in range(halves)]
    for half in range(halves):
        once_out[:, pl.ds(half * 128, 128)] = once[half]

    def inner(left, right):
        total = sum(one * other for one, other in zip(left, right))
        return jnp.sum(total, axis=1, keepdims=True)

    cross = jnp.sum(row_values[...] * twice, axis=0, keepdims=True)
    scalars = [inner(start, start), inner(start, once), jnp.sum(cross, axis=1, keepdims=True)]
    shape = (rows, 128)
    row_id, lane_id = iota(shape, 0), iota(shape, 1)
    line = jnp.zeros(shape, jnp.float32)
    for number, value in enumerate(scalars):
        line = jnp.where(lane_id == number, value, line)
    spare = lax.rem(src_index + 1, src_count) * halves
    extra = jnp.where(row_id == spare, line, 0.0)
    for half in range(halves):
        extra = jnp.where(row_id == src_index * halves + half, once[half], extra)
    for there in range(src_count * tgt_count):
        message[there, pl.ds(0, rows), :] = twice
        message[there, pl.ds(rows, rows), :] = extra


def third_kernel(received, values, once_in, result, *, src_count, tgt_count, leaf):
    halves = leaf // 128
    rows = stack_rows(src_count, leaf)
    row_id = iota((rows, 128), 0)
    places = [row_id // halves == source for source in range(src_count)]
    spares = [row_id == ((source + 1) % src_count) * halves for source in range(src_count)]
    s11 = s12 = s22 = scalars = jnp.zeros((rows, 128), jnp.float32)
    for there in range(tgt_count):
        twice = once = None
        for source in range(src_count):
            device = there * src_count + source
            piece = received[device, pl.ds(0, rows), :]
            extra = received[device, pl.ds(rows, rows), :]
            twice = piece if twice is None else twice + piece
            once = extra if once is None else jnp.where(places[source], extra, once)
            scalars = scalars + jnp.where(spares[source], extra, 0.0)
        if rows > src_count * halves:
            once = jnp.where(row_id < src_count * halves, once, 0.0)
        s11 = s11 + once * once
        s12 = s12 + once * twice
        s22 = s22 + twice * twice

    def whole(value):
        return jnp.sum(jnp.sum(value, axis=0, keepdims=True), axis=1, keepdims=True)

    g11, g12, g22 = whole(s11), whole(s12), whole(s22)
    scalars = jnp.sum(scalars, axis=0, keepdims=True)
    g00, g01, g02 = [scalars[:, number : number + 1] for number in range(3)]
    rhs_norm = jnp.sqrt(g00 + norm_floor)
    scale = 1.0 / rhs_norm
    proj_first = scale * scale * (0.5 * g00 + g01)
    left = 0.5 - proj_first
    rest_sq = scale * scale * (left * left * g00 + 2.0 * left * g01 + g11)
    height_first = jnp.sqrt(jnp.maximum(rest_sq, 0.0) + norm_floor)
    c1 = scale / height_first
    c0 = left * c1
    i0 = 0.5 * c0
    i1 = 0.5 * c1 + c0
    i2 = c1
    to_start = i0 * g00 + i1 * g01 + i2 * g02
    to_once = i0 * g01 + i1 * g11 + i2 * g12
    proj_cross = scale * to_start
    proj_second = c0 * to_start + c1 * to_once
    r0 = i0 - proj_cross * scale - proj_second * c0
    r1 = i1 - proj_second * c1
    r2 = i2
    last_sq = (
        r0 * (r0 * g00 + 2.0 * (r1 * g01 + r2 * g02))
        + r1 * (r1 * g11 + 2.0 * r2 * g12)
        + r2 * r2 * g22
    )
    height_second = jnp.sqrt(jnp.maximum(last_sq, 0.0) + norm_floor)
    radius_first = jnp.sqrt(proj_first * proj_first + height_first * height_first)
    cos_first = proj_first / radius_first
    sin_first = height_first / radius_first
    rotated_top = cos_first * proj_cross + sin_first * proj_second
    rotated_low = cos_first * proj_second - sin_first * proj_cross
    radius_second = jnp.sqrt(rotated_low * rotated_low + height_second * height_second)
    coeff_second = -sin_first * rhs_norm * (rotated_low / radius_second) / radius_second
    coeff_first = (cos_first * rhs_norm - rotated_top * coeff_second) / radius_first
    once = once_in[...]
    start = values[...]
    result[...] = (coeff_first * scale + coeff_second * c0) * start + (coeff_second * c1) * once


def per_device(
    right_side,
    targets,
    source_nodes,
    node_weights,
    near_list,
    near_count,
    row_basis,
    column_basis,
    coupling,
):
    src_count = lax.axis_size("src")
    tgt_count = lax.axis_size("tgt")
    leaf = right_side.shape[0]
    node_rows = node_weights.shape[0]
    rank = row_basis.shape[1]
    slots = near_list.shape[1]
    stacked = src_count * rank
    device_count = src_count * tgt_count
    values = right_side.reshape(1, leaf)
    couplings = coupling.reshape(src_count * tgt_count, 1, rank * rank)
    packed_rows = 4 * node_rows + 8

    basis_rows = 2 * rank + 8
    packed, basis, near_list, couplings, values = pl.pallas_call(
        functools.partial(pack_kernel, node_rows=node_rows, rank=rank),
        out_shape=(
            jax.ShapeDtypeStruct((packed_rows, leaf), jnp.float32),
            jax.ShapeDtypeStruct((basis_rows, leaf), jnp.float32),
            jax.ShapeDtypeStruct(near_list.shape, jnp.int32),
            jax.ShapeDtypeStruct(couplings.shape, jnp.float32),
            jax.ShapeDtypeStruct(values.shape, jnp.float32),
        ),
        in_specs=[hbm_space] * 8,
        out_specs=(vmem_space,) * 5,
        scratch_shapes=[
            pltpu.VMEM(targets.shape, jnp.float32),
            pltpu.SemaphoreType.DMA((10,)),
        ],
        compiler_params=kernel_params,
        name="pack",
    )(
        *[
            pltpu.with_memory_space_constraint(value, pltpu.HBM)
            for value in (
                source_nodes,
                node_weights,
                values,
                targets,
                row_basis,
                column_basis,
                near_list,
                couplings,
            )
        ]
    )

    group = 2 if tgt_count % 2 == 0 else 1
    lines = tgt_count // group

    def from_line(value, shift):
        pairs = [
            (line * group + core, there * group + core)
            for line, there in partner_pairs(shift, lines)
            for core in range(group)
        ]
        return lax.ppermute(value, "tgt", pairs)

    def from_flip(value):
        return lax.ppermute(value, "tgt", [(tgt, tgt ^ 1) for tgt in range(tgt_count)])

    def from_source(value, shift):
        return lax.ppermute(value, "src", partner_pairs(shift, src_count))

    columns = [packed] + [from_line(packed, shift) for shift in range(1, lines)]
    if group == 2:
        columns = columns + [from_flip(value) for value in columns]
    bases = [basis] + [from_source(basis, shift) for shift in range(1, src_count)]

    flag_shape = jax.ShapeDtypeStruct((stacked, rank * rank), jnp.bfloat16)
    kept, spread_flags, group_flags = pl.pallas_call(
        functools.partial(prepare_kernel, counts=(src_count, tgt_count, rank)),
        out_shape=(
            jax.ShapeDtypeStruct((device_count, rank * rank), jnp.float32),
            flag_shape,
            flag_shape,
        ),
        in_specs=[smem_space, smem_space, vmem_space],
        out_specs=(vmem_space,) * 3,
        compiler_params=kernel_params,
        name="prepare",
    )(near_list, near_count, couplings)

    sizes = dict(src_count=src_count, tgt_count=tgt_count, rank=rank, leaf=leaf)
    halves = leaf // 128
    stack = stack_rows(src_count, leaf)
    lines_sent = -(-(halves + stacked // 128) // 8) * 8
    target_rows = max(8, src_count)
    message, tiles, row_bases, row_values = pl.pallas_call(
        functools.partial(first_kernel, node_rows=node_rows, **sizes),
        out_shape=(
            jax.ShapeDtypeStruct((device_count, lines_sent, 128), jnp.float32),
            jax.ShapeDtypeStruct((slots, leaf, leaf), jnp.float32),
            jax.ShapeDtypeStruct((stacked, leaf), jnp.float32),
            jax.ShapeDtypeStruct((stack, 128), jnp.float32),
        ),
        in_specs=[smem_space, smem_space] + [vmem_space] * (3 + tgt_count + src_count),
        out_specs=(vmem_space,) * 4,
        scratch_shapes=[
            pltpu.VMEM((tgt_count, packed_rows, leaf), jnp.float32),
            pltpu.VMEM((stacked, leaf), jnp.float32),
            pltpu.VMEM((3, target_rows, leaf), jnp.float32),
            pltpu.VMEM((halves, term_count * target_rows, 128), jnp.float32),
            pltpu.VMEM((src_count, leaf, term_count), jnp.bfloat16),
            pltpu.VMEM((halves, unique_terms * node_rows, 128), jnp.float32),
            pltpu.VMEM((tgt_count, node_rows, unique_terms, leaf), jnp.bfloat16),
            pltpu.SMEM((tgt_count,), jnp.int32),
            pltpu.VMEM((src_count, leaf, 128), jnp.float32),
            pltpu.VMEM((tgt_count, 128), jnp.float32),
        ],
        compiler_params=kernel_params,
        name="first",
    )(near_list, near_count, kept, spread_flags, group_flags, *columns, *bases)

    received = lax.all_to_all(message, both_axes, 0, 0, tiled=True)

    message, once = pl.pallas_call(
        functools.partial(second_kernel, **sizes),
        out_shape=(
            jax.ShapeDtypeStruct((device_count, 2 * stack, 128), jnp.float32),
            jax.ShapeDtypeStruct((1, leaf), jnp.float32),
        ),
        in_specs=[smem_space, smem_space] + [vmem_space] * 8,
        out_specs=(vmem_space, vmem_space),
        scratch_shapes=[
            pltpu.VMEM((src_count, leaf, 128), jnp.float32),
            pltpu.VMEM((tgt_count * lines_sent, 128), jnp.float32),
        ],
        compiler_params=kernel_params,
        name="second",
    )(
        near_list,
        near_count,
        kept,
        spread_flags,
        group_flags,
        received,
        values,
        row_bases,
        row_values,
        tiles,
    )

    received = lax.all_to_all(message, both_axes, 0, 0, tiled=True)

    result = pl.pallas_call(
        functools.partial(third_kernel, src_count=src_count, tgt_count=tgt_count, leaf=leaf),
        out_shape=jax.ShapeDtypeStruct((1, leaf), jnp.float32),
        in_specs=[vmem_space] * 3,
        out_specs=vmem_space,
        compiler_params=kernel_params,
        name="third",
    )(received, values, once)
    return result.reshape(leaf)


def solution(mesh):
    return jax.shard_map(
        per_device,
        mesh=mesh,
        in_specs=(
            P(("tgt", "src")),
            P(None, ("tgt", "src")),
            P(None, None, ("tgt", "src")),
            P(None, ("tgt", "src")),
            P(None, ("tgt", "src")),
            P(("tgt", "src")),
            P(("tgt", "src"), None, None),
            P(("tgt", "src"), None, None),
            P("tgt", None, None, "src", None),
        ),
        out_specs=P(("tgt", "src")),
        check_vma=False,
    )
```

```python
import functools

import jax
import jax.numpy as jnp
from jax import lax
from jax.experimental import pallas as pl
from jax.experimental.pallas import tpu as pltpu
from jax.sharding import PartitionSpec as P

spread_sq = 0.0004
norm_floor = 1e-06
highest = lax.Precision.HIGHEST
both_axes = ("tgt", "src")
lane_contract = (((1,), (1,)), ((), ()))
plain_contract = (((1,), (0,)), ((), ()))
unique_terms = 16
term_repeats = 4
term_count = unique_terms * term_repeats
vmem_space = pl.BlockSpec(memory_space=pltpu.VMEM)
smem_space = pl.BlockSpec(memory_space=pltpu.SMEM)
hbm_space = pl.BlockSpec(memory_space=pltpu.HBM)
kernel_params = pltpu.CompilerParams(vmem_limit_bytes=32 * 1024 * 1024)


def in_three(value):
    top = value.astype(jnp.bfloat16)
    rest = value - top.astype(jnp.float32)
    middle = rest.astype(jnp.bfloat16)
    low = (rest - middle.astype(jnp.float32)).astype(jnp.bfloat16)
    return top, middle, low


def exact_dot(value, flags, contract):
    rows = value.shape[0]
    parts = jnp.concatenate([part.astype(jnp.float32) for part in in_three(value)], axis=0)
    product = lax.dot_general(
        parts.astype(jnp.bfloat16), flags, contract, preferred_element_type=jnp.float32
    )
    return product[0:rows] + (product[rows : 2 * rows] + product[2 * rows :])


def iota(shape, dim):
    return lax.broadcasted_iota(jnp.int32, shape, dim)


def stack_rows(src_count, leaf):
    return max(8, src_count * (leaf // 128))


def partner(index, shift, count):
    if count & (count - 1) == 0:
        return index ^ shift
    return lax.rem(index - shift + count, count)


def partner_pairs(shift, count):
    if count & (count - 1) == 0:
        return [(place, place ^ shift) for place in range(count)]
    return [(place, (place + shift) % count) for place in range(count)]


def on_grid(value, steps):
    return lax.round(value * steps, lax.RoundingMethod.TO_NEAREST_EVEN) * (1.0 / steps)


def as_bfloat16(value):
    return value.astype(jnp.bfloat16).astype(jnp.float32)


def coordinate_parts(coords):
    parts = []
    for value in coords:
        high = on_grid(value, 128.0)
        rest = value - high
        mid = on_grid(rest, 32768.0)
        parts.append((high, mid, as_bfloat16(rest - mid)))
    return parts


def split_terms(coords, shift):
    parts = coordinate_parts(coords)
    high_sum = sum(high * high for high, mid, low in parts)
    top = as_bfloat16(high_sum)
    rest_sum = sum((mid + low) * (2.0 * high + (mid + low)) for high, mid, low in parts) + shift
    first = as_bfloat16(rest_sum)
    second = as_bfloat16(rest_sum - first)
    return parts, [top, high_sum - top], [first, second, rest_sum - first - second]


def node_side(coords):
    parts, squares, rests = split_terms(coords, 0.0)
    terms = [piece for part in parts for piece in part] + squares + rests
    return dict(enumerate(terms))


def target_side(coords, shift):
    parts, squares, rests = split_terms(coords, shift)
    one = jnp.ones_like(squares[0])
    terms = {}
    for coord, part in enumerate(parts):
        high, mid, low = [-2.0 * piece for piece in part]
        spot = 3 * coord
        terms[spot] = high
        terms[unique_terms + spot] = mid
        terms[2 * unique_terms + spot] = low
        for piece in (1, 2):
            terms[unique_terms + spot + piece] = high
            terms[2 * unique_terms + spot + piece] = mid
            terms[3 * unique_terms + spot + piece] = low
    terms[9] = one
    terms[10] = one
    terms[14] = squares[0]
    terms[15] = squares[1]
    for piece in range(3):
        terms[unique_terms + 11 + piece] = one
    terms[unique_terms + 14] = rests[0]
    terms[unique_terms + 15] = rests[1]
    terms[2 * unique_terms + 14] = rests[2]
    return terms


def store_terms(staged, terms, rows, count, fill):
    for number in range(count):
        for half in range(staged.shape[0]):
            here = pl.ds(number * rows, rows)
            if number in terms:
                staged[half, here, :] = terms[number][:, half * 128 : (half + 1) * 128]
            elif fill is not None:
                staged[half, here, :] = jnp.full((rows, 128), fill, jnp.float32)


def pack_kernel(
    nodes,
    weights,
    values_in,
    targets,
    row_basis,
    column_basis,
    near_in,
    coupling_in,
    packed,
    basis,
    near,
    coupling,
    values,
    points,
    sems,
    *,
    node_rows,
    rank,
):
    pieces = [
        (column_basis.at[0], basis.at[pl.ds(rank, rank), :]),
        (values_in, values),
        (targets, points),
        (row_basis.at[0], basis.at[pl.ds(0, rank), :]),
        (weights, packed.at[pl.ds(3 * node_rows, node_rows), :]),
        (near_in, near),
        (coupling_in, coupling),
    ]
    for coord in range(3):
        pieces.append((nodes.at[coord], packed.at[pl.ds(coord * node_rows, node_rows), :]))
    copies = [
        pltpu.make_async_copy(source, place, sems.at[number])
        for number, (source, place) in enumerate(pieces)
    ]
    for copy in copies:
        copy.start()
    leaf = values.shape[1]
    packed[pl.ds(4 * node_rows, 8), :] = jnp.zeros((8, leaf), jnp.float32)
    basis[pl.ds(2 * rank, 8), :] = jnp.zeros((8, leaf), jnp.float32)
    for copy in copies[:3]:
        copy.wait()
    vector = values[...]
    packed[pl.ds(4 * node_rows, 1), :] = vector
    tall = jnp.broadcast_to(vector, (8, leaf))
    coeffs = lax.dot_general(
        tall,
        basis[pl.ds(rank, rank), :],
        lane_contract,
        precision=highest,
        preferred_element_type=jnp.float32,
    )
    packed[pl.ds(4 * node_rows + 1, 1), pl.ds(0, rank)] = coeffs[0:1]
    basis[pl.ds(2 * rank, 3), :] = points[...]
    basis[pl.ds(2 * rank + 3, 1), :] = vector
    for copy in copies[3:]:
        copy.wait()


def prepare_kernel(near_list, near_count, coupling, kept, spread_flags, group_flags, *, counts):
    src_count, tgt_count, rank = counts
    tgt_index = lax.axis_index("tgt")
    kept[...] = coupling[:, 0, :]
    width = kept.shape[1]

    def one_slot(slot, carry):
        target = near_list[0, slot] - tgt_index * src_count
        source = near_list[1, slot] // src_count
        kept[pl.ds(target * tgt_count + source, 1), :] = jnp.zeros((1, width), jnp.float32)
        return carry

    lax.fori_loop(0, near_count[0], one_slot, 0)
    shape = spread_flags.shape
    row, lane = iota(shape, 0), iota(shape, 1)
    spread_flags[...] = ((row % rank) == (lane % rank)).astype(jnp.bfloat16)
    group_flags[...] = ((row % rank) == (lane // rank)).astype(jnp.bfloat16)


def far_stack(coeffs, kept, spread_flags, group_flags, row_bases, src_count, tgt_count, rank):
    stacked, leaf = row_bases.shape
    halves = leaf // 128
    rows = stack_rows(src_count, leaf)
    tiled = exact_dot(coeffs, spread_flags[pl.ds(0, coeffs.shape[1]), :], plain_contract)
    row_id = iota((rows, rank * rank), 0) // halves
    summed = jnp.zeros((rows, rank * rank), jnp.float32)
    for target in range(src_count):
        block = kept[pl.ds(target * tgt_count, tgt_count), :]
        total = jnp.sum(block * tiled, axis=0, keepdims=True)
        summed = jnp.where(row_id == target, total, summed)
    far = exact_dot(summed, group_flags[...], lane_contract)
    own = (iota((rows, stacked), 1) // rank) == (iota((rows, stacked), 0) // halves)
    own = own & (iota((rows, stacked), 0) % halves == 0)
    far = jnp.sum(jnp.where(own, far, 0.0), axis=0, keepdims=True)
    lines = []
    for first in range(0, stacked, 128):
        upright = jnp.transpose(jnp.broadcast_to(far[:, first : first + 128], (128, 128)))
        for half in range(halves):
            block = row_bases[pl.ds(first, 128), pl.ds(half * 128, 128)] * upright
            for start in range(0, 128, rank):
                line = jnp.sum(block[start : start + rank], axis=0, keepdims=True)
                lines.append(((first + start) // rank * halves + half, line))
    return stack_lines(lines, rows)


def stack_lines(lines, rows):
    row_id = iota((rows, 128), 0)
    result = jnp.zeros((rows, 128), jnp.float32)
    for number, line in lines:
        result = jnp.where(row_id == number, line, result)
    return result


def near_stack(partial, src_count, leaf):
    halves = leaf // 128
    lines = []
    for target in range(src_count):
        for half in range(halves):
            flat = jnp.transpose(partial[target, pl.ds(half * 128, 128), :])
            lines.append((target * halves + half, jnp.sum(flat, axis=0, keepdims=True)))
    return stack_lines(lines, stack_rows(src_count, leaf))


def clear_partials(partial, src_count):
    for target in range(src_count):
        partial[target] = jnp.zeros(partial.shape[1:], jnp.float32)


def add_product(partial, target, start, size, pieces, vectors):
    total = None
    for piece, vector in zip(pieces, vectors):
        total = piece * vector if total is None else total + piece * vector
    here = pl.ds(start, size)
    partial[target, here, :] = partial[target, here, :] + total


def first_kernel(
    near_list,
    near_count,
    kept,
    spread_flags,
    group_flags,
    *refs,
    src_count,
    tgt_count,
    node_rows,
    rank,
    leaf,
):
    columns, refs = refs[:tgt_count], refs[tgt_count:]
    bases, refs = refs[:src_count], refs[src_count:]
    message, tiles, row_bases, row_values = refs[:4]
    held, col_bases, point_rows, point_staged, point_terms = refs[4:9]
    node_staged, node_terms, built, partial, far_values = refs[9:]
    tgt_index = lax.axis_index("tgt")
    src_index = lax.axis_index("src")
    halves = leaf // 128
    stacked = src_count * rank
    rows = stack_rows(src_count, leaf)
    clear_partials(partial, src_count)
    for spot in range(tgt_count):
        there = column_place(tgt_index, spot, tgt_count)
        held[there] = columns[spot][...]
        far_values[pl.ds(there, 1), :] = columns[spot][pl.ds(4 * node_rows + 1, 1), pl.ds(0, 128)]
        built[spot] = 0
    for shift in range(src_count):
        there = partner(src_index, shift, src_count)
        here = pl.ds(pl.multiple_of(there * rank, rank), rank)
        row_bases[here, :] = bases[shift][pl.ds(0, rank), :]
        col_bases[here, :] = bases[shift][pl.ds(rank, rank), :]
        for coord in range(3):
            point_rows[coord, pl.ds(there, 1), :] = bases[shift][pl.ds(2 * rank + coord, 1), :]
        for half in range(halves):
            row_values[pl.ds(there * halves + half, 1), :] = bases[shift][
                pl.ds(2 * rank + 3, 1), pl.ds(half * 128, 128)
            ]
    ones_here = pl.ds((unique_terms - 2) * node_rows, 2 * node_rows)
    node_staged[:, ones_here, :] = jnp.ones((halves, 2 * node_rows, 128), jnp.float32)
    coords = [point_rows[coord] for coord in range(3)]
    target_rows = point_rows.shape[1]
    store_terms(point_staged, target_side(coords, spread_sq), target_rows, term_count, 0.0)
    for target in range(src_count):
        for half in range(halves):
            across = point_staged[half, pl.ds(target, term_count, stride=target_rows), :]
            point_terms[target, pl.ds(half * 128, 128), :] = jnp.transpose(across).astype(
                jnp.bfloat16
            )
    block = 128

    def one_slot(slot, carry):
        target = near_list[0, slot] - tgt_index * src_count
        source = near_list[1, slot] // src_count

        @pl.when(built[source] == 0)
        def _():
            built[source] = 1
            coords = [held[source, pl.ds(coord * node_rows, node_rows), :] for coord in range(3)]
            store_terms(node_staged, node_side(coords), node_rows, unique_terms, None)
            for node in range(node_rows):
                for half in range(halves):
                    across = node_staged[half, pl.ds(node, unique_terms, stride=node_rows), :]
                    node_terms[source, node, :, pl.ds(half * 128, 128)] = across.astype(jnp.bfloat16)

        vectors = [
            held[source, pl.ds(4 * node_rows, 1), pl.ds(half * 128, 128)] for half in range(halves)
        ]
        for start in range(0, leaf, block):
            here = pl.ds(start, block)
            lhs = point_terms[target, here, :]
            tile = None
            for node in range(node_rows):
                rhs = jnp.concatenate([node_terms[source, node]] * term_repeats, axis=0)
                square = lax.dot_general(
                    lhs, rhs, plain_contract, preferred_element_type=jnp.float32
                )
                term = held[source, pl.ds(3 * node_rows + node, 1), :] * lax.rsqrt(square)
                tile = term if tile is None else tile + term
            tiles[slot, here, :] = tile
            pieces = [tile[:, half * 128 : (half + 1) * 128] for half in range(halves)]
            add_product(partial, target, start, block, pieces, vectors)
        return carry

    lax.fori_loop(0, near_count[0], one_slot, 0)
    total = near_stack(partial, src_count, leaf) + far_stack(
        far_values[...], kept, spread_flags, group_flags, row_bases, src_count, tgt_count, rank
    )
    coeffs = []
    for first in range(0, stacked, 128):
        blocks = []
        for start in range(first, first + 128, rank):
            target = start // rank
            block = None
            for half in range(halves):
                line = total[target * halves + half : target * halves + half + 1]
                piece = col_bases[pl.ds(start, rank), pl.ds(half * 128, 128)] * line
                block = piece if block is None else block + piece
            blocks.append(block)
        flat = jnp.transpose(jnp.concatenate(blocks, axis=0))
        coeffs.append(jnp.sum(flat, axis=0, keepdims=True))
    for target in range(src_count):
        lines = [total[target * halves + half : target * halves + half + 1] for half in range(halves)]
        for number, line in enumerate(lines + coeffs):
            for there in range(tgt_count):
                message[there * src_count + target, :, pl.ds(number * 128, 128)] = line


def column_place(tgt_index, spot, tgt_count):
    group = 2 if tgt_count % 2 == 0 else 1
    lines = tgt_count // group
    shift, flip = spot % lines, spot // lines
    return partner(tgt_index // group, shift, lines) * group + lax.rem(
        tgt_index % group + flip, group
    )


def second_kernel(
    near_list,
    near_count,
    kept,
    spread_flags,
    group_flags,
    received,
    values,
    row_bases,
    row_values,
    tiles,
    message,
    once_out,
    partial,
    image,
    *,
    src_count,
    tgt_count,
    rank,
    leaf,
):
    tgt_index = lax.axis_index("tgt")
    src_index = lax.axis_index("src")
    halves = leaf // 128
    stacked = src_count * rank
    rows = stack_rows(src_count, leaf)
    lines = image.shape[0] // tgt_count
    clear_partials(partial, src_count)
    for there in range(tgt_count):
        for number in range(halves + stacked // 128):
            lanes = pl.ds(number * 128, 128)
            total = received[there * src_count, :, lanes]
            for source in range(1, src_count):
                total = total + received[there * src_count + source, :, lanes]
            image[pl.ds(there * lines + number, 1), :] = total

    def one_slot(slot, carry):
        target = near_list[0, slot] - tgt_index * src_count
        source = near_list[1, slot] // src_count
        vectors = [image[pl.ds(source * lines + half, 1), :] for half in range(halves)]
        block = 64
        for start in range(0, leaf, block):
            here = pl.ds(start, block)
            pieces = [tiles[slot, here, pl.ds(half * 128, 128)] for half in range(halves)]
            add_product(partial, target, start, block, pieces, vectors)
        return carry

    lax.fori_loop(0, near_count[0], one_slot, 0)
    coeffs = jnp.concatenate(
        [
            image[pl.ds(halves + piece, tgt_count, stride=lines), :]
            for piece in range(stacked // 128)
        ],
        axis=1,
    )
    mine = (iota((tgt_count, stacked), 1) // rank) == src_index
    coeffs = jnp.where(mine, coeffs, 0.0)
    twice = near_stack(partial, src_count, leaf) + far_stack(
        coeffs, kept, spread_flags, group_flags, row_bases, src_count, tgt_count, rank
    )
    once = [image[pl.ds(tgt_index * lines + half, 1), :] for half in range(halves)]
    start = [values[:, pl.ds(half * 128, 128)] for half in range(halves)]
    for half in range(halves):
        once_out[:, pl.ds(half * 128, 128)] = once[half]

    def inner(left, right):
        total = sum(one * other for one, other in zip(left, right))
        return jnp.sum(total, axis=1, keepdims=True)

    cross = jnp.sum(row_values[...] * twice, axis=0, keepdims=True)
    scalars = [inner(start, start), inner(start, once), jnp.sum(cross, axis=1, keepdims=True)]
    lane_id = iota((1, 128), 1)
    line = jnp.zeros((1, 128), jnp.float32)
    for number, value in enumerate(scalars):
        line = jnp.where(lane_id == number, value, line)
    piece_rows = message.shape[2]
    share = piece_rows // halves
    row_id = iota((piece_rows, 128), 0)
    spare = lax.rem(src_index + 1, share) * halves
    extra = jnp.where(row_id == spare, line, 0.0)
    for half in range(halves):
        extra = jnp.where(row_id == lax.rem(src_index, share) * halves + half, once[half], extra)
    pieces = [twice[first : first + piece_rows] for first in range(0, rows, piece_rows)]
    for there in range(src_count * tgt_count):
        for number, piece in enumerate(pieces + [extra]):
            message[there, number] = piece


def third_kernel(received, values, once_in, result, *, src_count, tgt_count, leaf):
    halves = leaf // 128
    piece_rows = received.shape[2]
    share = piece_rows // halves
    row_id = iota((piece_rows, 128), 0)
    s11 = s12 = s22 = scalars = jnp.zeros((piece_rows, 128), jnp.float32)
    for there in range(tgt_count):
        for piece in range(src_count // share):
            twice = once = None
            for source in range(src_count):
                part = received[there * src_count + source, piece]
                twice = part if twice is None else twice + part
            for spot in range(share):
                extra = received[there * src_count + piece * share + spot, received.shape[1] - 1]
                mine = row_id // halves == spot
                once = extra if once is None else jnp.where(mine, extra, once)
                spare = row_id == ((spot + 1) % share) * halves
                scalars = scalars + jnp.where(spare, extra, 0.0)
            s11 = s11 + once * once
            s12 = s12 + once * twice
            s22 = s22 + twice * twice

    def whole(value):
        return jnp.sum(jnp.sum(value, axis=0, keepdims=True), axis=1, keepdims=True)

    g11, g12, g22 = whole(s11), whole(s12), whole(s22)
    scalars = jnp.sum(scalars, axis=0, keepdims=True)
    g00, g01, g02 = [scalars[:, number : number + 1] for number in range(3)]
    rhs_norm = jnp.sqrt(g00 + norm_floor)
    scale = 1.0 / rhs_norm
    proj_first = scale * scale * (0.5 * g00 + g01)
    left = 0.5 - proj_first
    rest_sq = scale * scale * (left * left * g00 + 2.0 * left * g01 + g11)
    height_first = jnp.sqrt(jnp.maximum(rest_sq, 0.0) + norm_floor)
    c1 = scale / height_first
    c0 = left * c1
    i0 = 0.5 * c0
    i1 = 0.5 * c1 + c0
    i2 = c1
    to_start = i0 * g00 + i1 * g01 + i2 * g02
    to_once = i0 * g01 + i1 * g11 + i2 * g12
    proj_cross = scale * to_start
    proj_second = c0 * to_start + c1 * to_once
    r0 = i0 - proj_cross * scale - proj_second * c0
    r1 = i1 - proj_second * c1
    r2 = i2
    last_sq = (
        r0 * (r0 * g00 + 2.0 * (r1 * g01 + r2 * g02))
        + r1 * (r1 * g11 + 2.0 * r2 * g12)
        + r2 * r2 * g22
    )
    height_second = jnp.sqrt(jnp.maximum(last_sq, 0.0) + norm_floor)
    radius_first = jnp.sqrt(proj_first * proj_first + height_first * height_first)
    cos_first = proj_first / radius_first
    sin_first = height_first / radius_first
    rotated_top = cos_first * proj_cross + sin_first * proj_second
    rotated_low = cos_first * proj_second - sin_first * proj_cross
    radius_second = jnp.sqrt(rotated_low * rotated_low + height_second * height_second)
    coeff_second = -sin_first * rhs_norm * (rotated_low / radius_second) / radius_second
    coeff_first = (cos_first * rhs_norm - rotated_top * coeff_second) / radius_first
    once = once_in[...]
    start = values[...]
    result[...] = (coeff_first * scale + coeff_second * c0) * start + (coeff_second * c1) * once


def per_device(
    right_side,
    targets,
    source_nodes,
    node_weights,
    near_list,
    near_count,
    row_basis,
    column_basis,
    coupling,
):
    src_count = lax.axis_size("src")
    tgt_count = lax.axis_size("tgt")
    leaf = right_side.shape[0]
    node_rows = node_weights.shape[0]
    rank = row_basis.shape[1]
    slots = near_list.shape[1]
    stacked = src_count * rank
    device_count = src_count * tgt_count
    values = right_side.reshape(1, leaf)
    couplings = coupling.reshape(src_count * tgt_count, 1, rank * rank)
    packed_rows = 4 * node_rows + 8

    basis_rows = 2 * rank + 8
    packed, basis, near_list, couplings, values = pl.pallas_call(
        functools.partial(pack_kernel, node_rows=node_rows, rank=rank),
        out_shape=(
            jax.ShapeDtypeStruct((packed_rows, leaf), jnp.float32),
            jax.ShapeDtypeStruct((basis_rows, leaf), jnp.float32),
            jax.ShapeDtypeStruct(near_list.shape, jnp.int32),
            jax.ShapeDtypeStruct(couplings.shape, jnp.float32),
            jax.ShapeDtypeStruct(values.shape, jnp.float32),
        ),
        in_specs=[hbm_space] * 8,
        out_specs=(vmem_space,) * 5,
        scratch_shapes=[
            pltpu.VMEM(targets.shape, jnp.float32),
            pltpu.SemaphoreType.DMA((10,)),
        ],
        compiler_params=kernel_params,
        name="pack",
    )(
        *[
            pltpu.with_memory_space_constraint(value, pltpu.HBM)
            for value in (
                source_nodes,
                node_weights,
                values,
                targets,
                row_basis,
                column_basis,
                near_list,
                couplings,
            )
        ]
    )

    group = 2 if tgt_count % 2 == 0 else 1
    lines = tgt_count // group

    def from_line(value, shift):
        pairs = [
            (line * group + core, there * group + core)
            for line, there in partner_pairs(shift, lines)
            for core in range(group)
        ]
        return lax.ppermute(value, "tgt", pairs)

    def from_flip(value):
        return lax.ppermute(value, "tgt", [(tgt, tgt ^ 1) for tgt in range(tgt_count)])

    def from_source(value, shift):
        return lax.ppermute(value, "src", partner_pairs(shift, src_count))

    columns = [packed] + [from_line(packed, shift) for shift in range(1, lines)]
    if group == 2:
        columns = columns + [from_flip(value) for value in columns]
    bases = [basis] + [from_source(basis, shift) for shift in range(1, src_count)]

    flag_shape = jax.ShapeDtypeStruct((stacked, rank * rank), jnp.bfloat16)
    kept, spread_flags, group_flags = pl.pallas_call(
        functools.partial(prepare_kernel, counts=(src_count, tgt_count, rank)),
        out_shape=(
            jax.ShapeDtypeStruct((device_count, rank * rank), jnp.float32),
            flag_shape,
            flag_shape,
        ),
        in_specs=[smem_space, smem_space, vmem_space],
        out_specs=(vmem_space,) * 3,
        compiler_params=kernel_params,
        name="prepare",
    )(near_list, near_count, couplings)

    sizes = dict(src_count=src_count, tgt_count=tgt_count, rank=rank, leaf=leaf)
    halves = leaf // 128
    stack = stack_rows(src_count, leaf)
    lines_held = -(-(halves + stacked // 128) // 8) * 8
    piece_rows = 2 * halves
    target_rows = max(8, src_count)
    message, tiles, row_bases, row_values = pl.pallas_call(
        functools.partial(first_kernel, node_rows=node_rows, **sizes),
        out_shape=(
            jax.ShapeDtypeStruct((device_count, 1, leaf + stacked), jnp.float32),
            jax.ShapeDtypeStruct((slots, leaf, leaf), jnp.float32),
            jax.ShapeDtypeStruct((stacked, leaf), jnp.float32),
            jax.ShapeDtypeStruct((stack, 128), jnp.float32),
        ),
        in_specs=[smem_space, smem_space] + [vmem_space] * (3 + tgt_count + src_count),
        out_specs=(vmem_space,) * 4,
        scratch_shapes=[
            pltpu.VMEM((tgt_count, packed_rows, leaf), jnp.float32),
            pltpu.VMEM((stacked, leaf), jnp.float32),
            pltpu.VMEM((3, target_rows, leaf), jnp.float32),
            pltpu.VMEM((halves, term_count * target_rows, 128), jnp.float32),
            pltpu.VMEM((src_count, leaf, term_count), jnp.bfloat16),
            pltpu.VMEM((halves, unique_terms * node_rows, 128), jnp.float32),
            pltpu.VMEM((tgt_count, node_rows, unique_terms, leaf), jnp.bfloat16),
            pltpu.SMEM((tgt_count,), jnp.int32),
            pltpu.VMEM((src_count, leaf, 128), jnp.float32),
            pltpu.VMEM((tgt_count, 128), jnp.float32),
        ],
        compiler_params=kernel_params,
        name="first",
    )(near_list, near_count, kept, spread_flags, group_flags, *columns, *bases)

    received = lax.all_to_all(message, both_axes, 0, 0, tiled=True)

    message, once = pl.pallas_call(
        functools.partial(second_kernel, **sizes),
        out_shape=(
            jax.ShapeDtypeStruct(
                (device_count, stack // piece_rows + 1, piece_rows, 128), jnp.float32
            ),
            jax.ShapeDtypeStruct((1, leaf), jnp.float32),
        ),
        in_specs=[smem_space, smem_space] + [vmem_space] * 8,
        out_specs=(vmem_space, vmem_space),
        scratch_shapes=[
            pltpu.VMEM((src_count, leaf, 128), jnp.float32),
            pltpu.VMEM((tgt_count * lines_held, 128), jnp.float32),
        ],
        compiler_params=kernel_params,
        name="second",
    )(
        near_list,
        near_count,
        kept,
        spread_flags,
        group_flags,
        received,
        values,
        row_bases,
        row_values,
        tiles,
    )

    received = lax.all_to_all(message, both_axes, 0, 0, tiled=True)

    result = pl.pallas_call(
        functools.partial(third_kernel, src_count=src_count, tgt_count=tgt_count, leaf=leaf),
        out_shape=jax.ShapeDtypeStruct((1, leaf), jnp.float32),
        in_specs=[vmem_space] * 3,
        out_specs=vmem_space,
        compiler_params=kernel_params,
        name="third",
    )(received, values, once)
    return result.reshape(leaf)


def solution(mesh):
    return jax.shard_map(
        per_device,
        mesh=mesh,
        in_specs=(
            P(("tgt", "src")),
            P(None, ("tgt", "src")),
            P(None, None, ("tgt", "src")),
            P(None, ("tgt", "src")),
            P(None, ("tgt", "src")),
            P(("tgt", "src")),
            P(("tgt", "src"), None, None),
            P(("tgt", "src"), None, None),
            P("tgt", None, None, "src", None),
        ),
        out_specs=P(("tgt", "src")),
        check_vma=False,
    )
```

```python
import functools

import jax
import jax.numpy as jnp
from jax import lax
from jax.experimental import pallas as pl
from jax.experimental.pallas import tpu as pltpu
from jax.sharding import PartitionSpec as P

spread_sq = 0.0004
norm_floor = 1e-06
highest = lax.Precision.HIGHEST
both_axes = ("tgt", "src")
lane_contract = (((1,), (1,)), ((), ()))
plain_contract = (((1,), (0,)), ((), ()))
unique_terms = 16
term_repeats = 4
term_count = unique_terms * term_repeats
vmem_space = pl.BlockSpec(memory_space=pltpu.VMEM)
smem_space = pl.BlockSpec(memory_space=pltpu.SMEM)
hbm_space = pl.BlockSpec(memory_space=pltpu.HBM)
kernel_params = pltpu.CompilerParams(vmem_limit_bytes=32 * 1024 * 1024)


def in_three(value):
    top = value.astype(jnp.bfloat16)
    rest = value - top.astype(jnp.float32)
    middle = rest.astype(jnp.bfloat16)
    low = (rest - middle.astype(jnp.float32)).astype(jnp.bfloat16)
    return top, middle, low


def exact_dot(value, flags, contract):
    rows = value.shape[0]
    parts = jnp.concatenate([part.astype(jnp.float32) for part in in_three(value)], axis=0)
    product = lax.dot_general(
        parts.astype(jnp.bfloat16), flags, contract, preferred_element_type=jnp.float32
    )
    return product[0:rows] + (product[rows : 2 * rows] + product[2 * rows :])


def iota(shape, dim):
    return lax.broadcasted_iota(jnp.int32, shape, dim)


def stack_rows(src_count, leaf):
    return max(8, src_count * (leaf // 128))


def partner(index, shift, count):
    if count & (count - 1) == 0:
        return index ^ shift
    return lax.rem(index - shift + count, count)


def partner_pairs(shift, count):
    if count & (count - 1) == 0:
        return [(place, place ^ shift) for place in range(count)]
    return [(place, (place + shift) % count) for place in range(count)]


def on_grid(value, steps):
    return lax.round(value * steps, lax.RoundingMethod.TO_NEAREST_EVEN) * (1.0 / steps)


def as_bfloat16(value):
    return value.astype(jnp.bfloat16).astype(jnp.float32)


def coordinate_parts(coords):
    parts = []
    for value in coords:
        high = on_grid(value, 128.0)
        rest = value - high
        mid = on_grid(rest, 32768.0)
        parts.append((high, mid, as_bfloat16(rest - mid)))
    return parts


def split_terms(coords, shift):
    parts = coordinate_parts(coords)
    high_sum = sum(high * high for high, mid, low in parts)
    top = as_bfloat16(high_sum)
    rest_sum = sum((mid + low) * (2.0 * high + (mid + low)) for high, mid, low in parts) + shift
    first = as_bfloat16(rest_sum)
    second = as_bfloat16(rest_sum - first)
    return parts, [top, high_sum - top], [first, second, rest_sum - first - second]


def node_side(coords):
    parts, squares, rests = split_terms(coords, 0.0)
    terms = [piece for part in parts for piece in part] + squares + rests
    return dict(enumerate(terms))


def target_side(coords, shift):
    parts, squares, rests = split_terms(coords, shift)
    one = jnp.ones_like(squares[0])
    terms = {}
    for coord, part in enumerate(parts):
        high, mid, low = [-2.0 * piece for piece in part]
        spot = 3 * coord
        terms[spot] = high
        terms[unique_terms + spot] = mid
        terms[2 * unique_terms + spot] = low
        for piece in (1, 2):
            terms[unique_terms + spot + piece] = high
            terms[2 * unique_terms + spot + piece] = mid
            terms[3 * unique_terms + spot + piece] = low
    terms[9] = one
    terms[10] = one
    terms[14] = squares[0]
    terms[15] = squares[1]
    for piece in range(3):
        terms[unique_terms + 11 + piece] = one
    terms[unique_terms + 14] = rests[0]
    terms[unique_terms + 15] = rests[1]
    terms[2 * unique_terms + 14] = rests[2]
    return terms


def store_terms(staged, terms, rows, count, fill):
    for number in range(count):
        for half in range(staged.shape[0]):
            here = pl.ds(number * rows, rows)
            if number in terms:
                staged[half, here, :] = terms[number][:, half * 128 : (half + 1) * 128]
            elif fill is not None:
                staged[half, here, :] = jnp.full((rows, 128), fill, jnp.float32)


def pack_kernel(
    nodes,
    weights,
    values_in,
    targets,
    row_basis,
    column_basis,
    near_in,
    coupling_in,
    packed,
    basis,
    near,
    flat,
    spread_flags,
    group_flags,
    values,
    points,
    coupling,
    sems,
    *,
    node_rows,
    rank,
):
    pieces = [
        (column_basis.at[0], basis.at[pl.ds(rank, rank), :]),
        (values_in, values),
        (targets, points),
        (near_in, near),
        (row_basis.at[0], basis.at[pl.ds(0, rank), :]),
        (weights, packed.at[pl.ds(3 * node_rows, node_rows), :]),
        (coupling_in, coupling),
    ]
    for coord in range(3):
        pieces.append((nodes.at[coord], packed.at[pl.ds(coord * node_rows, node_rows), :]))
    copies = [
        pltpu.make_async_copy(source, place, sems.at[number])
        for number, (source, place) in enumerate(pieces)
    ]
    for copy in copies:
        copy.start()
    leaf = values.shape[1]
    packed[pl.ds(4 * node_rows, 8), :] = jnp.zeros((8, leaf), jnp.float32)
    basis[pl.ds(2 * rank, 8), :] = jnp.zeros((8, leaf), jnp.float32)
    shape = spread_flags.shape
    row, lane = iota(shape, 0), iota(shape, 1)
    spread_flags[...] = ((row % rank) == (lane % rank)).astype(jnp.bfloat16)
    group_flags[...] = ((row % rank) == (lane // rank)).astype(jnp.bfloat16)
    for copy in copies[:3]:
        copy.wait()
    vector = values[...]
    packed[pl.ds(4 * node_rows, 1), :] = vector
    tall = jnp.broadcast_to(vector, (8, leaf))
    coeffs = lax.dot_general(
        tall,
        basis[pl.ds(rank, rank), :],
        lane_contract,
        precision=highest,
        preferred_element_type=jnp.float32,
    )
    packed[pl.ds(4 * node_rows + 1, 1), pl.ds(0, rank)] = coeffs[0:1]
    basis[pl.ds(2 * rank, 3), :] = points[...]
    basis[pl.ds(2 * rank + 3, 1), :] = vector
    for copy in copies[3:]:
        copy.wait()
    flat[...] = coupling[:, 0, :]


def far_stack(coeffs, kept, spread_flags, group_flags, row_bases, src_count, tgt_count, rank):
    stacked, leaf = row_bases.shape
    halves = leaf // 128
    rows = stack_rows(src_count, leaf)
    tiled = exact_dot(coeffs, spread_flags[pl.ds(0, coeffs.shape[1]), :], plain_contract)
    row_id = iota((rows, rank * rank), 0) // halves
    summed = jnp.zeros((rows, rank * rank), jnp.float32)
    for target in range(src_count):
        block = kept[pl.ds(target * tgt_count, tgt_count), :]
        total = jnp.sum(block * tiled, axis=0, keepdims=True)
        summed = jnp.where(row_id == target, total, summed)
    far = exact_dot(summed, group_flags[...], lane_contract)
    own = (iota((rows, stacked), 1) // rank) == (iota((rows, stacked), 0) // halves)
    own = own & (iota((rows, stacked), 0) % halves == 0)
    far = jnp.sum(jnp.where(own, far, 0.0), axis=0, keepdims=True)
    lines = []
    for first in range(0, stacked, 128):
        upright = jnp.transpose(jnp.broadcast_to(far[:, first : first + 128], (128, 128)))
        for half in range(halves):
            block = row_bases[pl.ds(first, 128), pl.ds(half * 128, 128)] * upright
            for start in range(0, 128, rank):
                line = jnp.sum(block[start : start + rank], axis=0, keepdims=True)
                lines.append(((first + start) // rank * halves + half, line))
    return stack_lines(lines, rows)


def stack_lines(lines, rows):
    row_id = iota((rows, 128), 0)
    result = jnp.zeros((rows, 128), jnp.float32)
    for number, line in lines:
        result = jnp.where(row_id == number, line, result)
    return result


def near_stack(partial, src_count, leaf):
    halves = leaf // 128
    lines = []
    for target in range(src_count):
        for half in range(halves):
            flat = jnp.transpose(partial[target, pl.ds(half * 128, 128), :])
            lines.append((target * halves + half, jnp.sum(flat, axis=0, keepdims=True)))
    return stack_lines(lines, stack_rows(src_count, leaf))


def clear_partials(partial, src_count):
    for target in range(src_count):
        partial[target] = jnp.zeros(partial.shape[1:], jnp.float32)


def add_product(partial, target, start, size, pieces, vectors):
    total = None
    for piece, vector in zip(pieces, vectors):
        total = piece * vector if total is None else total + piece * vector
    here = pl.ds(start, size)
    partial[target, here, :] = partial[target, here, :] + total


def first_kernel(
    near,
    near_count,
    flat,
    spread_flags,
    group_flags,
    *refs,
    src_count,
    tgt_count,
    node_rows,
    rank,
    leaf,
):
    columns, refs = refs[:tgt_count], refs[tgt_count:]
    bases, refs = refs[:src_count], refs[src_count:]
    message, tiles, row_bases, row_values, kept = refs[:5]
    held, col_bases, point_rows, point_staged, point_terms = refs[5:10]
    node_staged, node_terms, built, partial, far_values = refs[10:]
    tgt_index = lax.axis_index("tgt")
    src_index = lax.axis_index("src")
    halves = leaf // 128
    stacked = src_count * rank
    rows = stack_rows(src_count, leaf)
    clear_partials(partial, src_count)
    kept[...] = flat[...]
    for spot in range(tgt_count):
        there = column_place(tgt_index, spot, tgt_count)
        held[there] = columns[spot][...]
        far_values[pl.ds(there, 1), :] = columns[spot][pl.ds(4 * node_rows + 1, 1), pl.ds(0, 128)]
        built[spot] = 0
    for shift in range(src_count):
        there = partner(src_index, shift, src_count)
        here = pl.ds(pl.multiple_of(there * rank, rank), rank)
        row_bases[here, :] = bases[shift][pl.ds(0, rank), :]
        col_bases[here, :] = bases[shift][pl.ds(rank, rank), :]
        for coord in range(3):
            point_rows[coord, pl.ds(there, 1), :] = bases[shift][pl.ds(2 * rank + coord, 1), :]
        for half in range(halves):
            row_values[pl.ds(there * halves + half, 1), :] = bases[shift][
                pl.ds(2 * rank + 3, 1), pl.ds(half * 128, 128)
            ]
    ones_here = pl.ds((unique_terms - 2) * node_rows, 2 * node_rows)
    node_staged[:, ones_here, :] = jnp.ones((halves, 2 * node_rows, 128), jnp.float32)
    coords = [point_rows[coord] for coord in range(3)]
    target_rows = point_rows.shape[1]
    store_terms(point_staged, target_side(coords, spread_sq), target_rows, term_count, 0.0)
    for target in range(src_count):
        for half in range(halves):
            across = point_staged[half, pl.ds(target, term_count, stride=target_rows), :]
            point_terms[target, pl.ds(half * 128, 128), :] = jnp.transpose(across).astype(
                jnp.bfloat16
            )
    block = 128

    live = near_count[0]
    slots = tiles.shape[0]
    together = 2 if slots % 2 == 0 else 1

    def some_slots(number, carry):
        numbers = [number * together + offset for offset in range(together)]
        places = []
        for slot in numbers:
            target, source = near[0, slot] - tgt_index * src_count, near[1, slot] // src_count
            places.append((slot, target, source))

            @pl.when(slot < live)
            def _():
                row = pl.ds(target * tgt_count + source, 1)
                kept[row, :] = jnp.zeros((1, kept.shape[1]), jnp.float32)

            @pl.when(built[source] == 0)
            def _():
                built[source] = 1
                coords = [held[source, pl.ds(coord * node_rows, node_rows), :] for coord in range(3)]
                store_terms(node_staged, node_side(coords), node_rows, unique_terms, None)
                for node in range(node_rows):
                    for half in range(halves):
                        across = node_staged[half, pl.ds(node, unique_terms, stride=node_rows), :]
                        lanes = pl.ds(half * 128, 128)
                        node_terms[source, node, :, lanes] = across.astype(jnp.bfloat16)

        for slot, target, source in places:
            weight = (slot < live).astype(jnp.float32)
            vectors = [
                weight * held[source, pl.ds(4 * node_rows, 1), pl.ds(half * 128, 128)]
                for half in range(halves)
            ]
            for start in range(0, leaf, block):
                here = pl.ds(start, block)
                lhs = point_terms[target, here, :]
                tile = None
                for node in range(node_rows):
                    rhs = jnp.concatenate([node_terms[source, node]] * term_repeats, axis=0)
                    square = lax.dot_general(
                        lhs, rhs, plain_contract, preferred_element_type=jnp.float32
                    )
                    term = held[source, pl.ds(3 * node_rows + node, 1), :] * lax.rsqrt(square)
                    tile = term if tile is None else tile + term
                tiles[slot, here, :] = tile
                pieces = [tile[:, half * 128 : (half + 1) * 128] for half in range(halves)]
                add_product(partial, target, start, block, pieces, vectors)
        return carry

    lax.fori_loop(0, (live + together - 1) // together, some_slots, 0)
    total = near_stack(partial, src_count, leaf) + far_stack(
        far_values[...], kept, spread_flags, group_flags, row_bases, src_count, tgt_count, rank
    )
    coeffs = []
    for first in range(0, stacked, 128):
        blocks = []
        for start in range(first, first + 128, rank):
            target = start // rank
            block = None
            for half in range(halves):
                line = total[target * halves + half : target * halves + half + 1]
                piece = col_bases[pl.ds(start, rank), pl.ds(half * 128, 128)] * line
                block = piece if block is None else block + piece
            blocks.append(block)
        flat = jnp.transpose(jnp.concatenate(blocks, axis=0))
        coeffs.append(jnp.sum(flat, axis=0, keepdims=True))
    for target in range(src_count):
        lines = [total[target * halves + half : target * halves + half + 1] for half in range(halves)]
        for number, line in enumerate(lines + coeffs):
            for there in range(tgt_count):
                message[there * src_count + target, :, pl.ds(number * 128, 128)] = line


def column_place(tgt_index, spot, tgt_count):
    group = 2 if tgt_count % 2 == 0 else 1
    lines = tgt_count // group
    shift, flip = spot % lines, spot // lines
    return partner(tgt_index // group, shift, lines) * group + lax.rem(
        tgt_index % group + flip, group
    )


def second_kernel(
    near,
    near_count,
    kept,
    spread_flags,
    group_flags,
    received,
    values,
    row_bases,
    row_values,
    tiles,
    message,
    once_out,
    partial,
    image,
    *,
    src_count,
    tgt_count,
    rank,
    leaf,
):
    tgt_index = lax.axis_index("tgt")
    src_index = lax.axis_index("src")
    halves = leaf // 128
    stacked = src_count * rank
    rows = stack_rows(src_count, leaf)
    lines = image.shape[0] // tgt_count
    clear_partials(partial, src_count)
    for there in range(tgt_count):
        for number in range(halves + stacked // 128):
            lanes = pl.ds(number * 128, 128)
            total = received[there * src_count, :, lanes]
            for source in range(1, src_count):
                total = total + received[there * src_count + source, :, lanes]
            image[pl.ds(there * lines + number, 1), :] = total

    def one_slot(slot, carry):
        target, source = near[0, slot] - tgt_index * src_count, near[1, slot] // src_count
        vectors = [image[pl.ds(source * lines + half, 1), :] for half in range(halves)]
        block = 64
        for start in range(0, leaf, block):
            here = pl.ds(start, block)
            pieces = [tiles[slot, here, pl.ds(half * 128, 128)] for half in range(halves)]
            add_product(partial, target, start, block, pieces, vectors)
        return carry

    lax.fori_loop(0, near_count[0], one_slot, 0)
    coeffs = jnp.concatenate(
        [
            image[pl.ds(halves + piece, tgt_count, stride=lines), :]
            for piece in range(stacked // 128)
        ],
        axis=1,
    )
    mine = (iota((tgt_count, stacked), 1) // rank) == src_index
    coeffs = jnp.where(mine, coeffs, 0.0)
    twice = near_stack(partial, src_count, leaf) + far_stack(
        coeffs, kept, spread_flags, group_flags, row_bases, src_count, tgt_count, rank
    )
    once = [image[pl.ds(tgt_index * lines + half, 1), :] for half in range(halves)]
    start = [values[:, pl.ds(half * 128, 128)] for half in range(halves)]
    for half in range(halves):
        once_out[:, pl.ds(half * 128, 128)] = once[half]

    def inner(left, right):
        total = sum(one * other for one, other in zip(left, right))
        return jnp.sum(total, axis=1, keepdims=True)

    cross = jnp.sum(row_values[...] * twice, axis=0, keepdims=True)
    scalars = [inner(start, start), inner(start, once), jnp.sum(cross, axis=1, keepdims=True)]
    lane_id = iota((1, 128), 1)
    line = jnp.zeros((1, 128), jnp.float32)
    for number, value in enumerate(scalars):
        line = jnp.where(lane_id == number, value, line)
    piece_rows = message.shape[2]
    share = piece_rows // halves
    row_id = iota((piece_rows, 128), 0)
    spare = lax.rem(src_index + 1, share) * halves
    extra = jnp.where(row_id == spare, line, 0.0)
    for half in range(halves):
        extra = jnp.where(row_id == lax.rem(src_index, share) * halves + half, once[half], extra)
    pieces = [twice[first : first + piece_rows] for first in range(0, rows, piece_rows)]
    for there in range(src_count * tgt_count):
        for number, piece in enumerate(pieces + [extra]):
            message[there, number] = piece


def third_kernel(received, values, once_in, result, *, src_count, tgt_count, leaf):
    halves = leaf // 128
    piece_rows = received.shape[2]
    share = piece_rows // halves
    row_id = iota((piece_rows, 128), 0)
    s11 = s12 = s22 = scalars = jnp.zeros((piece_rows, 128), jnp.float32)
    for there in range(tgt_count):
        for piece in range(src_count // share):
            twice = once = None
            for source in range(src_count):
                part = received[there * src_count + source, piece]
                twice = part if twice is None else twice + part
            for spot in range(share):
                extra = received[there * src_count + piece * share + spot, received.shape[1] - 1]
                mine = row_id // halves == spot
                once = extra if once is None else jnp.where(mine, extra, once)
                spare = row_id == ((spot + 1) % share) * halves
                scalars = scalars + jnp.where(spare, extra, 0.0)
            s11 = s11 + once * once
            s12 = s12 + once * twice
            s22 = s22 + twice * twice

    def whole(value):
        return jnp.sum(jnp.sum(value, axis=0, keepdims=True), axis=1, keepdims=True)

    g11, g12, g22 = whole(s11), whole(s12), whole(s22)
    scalars = jnp.sum(scalars, axis=0, keepdims=True)
    g00, g01, g02 = [scalars[:, number : number + 1] for number in range(3)]
    rhs_norm = jnp.sqrt(g00 + norm_floor)
    scale = 1.0 / rhs_norm
    proj_first = scale * scale * (0.5 * g00 + g01)
    left = 0.5 - proj_first
    rest_sq = scale * scale * (left * left * g00 + 2.0 * left * g01 + g11)
    height_first = jnp.sqrt(jnp.maximum(rest_sq, 0.0) + norm_floor)
    c1 = scale / height_first
    c0 = left * c1
    i0 = 0.5 * c0
    i1 = 0.5 * c1 + c0
    i2 = c1
    to_start = i0 * g00 + i1 * g01 + i2 * g02
    to_once = i0 * g01 + i1 * g11 + i2 * g12
    proj_cross = scale * to_start
    proj_second = c0 * to_start + c1 * to_once
    r0 = i0 - proj_cross * scale - proj_second * c0
    r1 = i1 - proj_second * c1
    r2 = i2
    last_sq = (
        r0 * (r0 * g00 + 2.0 * (r1 * g01 + r2 * g02))
        + r1 * (r1 * g11 + 2.0 * r2 * g12)
        + r2 * r2 * g22
    )
    height_second = jnp.sqrt(jnp.maximum(last_sq, 0.0) + norm_floor)
    radius_first = jnp.sqrt(proj_first * proj_first + height_first * height_first)
    cos_first = proj_first / radius_first
    sin_first = height_first / radius_first
    rotated_top = cos_first * proj_cross + sin_first * proj_second
    rotated_low = cos_first * proj_second - sin_first * proj_cross
    radius_second = jnp.sqrt(rotated_low * rotated_low + height_second * height_second)
    coeff_second = -sin_first * rhs_norm * (rotated_low / radius_second) / radius_second
    coeff_first = (cos_first * rhs_norm - rotated_top * coeff_second) / radius_first
    once = once_in[...]
    start = values[...]
    result[...] = (coeff_first * scale + coeff_second * c0) * start + (coeff_second * c1) * once


def per_device(
    right_side,
    targets,
    source_nodes,
    node_weights,
    near_list,
    near_count,
    row_basis,
    column_basis,
    coupling,
):
    src_count = lax.axis_size("src")
    tgt_count = lax.axis_size("tgt")
    leaf = right_side.shape[0]
    node_rows = node_weights.shape[0]
    rank = row_basis.shape[1]
    slots = near_list.shape[1]
    stacked = src_count * rank
    device_count = src_count * tgt_count
    values = right_side.reshape(1, leaf)
    couplings = coupling.reshape(src_count * tgt_count, 1, rank * rank)
    packed_rows = 4 * node_rows + 8

    basis_rows = 2 * rank + 8
    in_hbm = functools.partial(pltpu.with_memory_space_constraint, memory_space=pltpu.HBM)
    flag_shape = jax.ShapeDtypeStruct((stacked, rank * rank), jnp.bfloat16)
    packed, basis, near, flat, spread_flags, group_flags, values = pl.pallas_call(
        functools.partial(pack_kernel, node_rows=node_rows, rank=rank),
        out_shape=(
            jax.ShapeDtypeStruct((packed_rows, leaf), jnp.float32),
            jax.ShapeDtypeStruct((basis_rows, leaf), jnp.float32),
            jax.ShapeDtypeStruct(near_list.shape, jnp.int32),
            jax.ShapeDtypeStruct((device_count, rank * rank), jnp.float32),
            flag_shape,
            flag_shape,
            jax.ShapeDtypeStruct(values.shape, jnp.float32),
        ),
        in_specs=[hbm_space] * 8,
        out_specs=(vmem_space,) * 7,
        scratch_shapes=[
            pltpu.VMEM(targets.shape, jnp.float32),
            pltpu.VMEM(couplings.shape, jnp.float32),
            pltpu.SemaphoreType.DMA((10,)),
        ],
        compiler_params=kernel_params,
        name="pack",
    )(
        in_hbm(source_nodes),
        in_hbm(node_weights),
        in_hbm(values),
        in_hbm(targets),
        in_hbm(row_basis),
        in_hbm(column_basis),
        in_hbm(near_list),
        in_hbm(couplings),
    )

    group = 2 if tgt_count % 2 == 0 else 1
    lines = tgt_count // group

    def from_line(value, shift):
        pairs = [
            (line * group + core, there * group + core)
            for line, there in partner_pairs(shift, lines)
            for core in range(group)
        ]
        return lax.ppermute(value, "tgt", pairs)

    def from_flip(value):
        return lax.ppermute(value, "tgt", [(tgt, tgt ^ 1) for tgt in range(tgt_count)])

    def from_source(value, shift):
        return lax.ppermute(value, "src", partner_pairs(shift, src_count))

    columns = [packed] + [from_line(packed, shift) for shift in range(1, lines)]
    if group == 2:
        columns = columns + [from_flip(value) for value in columns]
    bases = [basis] + [from_source(basis, shift) for shift in range(1, src_count)]

    sizes = dict(src_count=src_count, tgt_count=tgt_count, rank=rank, leaf=leaf)
    halves = leaf // 128
    stack = stack_rows(src_count, leaf)
    lines_held = -(-(halves + stacked // 128) // 8) * 8
    piece_rows = 2 * halves
    target_rows = max(8, src_count)
    message, tiles, row_bases, row_values, kept = pl.pallas_call(
        functools.partial(first_kernel, node_rows=node_rows, **sizes),
        out_shape=(
            jax.ShapeDtypeStruct((device_count, 1, leaf + stacked), jnp.float32),
            jax.ShapeDtypeStruct((slots, leaf, leaf), jnp.float32),
            jax.ShapeDtypeStruct((stacked, leaf), jnp.float32),
            jax.ShapeDtypeStruct((stack, 128), jnp.float32),
            jax.ShapeDtypeStruct((device_count, rank * rank), jnp.float32),
        ),
        in_specs=[smem_space] * 2 + [vmem_space] * (3 + tgt_count + src_count),
        out_specs=(vmem_space,) * 5,
        scratch_shapes=[
            pltpu.VMEM((tgt_count, packed_rows, leaf), jnp.float32),
            pltpu.VMEM((stacked, leaf), jnp.float32),
            pltpu.VMEM((3, target_rows, leaf), jnp.float32),
            pltpu.VMEM((halves, term_count * target_rows, 128), jnp.float32),
            pltpu.VMEM((src_count, leaf, term_count), jnp.bfloat16),
            pltpu.VMEM((halves, unique_terms * node_rows, 128), jnp.float32),
            pltpu.VMEM((tgt_count, node_rows, unique_terms, leaf), jnp.bfloat16),
            pltpu.SMEM((tgt_count,), jnp.int32),
            pltpu.VMEM((src_count, leaf, 128), jnp.float32),
            pltpu.VMEM((tgt_count, 128), jnp.float32),
        ],
        compiler_params=kernel_params,
        name="first",
    )(near, near_count, flat, spread_flags, group_flags, *columns, *bases)

    received = lax.all_to_all(message, both_axes, 0, 0, tiled=True)

    message, once = pl.pallas_call(
        functools.partial(second_kernel, **sizes),
        out_shape=(
            jax.ShapeDtypeStruct(
                (device_count, stack // piece_rows + 1, piece_rows, 128), jnp.float32
            ),
            jax.ShapeDtypeStruct((1, leaf), jnp.float32),
        ),
        in_specs=[smem_space] * 2 + [vmem_space] * 8,
        out_specs=(vmem_space, vmem_space),
        scratch_shapes=[
            pltpu.VMEM((src_count, leaf, 128), jnp.float32),
            pltpu.VMEM((tgt_count * lines_held, 128), jnp.float32),
        ],
        compiler_params=kernel_params,
        name="second",
    )(
        near,
        near_count,
        kept,
        spread_flags,
        group_flags,
        received,
        values,
        row_bases,
        row_values,
        tiles,
    )

    received = lax.all_to_all(message, both_axes, 0, 0, tiled=True)

    result = pl.pallas_call(
        functools.partial(third_kernel, src_count=src_count, tgt_count=tgt_count, leaf=leaf),
        out_shape=jax.ShapeDtypeStruct((1, leaf), jnp.float32),
        in_specs=[vmem_space] * 3,
        out_specs=vmem_space,
        compiler_params=kernel_params,
        name="third",
    )(received, values, once)
    return result.reshape(leaf)


def solution(mesh):
    return jax.shard_map(
        per_device,
        mesh=mesh,
        in_specs=(
            P(("tgt", "src")),
            P(None, ("tgt", "src")),
            P(None, None, ("tgt", "src")),
            P(None, ("tgt", "src")),
            P(None, ("tgt", "src")),
            P(("tgt", "src")),
            P(("tgt", "src"), None, None),
            P(("tgt", "src"), None, None),
            P("tgt", None, None, "src", None),
        ),
        out_specs=P(("tgt", "src")),
        check_vma=False,
    )
```

```python
import functools

import jax
import jax.numpy as jnp
from jax import lax
from jax.experimental import pallas as pl
from jax.experimental.pallas import tpu as pltpu
from jax.sharding import PartitionSpec as P

spread_sq = 0.0004
norm_floor = 1e-06
highest = lax.Precision.HIGHEST
both_axes = ("tgt", "src")
lane_contract = (((1,), (1,)), ((), ()))
plain_contract = (((1,), (0,)), ((), ()))
unique_terms = 16
term_repeats = 4
term_count = unique_terms * term_repeats
vmem_space = pl.BlockSpec(memory_space=pltpu.VMEM)
smem_space = pl.BlockSpec(memory_space=pltpu.SMEM)
hbm_space = pl.BlockSpec(memory_space=pltpu.HBM)
kernel_params = pltpu.CompilerParams(vmem_limit_bytes=32 * 1024 * 1024)


def in_three(value):
    top = value.astype(jnp.bfloat16)
    rest = value - top.astype(jnp.float32)
    middle = rest.astype(jnp.bfloat16)
    low = (rest - middle.astype(jnp.float32)).astype(jnp.bfloat16)
    return top, middle, low


def exact_dot(value, flags, contract):
    rows = value.shape[0]
    parts = jnp.concatenate([part.astype(jnp.float32) for part in in_three(value)], axis=0)
    product = lax.dot_general(
        parts.astype(jnp.bfloat16), flags, contract, preferred_element_type=jnp.float32
    )
    return product[0:rows] + (product[rows : 2 * rows] + product[2 * rows :])


def iota(shape, dim):
    return lax.broadcasted_iota(jnp.int32, shape, dim)


def stack_rows(src_count, leaf):
    return max(8, src_count * (leaf // 128))


def partner(index, shift, count):
    if count & (count - 1) == 0:
        return index ^ shift
    return lax.rem(index - shift + count, count)


def partner_pairs(shift, count):
    if count & (count - 1) == 0:
        return [(place, place ^ shift) for place in range(count)]
    return [(place, (place + shift) % count) for place in range(count)]


def on_grid(value, steps):
    return lax.round(value * steps, lax.RoundingMethod.TO_NEAREST_EVEN) * (1.0 / steps)


def as_bfloat16(value):
    return value.astype(jnp.bfloat16).astype(jnp.float32)


def coordinate_parts(coords):
    parts = []
    for value in coords:
        high = on_grid(value, 128.0)
        rest = value - high
        mid = on_grid(rest, 32768.0)
        parts.append((high, mid, as_bfloat16(rest - mid)))
    return parts


def split_terms(coords, shift):
    parts = coordinate_parts(coords)
    high_sum = sum(high * high for high, mid, low in parts)
    top = as_bfloat16(high_sum)
    rest_sum = sum((mid + low) * (2.0 * high + (mid + low)) for high, mid, low in parts) + shift
    first = as_bfloat16(rest_sum)
    second = as_bfloat16(rest_sum - first)
    return parts, [top, high_sum - top], [first, second, rest_sum - first - second]


def node_side(coords):
    parts, squares, rests = split_terms(coords, 0.0)
    terms = [piece for part in parts for piece in part] + squares + rests
    return dict(enumerate(terms))


def target_side(coords, shift):
    parts, squares, rests = split_terms(coords, shift)
    one = jnp.ones_like(squares[0])
    terms = {}
    for coord, part in enumerate(parts):
        high, mid, low = [-2.0 * piece for piece in part]
        spot = 3 * coord
        terms[spot] = high
        terms[unique_terms + spot] = mid
        terms[2 * unique_terms + spot] = low
        for piece in (1, 2):
            terms[unique_terms + spot + piece] = high
            terms[2 * unique_terms + spot + piece] = mid
            terms[3 * unique_terms + spot + piece] = low
    terms[9] = one
    terms[10] = one
    terms[14] = squares[0]
    terms[15] = squares[1]
    for piece in range(3):
        terms[unique_terms + 11 + piece] = one
    terms[unique_terms + 14] = rests[0]
    terms[unique_terms + 15] = rests[1]
    terms[2 * unique_terms + 14] = rests[2]
    return terms


def store_terms(staged, terms, rows, count, fill):
    for number in range(count):
        for half in range(staged.shape[0]):
            here = pl.ds(number * rows, rows)
            if number in terms:
                staged[half, here, :] = terms[number][:, half * 128 : (half + 1) * 128]
            elif fill is not None:
                staged[half, here, :] = jnp.full((rows, 128), fill, jnp.float32)


def pack_kernel(
    nodes,
    weights,
    values_in,
    targets,
    row_basis,
    column_basis,
    near_in,
    coupling_in,
    packed,
    basis,
    near,
    flat,
    spread_flags,
    group_flags,
    values,
    points,
    coupling,
    sems,
    *,
    node_rows,
    rank,
):
    leaf = values.shape[1]
    halves = leaf // 128
    pieces = [(values_in, values), (targets, points)]
    for half in range(halves):
        lanes = pl.ds(half * 128, 128)
        here = pl.ds((halves + half) * rank, rank)
        pieces.append((column_basis.at[0, :, lanes], basis.at[here, :]))
    early = len(pieces)
    for half in range(halves):
        lanes = pl.ds(half * 128, 128)
        pieces.append((row_basis.at[0, :, lanes], basis.at[pl.ds(half * rank, rank), :]))
        for coord in range(4):
            source = weights.at[:, lanes] if coord == 3 else nodes.at[coord, :, lanes]
            here = pl.ds((half * 4 + coord) * node_rows, node_rows)
            pieces.append((source, packed.at[here, :]))
    pieces += [(near_in, near), (coupling_in, coupling)]
    copies = [
        pltpu.make_async_copy(source, place, sems.at[number])
        for number, (source, place) in enumerate(pieces)
    ]
    for copy in copies:
        copy.start()
    spare = 4 * halves * node_rows
    packed[pl.ds(spare, 8), :] = jnp.zeros((8, 128), jnp.float32)
    shape = spread_flags.shape
    row, lane = iota(shape, 0), iota(shape, 1)
    spread_flags[...] = ((row % rank) == (lane % rank)).astype(jnp.bfloat16)
    group_flags[...] = ((row % rank) == (lane // rank)).astype(jnp.bfloat16)
    for copy in copies[:early]:
        copy.wait()
    tall = jnp.broadcast_to(values[...], (8, leaf))
    coeffs = lax.dot_general(
        tall,
        jnp.concatenate(
            [basis[pl.ds((halves + half) * rank, rank), :] for half in range(halves)], axis=1
        ),
        lane_contract,
        precision=highest,
        preferred_element_type=jnp.float32,
    )
    packed[pl.ds(spare + halves, 1), pl.ds(0, rank)] = coeffs[0:1]
    for half in range(halves):
        lanes = pl.ds(half * 128, 128)
        packed[pl.ds(spare + half, 1), :] = values[:, lanes]
        for coord in range(3):
            here = pl.ds(2 * halves * rank + coord * halves + half, 1)
            basis[here, :] = points[pl.ds(coord, 1), lanes]
        basis[pl.ds(2 * halves * rank + 3 * halves + half, 1), :] = values[:, lanes]
    for copy in copies[early:]:
        copy.wait()
    flat[...] = coupling[:, 0, :]


def far_stack(coeffs, kept, spread_flags, group_flags, row_bases, src_count, tgt_count, rank):
    stacked, leaf = row_bases.shape
    halves = leaf // 128
    rows = stack_rows(src_count, leaf)
    tiled = exact_dot(coeffs, spread_flags[pl.ds(0, coeffs.shape[1]), :], plain_contract)
    row_id = iota((rows, rank * rank), 0) // halves
    summed = jnp.zeros((rows, rank * rank), jnp.float32)
    for target in range(src_count):
        block = kept[pl.ds(target * tgt_count, tgt_count), :]
        total = jnp.sum(block * tiled, axis=0, keepdims=True)
        summed = jnp.where(row_id == target, total, summed)
    far = exact_dot(summed, group_flags[...], lane_contract)
    own = (iota((rows, stacked), 1) // rank) == (iota((rows, stacked), 0) // halves)
    own = own & (iota((rows, stacked), 0) % halves == 0)
    far = jnp.sum(jnp.where(own, far, 0.0), axis=0, keepdims=True)
    lines = []
    for first in range(0, stacked, 128):
        upright = jnp.transpose(jnp.broadcast_to(far[:, first : first + 128], (128, 128)))
        for half in range(halves):
            block = row_bases[pl.ds(first, 128), pl.ds(half * 128, 128)] * upright
            for start in range(0, 128, rank):
                line = jnp.sum(block[start : start + rank], axis=0, keepdims=True)
                lines.append(((first + start) // rank * halves + half, line))
    return stack_lines(lines, rows)


def stack_lines(lines, rows):
    row_id = iota((rows, 128), 0)
    result = jnp.zeros((rows, 128), jnp.float32)
    for number, line in lines:
        result = jnp.where(row_id == number, line, result)
    return result


def near_stack(partial, src_count, leaf):
    halves = leaf // 128
    lines = []
    for target in range(src_count):
        for half in range(halves):
            flat = jnp.transpose(partial[target, pl.ds(half * 128, 128), :])
            lines.append((target * halves + half, jnp.sum(flat, axis=0, keepdims=True)))
    return stack_lines(lines, stack_rows(src_count, leaf))


def clear_partials(partial, src_count):
    for target in range(src_count):
        partial[target] = jnp.zeros(partial.shape[1:], jnp.float32)


def add_product(partial, target, start, size, pieces, vectors):
    total = None
    for piece, vector in zip(pieces, vectors):
        total = piece * vector if total is None else total + piece * vector
    here = pl.ds(start, size)
    partial[target, here, :] = partial[target, here, :] + total


def first_kernel(
    near,
    near_count,
    flat,
    spread_flags,
    group_flags,
    *refs,
    src_count,
    tgt_count,
    node_rows,
    rank,
    leaf,
):
    columns, refs = refs[:tgt_count], refs[tgt_count:]
    bases, refs = refs[:src_count], refs[src_count:]
    message, tiles, row_bases, row_values, kept = refs[:5]
    held, col_bases, point_rows, point_staged, point_terms = refs[5:10]
    node_staged, node_terms, built, partial, far_values = refs[10:]
    tgt_index = lax.axis_index("tgt")
    src_index = lax.axis_index("src")
    halves = leaf // 128
    stacked = src_count * rank
    rows = stack_rows(src_count, leaf)
    clear_partials(partial, src_count)
    kept[...] = flat[...]
    for spot in range(tgt_count):
        there = column_place(tgt_index, spot, tgt_count)
        held[there] = columns[spot][...]
        far_values[pl.ds(there, 1), :] = columns[spot][pl.ds(4 * halves * node_rows + halves, 1), :]
        built[spot] = 0
    for shift in range(src_count):
        there = partner(src_index, shift, src_count)
        here = pl.ds(pl.multiple_of(there * rank, rank), rank)
        for half in range(halves):
            lanes = pl.ds(half * 128, 128)
            row_bases[here, lanes] = bases[shift][pl.ds(half * rank, rank), :]
            col_bases[here, lanes] = bases[shift][pl.ds((halves + half) * rank, rank), :]
            spare = 2 * halves * rank + half
            row_values[pl.ds(there * halves + half, 1), :] = bases[shift][
                pl.ds(spare + 3 * halves, 1), :
            ]
        for coord in range(3):
            spare = 2 * halves * rank + coord * halves
            point_rows[coord, pl.ds(there, 1), :] = jnp.concatenate(
                [bases[shift][pl.ds(spare + half, 1), :] for half in range(halves)], axis=1
            )
    ones_here = pl.ds((unique_terms - 2) * node_rows, 2 * node_rows)
    node_staged[:, ones_here, :] = jnp.ones((halves, 2 * node_rows, 128), jnp.float32)
    coords = [point_rows[coord] for coord in range(3)]
    target_rows = point_rows.shape[1]
    store_terms(point_staged, target_side(coords, spread_sq), target_rows, term_count, 0.0)
    for target in range(src_count):
        for half in range(halves):
            across = point_staged[half, pl.ds(target, term_count, stride=target_rows), :]
            point_terms[target, pl.ds(half * 128, 128), :] = jnp.transpose(across).astype(
                jnp.bfloat16
            )
    block = 128

    def held_rows(source, coord, start, size):
        return jnp.concatenate(
            [
                held[source, pl.ds((half * 4 + coord) * node_rows + start, size), :]
                for half in range(halves)
            ],
            axis=1,
        )


    live = near_count[0]
    slots = tiles.shape[0]
    together = 2 if slots % 2 == 0 else 1

    def some_slots(number, carry):
        numbers = [number * together + offset for offset in range(together)]
        places = []
        for slot in numbers:
            target, source = near[0, slot] - tgt_index * src_count, near[1, slot] // src_count
            places.append((slot, target, source))

            @pl.when(slot < live)
            def _():
                row = pl.ds(target * tgt_count + source, 1)
                kept[row, :] = jnp.zeros((1, kept.shape[1]), jnp.float32)

            @pl.when(built[source] == 0)
            def _():
                built[source] = 1
                coords = [held_rows(source, coord, 0, node_rows) for coord in range(3)]
                store_terms(node_staged, node_side(coords), node_rows, unique_terms, None)
                for node in range(node_rows):
                    for half in range(halves):
                        across = node_staged[half, pl.ds(node, unique_terms, stride=node_rows), :]
                        lanes = pl.ds(half * 128, 128)
                        node_terms[source, node, :, lanes] = across.astype(jnp.bfloat16)

        for slot, target, source in places:
            weight = (slot < live).astype(jnp.float32)
            vectors = [
                weight * held[source, pl.ds(4 * halves * node_rows + half, 1), :]
                for half in range(halves)
            ]
            for start in range(0, leaf, block):
                here = pl.ds(start, block)
                lhs = point_terms[target, here, :]
                tile = None
                for node in range(node_rows):
                    rhs = jnp.concatenate([node_terms[source, node]] * term_repeats, axis=0)
                    square = lax.dot_general(
                        lhs, rhs, plain_contract, preferred_element_type=jnp.float32
                    )
                    term = held_rows(source, 3, node, 1) * lax.rsqrt(square)
                    tile = term if tile is None else tile + term
                tiles[slot, here, :] = tile
                pieces = [tile[:, half * 128 : (half + 1) * 128] for half in range(halves)]
                add_product(partial, target, start, block, pieces, vectors)
        return carry

    lax.fori_loop(0, (live + together - 1) // together, some_slots, 0)
    total = near_stack(partial, src_count, leaf) + far_stack(
        far_values[...], kept, spread_flags, group_flags, row_bases, src_count, tgt_count, rank
    )
    coeffs = []
    for first in range(0, stacked, 128):
        blocks = []
        for start in range(first, first + 128, rank):
            target = start // rank
            block = None
            for half in range(halves):
                line = total[target * halves + half : target * halves + half + 1]
                piece = col_bases[pl.ds(start, rank), pl.ds(half * 128, 128)] * line
                block = piece if block is None else block + piece
            blocks.append(block)
        flat = jnp.transpose(jnp.concatenate(blocks, axis=0))
        coeffs.append(jnp.sum(flat, axis=0, keepdims=True))
    for target in range(src_count):
        lines = [total[target * halves + half : target * halves + half + 1] for half in range(halves)]
        for number, line in enumerate(lines + coeffs):
            for there in range(tgt_count):
                message[there * src_count + target, :, pl.ds(number * 128, 128)] = line


def column_place(tgt_index, spot, tgt_count):
    group = 2 if tgt_count % 2 == 0 else 1
    lines = tgt_count // group
    shift, flip = spot % lines, spot // lines
    return partner(tgt_index // group, shift, lines) * group + lax.rem(
        tgt_index % group + flip, group
    )


def second_kernel(
    near_in,
    near_count,
    kept,
    spread_flags,
    group_flags,
    received,
    values,
    row_bases,
    row_values,
    tiles,
    message,
    once_out,
    partial,
    image,
    near,
    near_sem,
    *,
    src_count,
    tgt_count,
    rank,
    leaf,
):
    tgt_index = lax.axis_index("tgt")
    src_index = lax.axis_index("src")
    halves = leaf // 128
    stacked = src_count * rank
    rows = stack_rows(src_count, leaf)
    lines = image.shape[0] // tgt_count
    near_copy = pltpu.make_async_copy(near_in, near, near_sem)
    near_copy.start()
    clear_partials(partial, src_count)
    for there in range(tgt_count):
        for number in range(halves + stacked // 128):
            lanes = pl.ds(number * 128, 128)
            total = received[there * src_count, :, lanes]
            for source in range(1, src_count):
                total = total + received[there * src_count + source, :, lanes]
            image[pl.ds(there * lines + number, 1), :] = total

    near_copy.wait()

    def one_slot(slot, carry):
        target, source = near[0, slot] - tgt_index * src_count, near[1, slot] // src_count
        vectors = [image[pl.ds(source * lines + half, 1), :] for half in range(halves)]
        block = 64
        for start in range(0, leaf, block):
            here = pl.ds(start, block)
            pieces = [tiles[slot, here, pl.ds(half * 128, 128)] for half in range(halves)]
            add_product(partial, target, start, block, pieces, vectors)
        return carry

    lax.fori_loop(0, near_count[0], one_slot, 0)
    coeffs = jnp.concatenate(
        [
            image[pl.ds(halves + piece, tgt_count, stride=lines), :]
            for piece in range(stacked // 128)
        ],
        axis=1,
    )
    mine = (iota((tgt_count, stacked), 1) // rank) == src_index
    coeffs = jnp.where(mine, coeffs, 0.0)
    twice = near_stack(partial, src_count, leaf) + far_stack(
        coeffs, kept, spread_flags, group_flags, row_bases, src_count, tgt_count, rank
    )
    once = [image[pl.ds(tgt_index * lines + half, 1), :] for half in range(halves)]
    start = [values[:, pl.ds(half * 128, 128)] for half in range(halves)]
    for half in range(halves):
        once_out[:, pl.ds(half * 128, 128)] = once[half]

    def inner(left, right):
        total = sum(one * other for one, other in zip(left, right))
        return jnp.sum(total, axis=1, keepdims=True)

    cross = jnp.sum(row_values[...] * twice, axis=0, keepdims=True)
    scalars = [inner(start, start), inner(start, once), jnp.sum(cross, axis=1, keepdims=True)]
    lane_id = iota((1, 128), 1)
    line = jnp.zeros((1, 128), jnp.float32)
    for number, value in enumerate(scalars):
        line = jnp.where(lane_id == number, value, line)
    piece_rows = message.shape[2]
    share = piece_rows // halves
    row_id = iota((piece_rows, 128), 0)
    spare = lax.rem(src_index + 1, share) * halves
    extra = jnp.where(row_id == spare, line, 0.0)
    for half in range(halves):
        extra = jnp.where(row_id == lax.rem(src_index, share) * halves + half, once[half], extra)
    pieces = [twice[first : first + piece_rows] for first in range(0, rows, piece_rows)]
    for there in range(src_count * tgt_count):
        for number, piece in enumerate(pieces + [extra]):
            message[there, number] = piece


def third_kernel(received, values, once_in, result, *, src_count, tgt_count, leaf):
    halves = leaf // 128
    piece_rows = received.shape[2]
    share = piece_rows // halves
    row_id = iota((piece_rows, 128), 0)
    s11 = s12 = s22 = scalars = jnp.zeros((piece_rows, 128), jnp.float32)
    for there in range(tgt_count):
        for piece in range(src_count // share):
            twice = once = None
            for source in range(src_count):
                part = received[there * src_count + source, piece]
                twice = part if twice is None else twice + part
            for spot in range(share):
                extra = received[there * src_count + piece * share + spot, received.shape[1] - 1]
                mine = row_id // halves == spot
                once = extra if once is None else jnp.where(mine, extra, once)
                spare = row_id == ((spot + 1) % share) * halves
                scalars = scalars + jnp.where(spare, extra, 0.0)
            s11 = s11 + once * once
            s12 = s12 + once * twice
            s22 = s22 + twice * twice

    def whole(value):
        return jnp.sum(jnp.sum(value, axis=0, keepdims=True), axis=1, keepdims=True)

    g11, g12, g22 = whole(s11), whole(s12), whole(s22)
    scalars = jnp.sum(scalars, axis=0, keepdims=True)
    g00, g01, g02 = [scalars[:, number : number + 1] for number in range(3)]
    rhs_norm = jnp.sqrt(g00 + norm_floor)
    scale = 1.0 / rhs_norm
    proj_first = scale * scale * (0.5 * g00 + g01)
    left = 0.5 - proj_first
    rest_sq = scale * scale * (left * left * g00 + 2.0 * left * g01 + g11)
    height_first = jnp.sqrt(jnp.maximum(rest_sq, 0.0) + norm_floor)
    c1 = scale / height_first
    c0 = left * c1
    i0 = 0.5 * c0
    i1 = 0.5 * c1 + c0
    i2 = c1
    to_start = i0 * g00 + i1 * g01 + i2 * g02
    to_once = i0 * g01 + i1 * g11 + i2 * g12
    proj_cross = scale * to_start
    proj_second = c0 * to_start + c1 * to_once
    r0 = i0 - proj_cross * scale - proj_second * c0
    r1 = i1 - proj_second * c1
    r2 = i2
    last_sq = (
        r0 * (r0 * g00 + 2.0 * (r1 * g01 + r2 * g02))
        + r1 * (r1 * g11 + 2.0 * r2 * g12)
        + r2 * r2 * g22
    )
    height_second = jnp.sqrt(jnp.maximum(last_sq, 0.0) + norm_floor)
    radius_first = jnp.sqrt(proj_first * proj_first + height_first * height_first)
    cos_first = proj_first / radius_first
    sin_first = height_first / radius_first
    rotated_top = cos_first * proj_cross + sin_first * proj_second
    rotated_low = cos_first * proj_second - sin_first * proj_cross
    radius_second = jnp.sqrt(rotated_low * rotated_low + height_second * height_second)
    coeff_second = -sin_first * rhs_norm * (rotated_low / radius_second) / radius_second
    coeff_first = (cos_first * rhs_norm - rotated_top * coeff_second) / radius_first
    once = once_in[...]
    start = values[...]
    result[...] = (coeff_first * scale + coeff_second * c0) * start + (coeff_second * c1) * once


def per_device(
    right_side,
    targets,
    source_nodes,
    node_weights,
    near_list,
    near_count,
    row_basis,
    column_basis,
    coupling,
):
    src_count = lax.axis_size("src")
    tgt_count = lax.axis_size("tgt")
    leaf = right_side.shape[0]
    node_rows = node_weights.shape[0]
    rank = row_basis.shape[1]
    slots = near_list.shape[1]
    stacked = src_count * rank
    device_count = src_count * tgt_count
    values = right_side.reshape(1, leaf)
    couplings = coupling.reshape(src_count * tgt_count, 1, rank * rank)
    halves = leaf // 128
    packed_rows = 4 * halves * node_rows + 8

    basis_rows = 2 * halves * rank + 8
    in_hbm = functools.partial(pltpu.with_memory_space_constraint, memory_space=pltpu.HBM)
    flag_shape = jax.ShapeDtypeStruct((stacked, rank * rank), jnp.bfloat16)
    packed, basis, near, flat, spread_flags, group_flags, values = pl.pallas_call(
        functools.partial(pack_kernel, node_rows=node_rows, rank=rank),
        out_shape=(
            jax.ShapeDtypeStruct((packed_rows, 128), jnp.float32),
            jax.ShapeDtypeStruct((basis_rows, 128), jnp.float32),
            jax.ShapeDtypeStruct(near_list.shape, jnp.int32),
            jax.ShapeDtypeStruct((device_count, rank * rank), jnp.float32),
            flag_shape,
            flag_shape,
            jax.ShapeDtypeStruct(values.shape, jnp.float32),
        ),
        in_specs=[hbm_space] * 8,
        out_specs=(vmem_space,) * 7,
        scratch_shapes=[
            pltpu.VMEM(targets.shape, jnp.float32),
            pltpu.VMEM(couplings.shape, jnp.float32),
            pltpu.SemaphoreType.DMA((4 + 6 * halves,)),
        ],
        compiler_params=kernel_params,
        name="pack",
    )(
        in_hbm(source_nodes),
        in_hbm(node_weights),
        in_hbm(values),
        in_hbm(targets),
        in_hbm(row_basis),
        in_hbm(column_basis),
        in_hbm(near_list),
        in_hbm(couplings),
    )

    group = 2 if tgt_count % 2 == 0 else 1
    lines = tgt_count // group

    def from_line(value, shift):
        pairs = [
            (line * group + core, there * group + core)
            for line, there in partner_pairs(shift, lines)
            for core in range(group)
        ]
        return lax.ppermute(value, "tgt", pairs)

    def from_flip(value):
        return lax.ppermute(value, "tgt", [(tgt, tgt ^ 1) for tgt in range(tgt_count)])

    def from_source(value, shift):
        return lax.ppermute(value, "src", partner_pairs(shift, src_count))

    columns = [packed] + [from_line(packed, shift) for shift in range(1, lines)]
    if group == 2:
        columns = columns + [from_flip(value) for value in columns]
    bases = [basis] + [from_source(basis, shift) for shift in range(1, src_count)]

    sizes = dict(src_count=src_count, tgt_count=tgt_count, rank=rank, leaf=leaf)
    stack = stack_rows(src_count, leaf)
    lines_held = -(-(halves + stacked // 128) // 8) * 8
    piece_rows = 2 * halves
    target_rows = max(8, src_count)
    message, tiles, row_bases, row_values, kept = pl.pallas_call(
        functools.partial(first_kernel, node_rows=node_rows, **sizes),
        out_shape=(
            jax.ShapeDtypeStruct((device_count, 1, leaf + stacked), jnp.float32),
            jax.ShapeDtypeStruct((slots, leaf, leaf), jnp.float32),
            jax.ShapeDtypeStruct((stacked, leaf), jnp.float32),
            jax.ShapeDtypeStruct((stack, 128), jnp.float32),
            jax.ShapeDtypeStruct((device_count, rank * rank), jnp.float32),
        ),
        in_specs=[smem_space, smem_space] + [vmem_space] * (3 + tgt_count + src_count),
        out_specs=(vmem_space,) * 5,
        scratch_shapes=[
            pltpu.VMEM((tgt_count, packed_rows, 128), jnp.float32),
            pltpu.VMEM((stacked, leaf), jnp.float32),
            pltpu.VMEM((3, target_rows, leaf), jnp.float32),
            pltpu.VMEM((halves, term_count * target_rows, 128), jnp.float32),
            pltpu.VMEM((src_count, leaf, term_count), jnp.bfloat16),
            pltpu.VMEM((halves, unique_terms * node_rows, 128), jnp.float32),
            pltpu.VMEM((tgt_count, node_rows, unique_terms, leaf), jnp.bfloat16),
            pltpu.SMEM((tgt_count,), jnp.int32),
            pltpu.VMEM((src_count, leaf, 128), jnp.float32),
            pltpu.VMEM((tgt_count, 128), jnp.float32),
        ],
        compiler_params=kernel_params,
        name="first",
    )(near, near_count, flat, spread_flags, group_flags, *columns, *bases)

    received = lax.all_to_all(message, both_axes, 0, 0, tiled=True)

    message, once = pl.pallas_call(
        functools.partial(second_kernel, **sizes),
        out_shape=(
            jax.ShapeDtypeStruct(
                (device_count, stack // piece_rows + 1, piece_rows, 128), jnp.float32
            ),
            jax.ShapeDtypeStruct((1, leaf), jnp.float32),
        ),
        in_specs=[vmem_space, smem_space] + [vmem_space] * 8,
        out_specs=(vmem_space, vmem_space),
        scratch_shapes=[
            pltpu.VMEM((src_count, leaf, 128), jnp.float32),
            pltpu.VMEM((tgt_count * lines_held, 128), jnp.float32),
            pltpu.SMEM(near_list.shape, jnp.int32),
            pltpu.SemaphoreType.DMA,
        ],
        compiler_params=kernel_params,
        name="second",
    )(
        near,
        near_count,
        kept,
        spread_flags,
        group_flags,
        received,
        values,
        row_bases,
        row_values,
        tiles,
    )

    received = lax.all_to_all(message, both_axes, 0, 0, tiled=True)

    result = pl.pallas_call(
        functools.partial(third_kernel, src_count=src_count, tgt_count=tgt_count, leaf=leaf),
        out_shape=jax.ShapeDtypeStruct((1, leaf), jnp.float32),
        in_specs=[vmem_space] * 3,
        out_specs=vmem_space,
        compiler_params=kernel_params,
        name="third",
    )(received, values, once)
    return result.reshape(leaf)


def solution(mesh):
    return jax.shard_map(
        per_device,
        mesh=mesh,
        in_specs=(
            P(("tgt", "src")),
            P(None, ("tgt", "src")),
            P(None, None, ("tgt", "src")),
            P(None, ("tgt", "src")),
            P(None, ("tgt", "src")),
            P(("tgt", "src")),
            P(("tgt", "src"), None, None),
            P(("tgt", "src"), None, None),
            P("tgt", None, None, "src", None),
        ),
        out_specs=P(("tgt", "src")),
        check_vma=False,
    )
```

```python
import functools

import jax
import jax.numpy as jnp
from jax import lax
from jax.experimental import pallas as pl
from jax.experimental.pallas import tpu as pltpu
from jax.sharding import PartitionSpec as P

spread_sq = 0.0004
norm_floor = 1e-06
highest = lax.Precision.HIGHEST
both_axes = ("tgt", "src")
lane_contract = (((1,), (1,)), ((), ()))
plain_contract = (((1,), (0,)), ((), ()))
unique_terms = 16
term_repeats = 4
term_count = unique_terms * term_repeats
vmem_space = pl.BlockSpec(memory_space=pltpu.VMEM)
smem_space = pl.BlockSpec(memory_space=pltpu.SMEM)
hbm_space = pl.BlockSpec(memory_space=pltpu.HBM)
kernel_params = pltpu.CompilerParams(vmem_limit_bytes=32 * 1024 * 1024)


def in_three(value):
    top = value.astype(jnp.bfloat16)
    rest = value - top.astype(jnp.float32)
    middle = rest.astype(jnp.bfloat16)
    low = (rest - middle.astype(jnp.float32)).astype(jnp.bfloat16)
    return top, middle, low


def exact_dot(value, flags, contract):
    rows = value.shape[0]
    parts = jnp.concatenate([part.astype(jnp.float32) for part in in_three(value)], axis=0)
    product = lax.dot_general(
        parts.astype(jnp.bfloat16), flags, contract, preferred_element_type=jnp.float32
    )
    return product[0:rows] + (product[rows : 2 * rows] + product[2 * rows :])


def iota(shape, dim):
    return lax.broadcasted_iota(jnp.int32, shape, dim)


def stack_rows(src_count, leaf):
    return max(8, src_count * (leaf // 128))


def partner(index, shift, count):
    if count & (count - 1) == 0:
        return index ^ shift
    return lax.rem(index - shift + count, count)


def partner_pairs(shift, count):
    if count & (count - 1) == 0:
        return [(place, place ^ shift) for place in range(count)]
    return [(place, (place + shift) % count) for place in range(count)]


def on_grid(value, steps):
    return lax.round(value * steps, lax.RoundingMethod.TO_NEAREST_EVEN) * (1.0 / steps)


def as_bfloat16(value):
    return value.astype(jnp.bfloat16).astype(jnp.float32)


def coordinate_parts(coords):
    parts = []
    for value in coords:
        high = on_grid(value, 128.0)
        rest = value - high
        mid = on_grid(rest, 32768.0)
        parts.append((high, mid, as_bfloat16(rest - mid)))
    return parts


def split_terms(coords, shift):
    parts = coordinate_parts(coords)
    high_sum = sum(high * high for high, mid, low in parts)
    top = as_bfloat16(high_sum)
    rest_sum = sum((mid + low) * (2.0 * high + (mid + low)) for high, mid, low in parts) + shift
    first = as_bfloat16(rest_sum)
    second = as_bfloat16(rest_sum - first)
    return parts, [top, high_sum - top], [first, second, rest_sum - first - second]


def node_side(coords):
    parts, squares, rests = split_terms(coords, 0.0)
    terms = [piece for part in parts for piece in part] + squares + rests
    return dict(enumerate(terms))


def target_side(coords, shift):
    parts, squares, rests = split_terms(coords, shift)
    one = jnp.ones_like(squares[0])
    terms = {}
    for coord, part in enumerate(parts):
        high, mid, low = [-2.0 * piece for piece in part]
        spot = 3 * coord
        terms[spot] = high
        terms[unique_terms + spot] = mid
        terms[2 * unique_terms + spot] = low
        for piece in (1, 2):
            terms[unique_terms + spot + piece] = high
            terms[2 * unique_terms + spot + piece] = mid
            terms[3 * unique_terms + spot + piece] = low
    terms[9] = one
    terms[10] = one
    terms[14] = squares[0]
    terms[15] = squares[1]
    for piece in range(3):
        terms[unique_terms + 11 + piece] = one
    terms[unique_terms + 14] = rests[0]
    terms[unique_terms + 15] = rests[1]
    terms[2 * unique_terms + 14] = rests[2]
    return terms


def store_terms(staged, terms, rows, count, fill):
    for number in range(count):
        for half in range(staged.shape[0]):
            here = pl.ds(number * rows, rows)
            if number in terms:
                staged[half, here, :] = terms[number][:, half * 128 : (half + 1) * 128]
            elif fill is not None:
                staged[half, here, :] = jnp.full((rows, 128), fill, jnp.float32)


def pack_kernel(
    nodes,
    weights,
    values_in,
    targets,
    row_basis,
    column_basis,
    near_in,
    coupling_in,
    packed,
    basis,
    near,
    flat,
    spread_flags,
    group_flags,
    values,
    points,
    coupling,
    sems,
    *,
    node_rows,
    rank,
):
    pieces = [
        (column_basis.at[0], basis.at[pl.ds(rank, rank), :]),
        (values_in, values),
        (targets, points),
        (near_in, near),
        (row_basis.at[0], basis.at[pl.ds(0, rank), :]),
        (weights, packed.at[pl.ds(3 * node_rows, node_rows), :]),
        (coupling_in, coupling),
    ]
    for coord in range(3):
        pieces.append((nodes.at[coord], packed.at[pl.ds(coord * node_rows, node_rows), :]))
    copies = [
        pltpu.make_async_copy(source, place, sems.at[number])
        for number, (source, place) in enumerate(pieces)
    ]
    for copy in copies:
        copy.start()
    leaf = values.shape[1]
    packed[pl.ds(4 * node_rows, 8), :] = jnp.zeros((8, leaf), jnp.float32)
    basis[pl.ds(2 * rank, 8), :] = jnp.zeros((8, leaf), jnp.float32)
    shape = spread_flags.shape
    row, lane = iota(shape, 0), iota(shape, 1)
    spread_flags[...] = ((row % rank) == (lane % rank)).astype(jnp.bfloat16)
    group_flags[...] = ((row % rank) == (lane // rank)).astype(jnp.bfloat16)
    for copy in copies[:3]:
        copy.wait()
    vector = values[...]
    packed[pl.ds(4 * node_rows, 1), :] = vector
    tall = jnp.broadcast_to(vector, (8, leaf))
    coeffs = lax.dot_general(
        tall,
        basis[pl.ds(rank, rank), :],
        lane_contract,
        precision=highest,
        preferred_element_type=jnp.float32,
    )
    packed[pl.ds(4 * node_rows + 1, 1), pl.ds(0, rank)] = coeffs[0:1]
    basis[pl.ds(2 * rank, 3), :] = points[...]
    basis[pl.ds(2 * rank + 3, 1), :] = vector
    for copy in copies[3:]:
        copy.wait()
    flat[...] = coupling[:, 0, :]


def far_stack(coeffs, kept, spread_flags, group_flags, row_bases, src_count, tgt_count, rank):
    stacked, leaf = row_bases.shape
    halves = leaf // 128
    rows = stack_rows(src_count, leaf)
    tiled = exact_dot(coeffs, spread_flags[pl.ds(0, coeffs.shape[1]), :], plain_contract)
    row_id = iota((rows, rank * rank), 0) // halves
    summed = jnp.zeros((rows, rank * rank), jnp.float32)
    for target in range(src_count):
        block = kept[pl.ds(target * tgt_count, tgt_count), :]
        total = jnp.sum(block * tiled, axis=0, keepdims=True)
        summed = jnp.where(row_id == target, total, summed)
    far = exact_dot(summed, group_flags[...], lane_contract)
    own = (iota((rows, stacked), 1) // rank) == (iota((rows, stacked), 0) // halves)
    own = own & (iota((rows, stacked), 0) % halves == 0)
    far = jnp.sum(jnp.where(own, far, 0.0), axis=0, keepdims=True)
    lines = []
    for first in range(0, stacked, 128):
        upright = jnp.transpose(jnp.broadcast_to(far[:, first : first + 128], (128, 128)))
        for half in range(halves):
            block = row_bases[pl.ds(first, 128), pl.ds(half * 128, 128)] * upright
            for start in range(0, 128, rank):
                line = jnp.sum(block[start : start + rank], axis=0, keepdims=True)
                lines.append(((first + start) // rank * halves + half, line))
    return stack_lines(lines, rows)


def stack_lines(lines, rows):
    row_id = iota((rows, 128), 0)
    result = jnp.zeros((rows, 128), jnp.float32)
    for number, line in lines:
        result = jnp.where(row_id == number, line, result)
    return result


def near_stack(partial, src_count, leaf):
    halves = leaf // 128
    lines = []
    for target in range(src_count):
        for half in range(halves):
            flat = jnp.transpose(partial[target, pl.ds(half * 128, 128), :])
            lines.append((target * halves + half, jnp.sum(flat, axis=0, keepdims=True)))
    return stack_lines(lines, stack_rows(src_count, leaf))


def clear_partials(partial, src_count):
    for target in range(src_count):
        partial[target] = jnp.zeros(partial.shape[1:], jnp.float32)


def add_product(partial, target, start, size, pieces, vectors):
    total = None
    for piece, vector in zip(pieces, vectors):
        total = piece * vector if total is None else total + piece * vector
    here = pl.ds(start, size)
    partial[target, here, :] = partial[target, here, :] + total


def first_kernel(
    near,
    near_count,
    flat,
    spread_flags,
    group_flags,
    *refs,
    src_count,
    tgt_count,
    node_rows,
    rank,
    leaf,
):
    columns, refs = refs[:tgt_count], refs[tgt_count:]
    bases, refs = refs[:src_count], refs[src_count:]
    message, tiles, row_bases, row_values, kept = refs[:5]
    held, col_bases, point_rows, point_staged, point_terms = refs[5:10]
    node_staged, node_terms, built, partial, far_values = refs[10:]
    tgt_index = lax.axis_index("tgt")
    src_index = lax.axis_index("src")
    halves = leaf // 128
    stacked = src_count * rank
    rows = stack_rows(src_count, leaf)
    clear_partials(partial, src_count)
    kept[...] = flat[...]
    for spot in range(tgt_count):
        there = column_place(tgt_index, spot, tgt_count)
        held[there] = columns[spot][...]
        far_values[pl.ds(there, 1), :] = columns[spot][pl.ds(4 * node_rows + 1, 1), pl.ds(0, 128)]
        built[spot] = 0
    for shift in range(src_count):
        there = partner(src_index, shift, src_count)
        here = pl.ds(pl.multiple_of(there * rank, rank), rank)
        row_bases[here, :] = bases[shift][pl.ds(0, rank), :]
        col_bases[here, :] = bases[shift][pl.ds(rank, rank), :]
        for coord in range(3):
            point_rows[coord, pl.ds(there, 1), :] = bases[shift][pl.ds(2 * rank + coord, 1), :]
        for half in range(halves):
            row_values[pl.ds(there * halves + half, 1), :] = bases[shift][
                pl.ds(2 * rank + 3, 1), pl.ds(half * 128, 128)
            ]
    ones_here = pl.ds((unique_terms - 2) * node_rows, 2 * node_rows)
    node_staged[:, ones_here, :] = jnp.ones((halves, 2 * node_rows, 128), jnp.float32)
    coords = [point_rows[coord] for coord in range(3)]
    target_rows = point_rows.shape[1]
    store_terms(point_staged, target_side(coords, spread_sq), target_rows, term_count, 0.0)
    for target in range(src_count):
        for half in range(halves):
            across = point_staged[half, pl.ds(target, term_count, stride=target_rows), :]
            point_terms[target, pl.ds(half * 128, 128), :] = jnp.transpose(across).astype(
                jnp.bfloat16
            )
    block = 128

    live = near_count[0]
    slots = tiles.shape[0]
    together = 2 if slots % 2 == 0 else 1

    def some_slots(number, carry):
        numbers = [number * together + offset for offset in range(together)]
        places = []
        for slot in numbers:
            target, source = near[0, slot] - tgt_index * src_count, near[1, slot] // src_count
            places.append((slot, target, source))

            @pl.when(slot < live)
            def _():
                row = pl.ds(target * tgt_count + source, 1)
                kept[row, :] = jnp.zeros((1, kept.shape[1]), jnp.float32)

            @pl.when(built[source] == 0)
            def _():
                built[source] = 1
                coords = [held[source, pl.ds(coord * node_rows, node_rows), :] for coord in range(3)]
                store_terms(node_staged, node_side(coords), node_rows, unique_terms, None)
                for node in range(node_rows):
                    for half in range(halves):
                        across = node_staged[half, pl.ds(node, unique_terms, stride=node_rows), :]
                        lanes = pl.ds(half * 128, 128)
                        node_terms[source, node, :, lanes] = across.astype(jnp.bfloat16)

        for slot, target, source in places:
            weight = (slot < live).astype(jnp.float32)
            vectors = [
                weight * held[source, pl.ds(4 * node_rows, 1), pl.ds(half * 128, 128)]
                for half in range(halves)
            ]
            for start in range(0, leaf, block):
                here = pl.ds(start, block)
                lhs = point_terms[target, here, :]
                tile = None
                for node in range(node_rows):
                    rhs = jnp.concatenate([node_terms[source, node]] * term_repeats, axis=0)
                    square = lax.dot_general(
                        lhs, rhs, plain_contract, preferred_element_type=jnp.float32
                    )
                    term = held[source, pl.ds(3 * node_rows + node, 1), :] * lax.rsqrt(square)
                    tile = term if tile is None else tile + term
                tiles[slot, here, :] = tile
                pieces = [tile[:, half * 128 : (half + 1) * 128] for half in range(halves)]
                add_product(partial, target, start, block, pieces, vectors)
        return carry

    lax.fori_loop(0, (live + together - 1) // together, some_slots, 0)
    total = near_stack(partial, src_count, leaf) + far_stack(
        far_values[...], kept, spread_flags, group_flags, row_bases, src_count, tgt_count, rank
    )
    coeffs = []
    for first in range(0, stacked, 128):
        blocks = []
        for start in range(first, first + 128, rank):
            target = start // rank
            block = None
            for half in range(halves):
                line = total[target * halves + half : target * halves + half + 1]
                piece = col_bases[pl.ds(start, rank), pl.ds(half * 128, 128)] * line
                block = piece if block is None else block + piece
            blocks.append(block)
        flat = jnp.transpose(jnp.concatenate(blocks, axis=0))
        coeffs.append(jnp.sum(flat, axis=0, keepdims=True))
    for target in range(src_count):
        lines = [total[target * halves + half : target * halves + half + 1] for half in range(halves)]
        for number, line in enumerate(lines + coeffs):
            for there in range(tgt_count):
                message[there * src_count + target, :, pl.ds(number * 128, 128)] = line


def column_place(tgt_index, spot, tgt_count):
    group = 2 if tgt_count % 2 == 0 else 1
    lines = tgt_count // group
    shift, flip = spot % lines, spot // lines
    return partner(tgt_index // group, shift, lines) * group + lax.rem(
        tgt_index % group + flip, group
    )


def second_kernel(
    near_in,
    near_count,
    kept,
    spread_flags,
    group_flags,
    received,
    values,
    row_bases,
    row_values,
    tiles,
    message,
    once_out,
    partial,
    image,
    near,
    near_sem,
    *,
    src_count,
    tgt_count,
    rank,
    leaf,
):
    tgt_index = lax.axis_index("tgt")
    src_index = lax.axis_index("src")
    halves = leaf // 128
    stacked = src_count * rank
    rows = stack_rows(src_count, leaf)
    lines = image.shape[0] // tgt_count
    near_copy = pltpu.make_async_copy(near_in, near, near_sem)
    near_copy.start()
    clear_partials(partial, src_count)
    for there in range(tgt_count):
        for number in range(halves + stacked // 128):
            lanes = pl.ds(number * 128, 128)
            total = received[there * src_count, :, lanes]
            for source in range(1, src_count):
                total = total + received[there * src_count + source, :, lanes]
            image[pl.ds(there * lines + number, 1), :] = total

    near_copy.wait()

    def one_slot(slot, carry):
        target, source = near[0, slot] - tgt_index * src_count, near[1, slot] // src_count
        vectors = [image[pl.ds(source * lines + half, 1), :] for half in range(halves)]
        block = 64
        for start in range(0, leaf, block):
            here = pl.ds(start, block)
            pieces = [tiles[slot, here, pl.ds(half * 128, 128)] for half in range(halves)]
            add_product(partial, target, start, block, pieces, vectors)
        return carry

    lax.fori_loop(0, near_count[0], one_slot, 0)
    coeffs = jnp.concatenate(
        [
            image[pl.ds(halves + piece, tgt_count, stride=lines), :]
            for piece in range(stacked // 128)
        ],
        axis=1,
    )
    mine = (iota((tgt_count, stacked), 1) // rank) == src_index
    coeffs = jnp.where(mine, coeffs, 0.0)
    twice = near_stack(partial, src_count, leaf) + far_stack(
        coeffs, kept, spread_flags, group_flags, row_bases, src_count, tgt_count, rank
    )
    once = [image[pl.ds(tgt_index * lines + half, 1), :] for half in range(halves)]
    start = [values[:, pl.ds(half * 128, 128)] for half in range(halves)]
    for half in range(halves):
        once_out[:, pl.ds(half * 128, 128)] = once[half]

    def inner(left, right):
        total = sum(one * other for one, other in zip(left, right))
        return jnp.sum(total, axis=1, keepdims=True)

    cross = jnp.sum(row_values[...] * twice, axis=0, keepdims=True)
    scalars = [inner(start, start), inner(start, once), jnp.sum(cross, axis=1, keepdims=True)]
    lane_id = iota((1, 128), 1)
    line = jnp.zeros((1, 128), jnp.float32)
    for number, value in enumerate(scalars):
        line = jnp.where(lane_id == number, value, line)
    piece_rows = message.shape[2]
    share = piece_rows // halves
    row_id = iota((piece_rows, 128), 0)
    spare = lax.rem(src_index + 1, share) * halves
    extra = jnp.where(row_id == spare, line, 0.0)
    for half in range(halves):
        extra = jnp.where(row_id == lax.rem(src_index, share) * halves + half, once[half], extra)
    pieces = [twice[first : first + piece_rows] for first in range(0, rows, piece_rows)]
    for there in range(src_count * tgt_count):
        for number, piece in enumerate(pieces + [extra]):
            message[there, number] = piece


def third_kernel(received, values, once_in, result, *, src_count, tgt_count, leaf):
    halves = leaf // 128
    piece_rows = received.shape[2]
    share = piece_rows // halves
    row_id = iota((piece_rows, 128), 0)
    s11 = s12 = s22 = scalars = jnp.zeros((piece_rows, 128), jnp.float32)
    for there in range(tgt_count):
        for piece in range(src_count // share):
            twice = once = None
            for source in range(src_count):
                part = received[there * src_count + source, piece]
                twice = part if twice is None else twice + part
            for spot in range(share):
                extra = received[there * src_count + piece * share + spot, received.shape[1] - 1]
                mine = row_id // halves == spot
                once = extra if once is None else jnp.where(mine, extra, once)
                spare = row_id == ((spot + 1) % share) * halves
                scalars = scalars + jnp.where(spare, extra, 0.0)
            s11 = s11 + once * once
            s12 = s12 + once * twice
            s22 = s22 + twice * twice

    def whole(value):
        return jnp.sum(jnp.sum(value, axis=0, keepdims=True), axis=1, keepdims=True)

    g11, g12, g22 = whole(s11), whole(s12), whole(s22)
    scalars = jnp.sum(scalars, axis=0, keepdims=True)
    g00, g01, g02 = [scalars[:, number : number + 1] for number in range(3)]
    rhs_norm = jnp.sqrt(g00 + norm_floor)
    scale = 1.0 / rhs_norm
    proj_first = scale * scale * (0.5 * g00 + g01)
    left = 0.5 - proj_first
    rest_sq = scale * scale * (left * left * g00 + 2.0 * left * g01 + g11)
    height_first = jnp.sqrt(jnp.maximum(rest_sq, 0.0) + norm_floor)
    c1 = scale / height_first
    c0 = left * c1
    i0 = 0.5 * c0
    i1 = 0.5 * c1 + c0
    i2 = c1
    to_start = i0 * g00 + i1 * g01 + i2 * g02
    to_once = i0 * g01 + i1 * g11 + i2 * g12
    proj_cross = scale * to_start
    proj_second = c0 * to_start + c1 * to_once
    r0 = i0 - proj_cross * scale - proj_second * c0
    r1 = i1 - proj_second * c1
    r2 = i2
    last_sq = (
        r0 * (r0 * g00 + 2.0 * (r1 * g01 + r2 * g02))
        + r1 * (r1 * g11 + 2.0 * r2 * g12)
        + r2 * r2 * g22
    )
    height_second = jnp.sqrt(jnp.maximum(last_sq, 0.0) + norm_floor)
    radius_first = jnp.sqrt(proj_first * proj_first + height_first * height_first)
    cos_first = proj_first / radius_first
    sin_first = height_first / radius_first
    rotated_top = cos_first * proj_cross + sin_first * proj_second
    rotated_low = cos_first * proj_second - sin_first * proj_cross
    radius_second = jnp.sqrt(rotated_low * rotated_low + height_second * height_second)
    coeff_second = -sin_first * rhs_norm * (rotated_low / radius_second) / radius_second
    coeff_first = (cos_first * rhs_norm - rotated_top * coeff_second) / radius_first
    once = once_in[...]
    start = values[...]
    result[...] = (coeff_first * scale + coeff_second * c0) * start + (coeff_second * c1) * once


def per_device(
    right_side,
    targets,
    source_nodes,
    node_weights,
    near_list,
    near_count,
    row_basis,
    column_basis,
    coupling,
):
    src_count = lax.axis_size("src")
    tgt_count = lax.axis_size("tgt")
    leaf = right_side.shape[0]
    node_rows = node_weights.shape[0]
    rank = row_basis.shape[1]
    slots = near_list.shape[1]
    stacked = src_count * rank
    device_count = src_count * tgt_count
    values = right_side.reshape(1, leaf)
    couplings = coupling.reshape(src_count * tgt_count, 1, rank * rank)
    packed_rows = 4 * node_rows + 8

    basis_rows = 2 * rank + 8
    in_hbm = functools.partial(pltpu.with_memory_space_constraint, memory_space=pltpu.HBM)
    flag_shape = jax.ShapeDtypeStruct((stacked, rank * rank), jnp.bfloat16)
    packed, basis, near, flat, spread_flags, group_flags, values = pl.pallas_call(
        functools.partial(pack_kernel, node_rows=node_rows, rank=rank),
        out_shape=(
            jax.ShapeDtypeStruct((packed_rows, leaf), jnp.float32),
            jax.ShapeDtypeStruct((basis_rows, leaf), jnp.float32),
            jax.ShapeDtypeStruct(near_list.shape, jnp.int32),
            jax.ShapeDtypeStruct((device_count, rank * rank), jnp.float32),
            flag_shape,
            flag_shape,
            jax.ShapeDtypeStruct(values.shape, jnp.float32),
        ),
        in_specs=[hbm_space] * 8,
        out_specs=(vmem_space,) * 7,
        scratch_shapes=[
            pltpu.VMEM(targets.shape, jnp.float32),
            pltpu.VMEM(couplings.shape, jnp.float32),
            pltpu.SemaphoreType.DMA((10,)),
        ],
        compiler_params=kernel_params,
        name="pack",
    )(
        in_hbm(source_nodes),
        in_hbm(node_weights),
        in_hbm(values),
        in_hbm(targets),
        in_hbm(row_basis),
        in_hbm(column_basis),
        in_hbm(near_list),
        in_hbm(couplings),
    )

    group = 2 if tgt_count % 2 == 0 else 1
    lines = tgt_count // group

    def from_line(value, shift):
        pairs = [
            (line * group + core, there * group + core)
            for line, there in partner_pairs(shift, lines)
            for core in range(group)
        ]
        return lax.ppermute(value, "tgt", pairs)

    def from_flip(value):
        return lax.ppermute(value, "tgt", [(tgt, tgt ^ 1) for tgt in range(tgt_count)])

    def from_source(value, shift):
        return lax.ppermute(value, "src", partner_pairs(shift, src_count))

    columns = [packed] + [from_line(packed, shift) for shift in range(1, lines)]
    if group == 2:
        columns = columns + [from_flip(value) for value in columns]
    bases = [basis] + [from_source(basis, shift) for shift in range(1, src_count)]

    sizes = dict(src_count=src_count, tgt_count=tgt_count, rank=rank, leaf=leaf)
    halves = leaf // 128
    stack = stack_rows(src_count, leaf)
    lines_held = -(-(halves + stacked // 128) // 8) * 8
    piece_rows = 2 * halves
    target_rows = max(8, src_count)
    message, tiles, row_bases, row_values, kept = pl.pallas_call(
        functools.partial(first_kernel, node_rows=node_rows, **sizes),
        out_shape=(
            jax.ShapeDtypeStruct((device_count, 1, leaf + stacked), jnp.float32),
            jax.ShapeDtypeStruct((slots, leaf, leaf), jnp.float32),
            jax.ShapeDtypeStruct((stacked, leaf), jnp.float32),
            jax.ShapeDtypeStruct((stack, 128), jnp.float32),
            jax.ShapeDtypeStruct((device_count, rank * rank), jnp.float32),
        ),
        in_specs=[smem_space, smem_space] + [vmem_space] * (3 + tgt_count + src_count),
        out_specs=(vmem_space,) * 5,
        scratch_shapes=[
            pltpu.VMEM((tgt_count, packed_rows, leaf), jnp.float32),
            pltpu.VMEM((stacked, leaf), jnp.float32),
            pltpu.VMEM((3, target_rows, leaf), jnp.float32),
            pltpu.VMEM((halves, term_count * target_rows, 128), jnp.float32),
            pltpu.VMEM((src_count, leaf, term_count), jnp.bfloat16),
            pltpu.VMEM((halves, unique_terms * node_rows, 128), jnp.float32),
            pltpu.VMEM((tgt_count, node_rows, unique_terms, leaf), jnp.bfloat16),
            pltpu.SMEM((tgt_count,), jnp.int32),
            pltpu.VMEM((src_count, leaf, 128), jnp.float32),
            pltpu.VMEM((tgt_count, 128), jnp.float32),
        ],
        compiler_params=pltpu.CompilerParams(
            vmem_limit_bytes=32 * 1024 * 1024,
        ),
        name="first",
    )(near, near_count, flat, spread_flags, group_flags, *columns, *bases)

    received = lax.all_to_all(message, both_axes, 0, 0, tiled=True)

    message, once = pl.pallas_call(
        functools.partial(second_kernel, **sizes),
        out_shape=(
            jax.ShapeDtypeStruct(
                (device_count, stack // piece_rows + 1, piece_rows, 128), jnp.float32
            ),
            jax.ShapeDtypeStruct((1, leaf), jnp.float32),
        ),
        in_specs=[vmem_space, smem_space] + [vmem_space] * 8,
        out_specs=(vmem_space, vmem_space),
        scratch_shapes=[
            pltpu.VMEM((src_count, leaf, 128), jnp.float32),
            pltpu.VMEM((tgt_count * lines_held, 128), jnp.float32),
            pltpu.SMEM(near_list.shape, jnp.int32),
            pltpu.SemaphoreType.DMA,
        ],
        compiler_params=kernel_params,
        name="second",
    )(
        near,
        near_count,
        kept,
        spread_flags,
        group_flags,
        received,
        values,
        row_bases,
        row_values,
        tiles,
    )

    received = lax.all_to_all(message, both_axes, 0, 0, tiled=True)

    result = pl.pallas_call(
        functools.partial(third_kernel, src_count=src_count, tgt_count=tgt_count, leaf=leaf),
        out_shape=jax.ShapeDtypeStruct((1, leaf), jnp.float32),
        in_specs=[vmem_space] * 3,
        out_specs=vmem_space,
        compiler_params=kernel_params,
        name="third",
    )(received, values, once)
    return result.reshape(leaf)


def solution(mesh):
    return jax.shard_map(
        per_device,
        mesh=mesh,
        in_specs=(
            P(("tgt", "src")),
            P(None, ("tgt", "src")),
            P(None, None, ("tgt", "src")),
            P(None, ("tgt", "src")),
            P(None, ("tgt", "src")),
            P(("tgt", "src")),
            P(("tgt", "src"), None, None),
            P(("tgt", "src"), None, None),
            P("tgt", None, None, "src", None),
        ),
        out_specs=P(("tgt", "src")),
        check_vma=False,
    )
```

```python
import functools

import jax
import jax.numpy as jnp
from jax import lax
from jax.experimental import pallas as pl
from jax.experimental.pallas import tpu as pltpu
from jax.sharding import PartitionSpec as P

spread_sq = 0.0004
norm_floor = 1e-06
highest = lax.Precision.HIGHEST
both_axes = ("tgt", "src")
lane_contract = (((1,), (1,)), ((), ()))
plain_contract = (((1,), (0,)), ((), ()))
unique_terms = 16
term_repeats = 4
term_count = unique_terms * term_repeats
vmem_space = pl.BlockSpec(memory_space=pltpu.VMEM)
smem_space = pl.BlockSpec(memory_space=pltpu.SMEM)
hbm_space = pl.BlockSpec(memory_space=pltpu.HBM)
kernel_params = pltpu.CompilerParams(vmem_limit_bytes=32 * 1024 * 1024)


def in_three(value):
    top = value.astype(jnp.bfloat16)
    rest = value - top.astype(jnp.float32)
    middle = rest.astype(jnp.bfloat16)
    low = (rest - middle.astype(jnp.float32)).astype(jnp.bfloat16)
    return top, middle, low


def exact_dot(value, flags, contract):
    rows = value.shape[0]
    parts = jnp.concatenate([part.astype(jnp.float32) for part in in_three(value)], axis=0)
    product = lax.dot_general(
        parts.astype(jnp.bfloat16), flags, contract, preferred_element_type=jnp.float32
    )
    return product[0:rows] + (product[rows : 2 * rows] + product[2 * rows :])


def iota(shape, dim):
    return lax.broadcasted_iota(jnp.int32, shape, dim)


def stack_rows(src_count, leaf):
    return max(8, src_count * (leaf // 128))


def partner(index, shift, count):
    if count & (count - 1) == 0:
        return index ^ shift
    return lax.rem(index - shift + count, count)


def partner_pairs(shift, count):
    if count & (count - 1) == 0:
        return [(place, place ^ shift) for place in range(count)]
    return [(place, (place + shift) % count) for place in range(count)]


def on_grid(value, steps):
    return lax.round(value * steps, lax.RoundingMethod.TO_NEAREST_EVEN) * (1.0 / steps)


def as_bfloat16(value):
    return value.astype(jnp.bfloat16).astype(jnp.float32)


def coordinate_parts(coords):
    parts = []
    for value in coords:
        high = on_grid(value, 128.0)
        rest = value - high
        mid = on_grid(rest, 32768.0)
        parts.append((high, mid, as_bfloat16(rest - mid)))
    return parts


def split_terms(coords, shift):
    parts = coordinate_parts(coords)
    high_sum = sum(high * high for high, mid, low in parts)
    top = as_bfloat16(high_sum)
    rest_sum = sum((mid + low) * (2.0 * high + (mid + low)) for high, mid, low in parts) + shift
    first = as_bfloat16(rest_sum)
    second = as_bfloat16(rest_sum - first)
    return parts, [top, high_sum - top], [first, second, rest_sum - first - second]


def node_side(coords):
    parts, squares, rests = split_terms(coords, 0.0)
    terms = [piece for part in parts for piece in part] + squares + rests
    return dict(enumerate(terms))


def target_side(coords, shift):
    parts, squares, rests = split_terms(coords, shift)
    one = jnp.ones_like(squares[0])
    terms = {}
    for coord, part in enumerate(parts):
        high, mid, low = [-2.0 * piece for piece in part]
        spot = 3 * coord
        terms[spot] = high
        terms[unique_terms + spot] = mid
        terms[2 * unique_terms + spot] = low
        for piece in (1, 2):
            terms[unique_terms + spot + piece] = high
            terms[2 * unique_terms + spot + piece] = mid
            terms[3 * unique_terms + spot + piece] = low
    terms[9] = one
    terms[10] = one
    terms[14] = squares[0]
    terms[15] = squares[1]
    for piece in range(3):
        terms[unique_terms + 11 + piece] = one
    terms[unique_terms + 14] = rests[0]
    terms[unique_terms + 15] = rests[1]
    terms[2 * unique_terms + 14] = rests[2]
    return terms


def store_terms(staged, terms, rows, count, fill):
    for number in range(count):
        for half in range(staged.shape[0]):
            here = pl.ds(number * rows, rows)
            if number in terms:
                staged[half, here, :] = terms[number][:, half * 128 : (half + 1) * 128]
            elif fill is not None:
                staged[half, here, :] = jnp.full((rows, 128), fill, jnp.float32)


def pack_kernel(
    nodes,
    weights,
    values_in,
    targets,
    row_basis,
    column_basis,
    near_in,
    coupling_in,
    packed,
    basis,
    near,
    flat,
    spread_flags,
    group_flags,
    values,
    cleared,
    points,
    coupling,
    sems,
    *,
    node_rows,
    rank,
):
    pieces = [
        (column_basis.at[0], basis.at[pl.ds(rank, rank), :]),
        (values_in, values),
        (targets, points),
        (near_in, near),
        (row_basis.at[0], basis.at[pl.ds(0, rank), :]),
        (weights, packed.at[pl.ds(3 * node_rows, node_rows), :]),
        (coupling_in, coupling),
    ]
    for coord in range(3):
        pieces.append((nodes.at[coord], packed.at[pl.ds(coord * node_rows, node_rows), :]))
    copies = [
        pltpu.make_async_copy(source, place, sems.at[number])
        for number, (source, place) in enumerate(pieces)
    ]
    for copy in copies:
        copy.start()
    leaf = values.shape[1]
    packed[pl.ds(4 * node_rows, 8), :] = jnp.zeros((8, leaf), jnp.float32)
    basis[pl.ds(2 * rank, 8), :] = jnp.zeros((8, leaf), jnp.float32)
    cleared[...] = jnp.zeros_like(cleared)
    shape = spread_flags.shape
    row, lane = iota(shape, 0), iota(shape, 1)
    spread_flags[...] = ((row % rank) == (lane % rank)).astype(jnp.bfloat16)
    group_flags[...] = ((row % rank) == (lane // rank)).astype(jnp.bfloat16)
    for copy in copies[:3]:
        copy.wait()
    vector = values[...]
    packed[pl.ds(4 * node_rows, 1), :] = vector
    tall = jnp.broadcast_to(vector, (8, leaf))
    coeffs = lax.dot_general(
        tall,
        basis[pl.ds(rank, rank), :],
        lane_contract,
        precision=highest,
        preferred_element_type=jnp.float32,
    )
    packed[pl.ds(4 * node_rows + 1, 1), pl.ds(0, rank)] = coeffs[0:1]
    basis[pl.ds(2 * rank, 3), :] = points[...]
    basis[pl.ds(2 * rank + 3, 1), :] = vector
    for copy in copies[3:]:
        copy.wait()
    flat[...] = coupling[:, 0, :]


def far_stack(coeffs, kept, spread_flags, group_flags, row_bases, src_count, tgt_count, rank):
    stacked, leaf = row_bases.shape
    halves = leaf // 128
    rows = stack_rows(src_count, leaf)
    tiled = exact_dot(coeffs, spread_flags[pl.ds(0, coeffs.shape[1]), :], plain_contract)
    row_id = iota((rows, rank * rank), 0) // halves
    summed = jnp.zeros((rows, rank * rank), jnp.float32)
    for target in range(src_count):
        block = kept[pl.ds(target * tgt_count, tgt_count), :]
        total = jnp.sum(block * tiled, axis=0, keepdims=True)
        summed = jnp.where(row_id == target, total, summed)
    far = exact_dot(summed, group_flags[...], lane_contract)
    own = (iota((rows, stacked), 1) // rank) == (iota((rows, stacked), 0) // halves)
    own = own & (iota((rows, stacked), 0) % halves == 0)
    far = jnp.sum(jnp.where(own, far, 0.0), axis=0, keepdims=True)
    lines = []
    for first in range(0, stacked, 128):
        upright = jnp.transpose(jnp.broadcast_to(far[:, first : first + 128], (128, 128)))
        for half in range(halves):
            block = row_bases[pl.ds(first, 128), pl.ds(half * 128, 128)] * upright
            for start in range(0, 128, rank):
                line = jnp.sum(block[start : start + rank], axis=0, keepdims=True)
                lines.append(((first + start) // rank * halves + half, line))
    return stack_lines(lines, rows)


def stack_lines(lines, rows):
    row_id = iota((rows, 128), 0)
    result = jnp.zeros((rows, 128), jnp.float32)
    for number, line in lines:
        result = jnp.where(row_id == number, line, result)
    return result


def near_stack(partial, src_count, leaf):
    halves = leaf // 128
    lines = []
    for target in range(src_count):
        for half in range(halves):
            flat = jnp.transpose(partial[target, pl.ds(half * 128, 128), :])
            lines.append((target * halves + half, jnp.sum(flat, axis=0, keepdims=True)))
    return stack_lines(lines, stack_rows(src_count, leaf))


def clear_partials(partial, src_count):
    for target in range(src_count):
        partial[target] = jnp.zeros(partial.shape[1:], jnp.float32)


def add_product(partial, target, start, size, pieces, vectors):
    total = None
    for piece, vector in zip(pieces, vectors):
        total = piece * vector if total is None else total + piece * vector
    here = pl.ds(start, size)
    partial[target, here, :] = partial[target, here, :] + total


def first_kernel(
    near,
    near_count,
    flat,
    spread_flags,
    group_flags,
    cleared,
    *refs,
    src_count,
    tgt_count,
    node_rows,
    rank,
    leaf,
):
    columns, refs = refs[:tgt_count], refs[tgt_count:]
    bases, refs = refs[:src_count], refs[src_count:]
    message, tiles, row_bases, row_values, kept, partial = refs[:6]
    held, col_bases, point_rows, point_staged, point_terms = refs[6:11]
    node_staged, node_terms, built, far_values = refs[11:]
    tgt_index = lax.axis_index("tgt")
    src_index = lax.axis_index("src")
    halves = leaf // 128
    stacked = src_count * rank
    rows = stack_rows(src_count, leaf)
    for spot in range(tgt_count):
        there = column_place(tgt_index, spot, tgt_count)
        held[there] = columns[spot][...]
        far_values[pl.ds(there, 1), :] = columns[spot][pl.ds(4 * node_rows + 1, 1), pl.ds(0, 128)]
        built[spot] = 0
    for shift in range(src_count):
        there = partner(src_index, shift, src_count)
        here = pl.ds(pl.multiple_of(there * rank, rank), rank)
        row_bases[here, :] = bases[shift][pl.ds(0, rank), :]
        col_bases[here, :] = bases[shift][pl.ds(rank, rank), :]
        for coord in range(3):
            point_rows[coord, pl.ds(there, 1), :] = bases[shift][pl.ds(2 * rank + coord, 1), :]
        for half in range(halves):
            row_values[pl.ds(there * halves + half, 1), :] = bases[shift][
                pl.ds(2 * rank + 3, 1), pl.ds(half * 128, 128)
            ]
    ones_here = pl.ds((unique_terms - 2) * node_rows, 2 * node_rows)
    node_staged[:, ones_here, :] = jnp.ones((halves, 2 * node_rows, 128), jnp.float32)
    coords = [point_rows[coord] for coord in range(3)]
    target_rows = point_rows.shape[1]
    store_terms(point_staged, target_side(coords, spread_sq), target_rows, term_count, 0.0)
    for target in range(src_count):
        for half in range(halves):
            across = point_staged[half, pl.ds(target, term_count, stride=target_rows), :]
            point_terms[target, pl.ds(half * 128, 128), :] = jnp.transpose(across).astype(
                jnp.bfloat16
            )
    block = 128

    live = near_count[0]
    slots = tiles.shape[0]
    together = 2 if slots % 2 == 0 else 1

    def some_slots(number, carry):
        numbers = [number * together + offset for offset in range(together)]
        places = []
        for slot in numbers:
            target, source = near[0, slot] - tgt_index * src_count, near[1, slot] // src_count
            places.append((slot, target, source))

            @pl.when(slot < live)
            def _():
                row = pl.ds(target * tgt_count + source, 1)
                kept[row, :] = jnp.zeros((1, kept.shape[1]), jnp.float32)

            @pl.when(built[source] == 0)
            def _():
                built[source] = 1
                coords = [held[source, pl.ds(coord * node_rows, node_rows), :] for coord in range(3)]
                store_terms(node_staged, node_side(coords), node_rows, unique_terms, None)
                for node in range(node_rows):
                    for half in range(halves):
                        across = node_staged[half, pl.ds(node, unique_terms, stride=node_rows), :]
                        lanes = pl.ds(half * 128, 128)
                        node_terms[source, node, :, lanes] = across.astype(jnp.bfloat16)

        for slot, target, source in places:
            weight = (slot < live).astype(jnp.float32)
            vectors = [
                weight * held[source, pl.ds(4 * node_rows, 1), pl.ds(half * 128, 128)]
                for half in range(halves)
            ]
            for start in range(0, leaf, block):
                here = pl.ds(start, block)
                lhs = point_terms[target, here, :]
                tile = None
                for node in range(node_rows):
                    rhs = jnp.concatenate([node_terms[source, node]] * term_repeats, axis=0)
                    square = lax.dot_general(
                        lhs, rhs, plain_contract, preferred_element_type=jnp.float32
                    )
                    term = held[source, pl.ds(3 * node_rows + node, 1), :] * lax.rsqrt(square)
                    tile = term if tile is None else tile + term
                tiles[slot, here, :] = tile
                pieces = [tile[:, half * 128 : (half + 1) * 128] for half in range(halves)]
                add_product(partial, target, start, block, pieces, vectors)
        return carry

    lax.fori_loop(0, (live + together - 1) // together, some_slots, 0)
    total = near_stack(partial, src_count, leaf) + far_stack(
        far_values[...], kept, spread_flags, group_flags, row_bases, src_count, tgt_count, rank
    )
    coeffs = []
    for first in range(0, stacked, 128):
        blocks = []
        for start in range(first, first + 128, rank):
            target = start // rank
            block = None
            for half in range(halves):
                line = total[target * halves + half : target * halves + half + 1]
                piece = col_bases[pl.ds(start, rank), pl.ds(half * 128, 128)] * line
                block = piece if block is None else block + piece
            blocks.append(block)
        flat = jnp.transpose(jnp.concatenate(blocks, axis=0))
        coeffs.append(jnp.sum(flat, axis=0, keepdims=True))
    for target in range(src_count):
        lines = [total[target * halves + half : target * halves + half + 1] for half in range(halves)]
        for number, line in enumerate(lines + coeffs):
            for there in range(tgt_count):
                message[there * src_count + target, :, pl.ds(number * 128, 128)] = line


def column_place(tgt_index, spot, tgt_count):
    group = 2 if tgt_count % 2 == 0 else 1
    lines = tgt_count // group
    shift, flip = spot % lines, spot // lines
    return partner(tgt_index // group, shift, lines) * group + lax.rem(
        tgt_index % group + flip, group
    )


def second_kernel(
    near_in,
    near_count,
    kept,
    spread_flags,
    group_flags,
    received,
    values,
    row_bases,
    row_values,
    tiles,
    message,
    once_out,
    partial,
    image,
    near,
    near_sem,
    *,
    src_count,
    tgt_count,
    rank,
    leaf,
):
    tgt_index = lax.axis_index("tgt")
    src_index = lax.axis_index("src")
    halves = leaf // 128
    stacked = src_count * rank
    rows = stack_rows(src_count, leaf)
    lines = image.shape[0] // tgt_count
    near_copy = pltpu.make_async_copy(near_in, near, near_sem)
    near_copy.start()
    clear_partials(partial, src_count)
    for there in range(tgt_count):
        for number in range(halves + stacked // 128):
            lanes = pl.ds(number * 128, 128)
            total = received[there * src_count, :, lanes]
            for source in range(1, src_count):
                total = total + received[there * src_count + source, :, lanes]
            image[pl.ds(there * lines + number, 1), :] = total

    near_copy.wait()

    def one_slot(slot, carry):
        target, source = near[0, slot] - tgt_index * src_count, near[1, slot] // src_count
        vectors = [image[pl.ds(source * lines + half, 1), :] for half in range(halves)]
        block = 64
        for start in range(0, leaf, block):
            here = pl.ds(start, block)
            pieces = [tiles[slot, here, pl.ds(half * 128, 128)] for half in range(halves)]
            add_product(partial, target, start, block, pieces, vectors)
        return carry

    lax.fori_loop(0, near_count[0], one_slot, 0)
    coeffs = jnp.concatenate(
        [
            image[pl.ds(halves + piece, tgt_count, stride=lines), :]
            for piece in range(stacked // 128)
        ],
        axis=1,
    )
    mine = (iota((tgt_count, stacked), 1) // rank) == src_index
    coeffs = jnp.where(mine, coeffs, 0.0)
    twice = near_stack(partial, src_count, leaf) + far_stack(
        coeffs, kept, spread_flags, group_flags, row_bases, src_count, tgt_count, rank
    )
    once = [image[pl.ds(tgt_index * lines + half, 1), :] for half in range(halves)]
    start = [values[:, pl.ds(half * 128, 128)] for half in range(halves)]
    for half in range(halves):
        once_out[:, pl.ds(half * 128, 128)] = once[half]

    def inner(left, right):
        total = sum(one * other for one, other in zip(left, right))
        return jnp.sum(total, axis=1, keepdims=True)

    cross = jnp.sum(row_values[...] * twice, axis=0, keepdims=True)
    scalars = [inner(start, start), inner(start, once), jnp.sum(cross, axis=1, keepdims=True)]
    lane_id = iota((1, 128), 1)
    line = jnp.zeros((1, 128), jnp.float32)
    for number, value in enumerate(scalars):
        line = jnp.where(lane_id == number, value, line)
    piece_rows = message.shape[2]
    share = piece_rows // halves
    row_id = iota((piece_rows, 128), 0)
    spare = lax.rem(src_index + 1, share) * halves
    extra = jnp.where(row_id == spare, line, 0.0)
    for half in range(halves):
        extra = jnp.where(row_id == lax.rem(src_index, share) * halves + half, once[half], extra)
    pieces = [twice[first : first + piece_rows] for first in range(0, rows, piece_rows)]
    for there in range(src_count * tgt_count):
        for number, piece in enumerate(pieces + [extra]):
            message[there, number] = piece


def third_kernel(received, values, once_in, result, *, src_count, tgt_count, leaf):
    halves = leaf // 128
    piece_rows = received.shape[2]
    share = piece_rows // halves
    row_id = iota((piece_rows, 128), 0)
    s11 = s12 = s22 = scalars = jnp.zeros((piece_rows, 128), jnp.float32)
    for there in range(tgt_count):
        for piece in range(src_count // share):
            twice = once = None
            for source in range(src_count):
                part = received[there * src_count + source, piece]
                twice = part if twice is None else twice + part
            for spot in range(share):
                extra = received[there * src_count + piece * share + spot, received.shape[1] - 1]
                mine = row_id // halves == spot
                once = extra if once is None else jnp.where(mine, extra, once)
                spare = row_id == ((spot + 1) % share) * halves
                scalars = scalars + jnp.where(spare, extra, 0.0)
            s11 = s11 + once * once
            s12 = s12 + once * twice
            s22 = s22 + twice * twice

    def whole(value):
        return jnp.sum(jnp.sum(value, axis=0, keepdims=True), axis=1, keepdims=True)

    g11, g12, g22 = whole(s11), whole(s12), whole(s22)
    scalars = jnp.sum(scalars, axis=0, keepdims=True)
    g00, g01, g02 = [scalars[:, number : number + 1] for number in range(3)]
    rhs_norm = jnp.sqrt(g00 + norm_floor)
    scale = 1.0 / rhs_norm
    proj_first = scale * scale * (0.5 * g00 + g01)
    left = 0.5 - proj_first
    rest_sq = scale * scale * (left * left * g00 + 2.0 * left * g01 + g11)
    height_first = jnp.sqrt(jnp.maximum(rest_sq, 0.0) + norm_floor)
    c1 = scale / height_first
    c0 = left * c1
    i0 = 0.5 * c0
    i1 = 0.5 * c1 + c0
    i2 = c1
    to_start = i0 * g00 + i1 * g01 + i2 * g02
    to_once = i0 * g01 + i1 * g11 + i2 * g12
    proj_cross = scale * to_start
    proj_second = c0 * to_start + c1 * to_once
    r0 = i0 - proj_cross * scale - proj_second * c0
    r1 = i1 - proj_second * c1
    r2 = i2
    last_sq = (
        r0 * (r0 * g00 + 2.0 * (r1 * g01 + r2 * g02))
        + r1 * (r1 * g11 + 2.0 * r2 * g12)
        + r2 * r2 * g22
    )
    height_second = jnp.sqrt(jnp.maximum(last_sq, 0.0) + norm_floor)
    radius_first = jnp.sqrt(proj_first * proj_first + height_first * height_first)
    cos_first = proj_first / radius_first
    sin_first = height_first / radius_first
    rotated_top = cos_first * proj_cross + sin_first * proj_second
    rotated_low = cos_first * proj_second - sin_first * proj_cross
    radius_second = jnp.sqrt(rotated_low * rotated_low + height_second * height_second)
    coeff_second = -sin_first * rhs_norm * (rotated_low / radius_second) / radius_second
    coeff_first = (cos_first * rhs_norm - rotated_top * coeff_second) / radius_first
    once = once_in[...]
    start = values[...]
    result[...] = (coeff_first * scale + coeff_second * c0) * start + (coeff_second * c1) * once


def per_device(
    right_side,
    targets,
    source_nodes,
    node_weights,
    near_list,
    near_count,
    row_basis,
    column_basis,
    coupling,
):
    src_count = lax.axis_size("src")
    tgt_count = lax.axis_size("tgt")
    leaf = right_side.shape[0]
    node_rows = node_weights.shape[0]
    rank = row_basis.shape[1]
    slots = near_list.shape[1]
    stacked = src_count * rank
    device_count = src_count * tgt_count
    values = right_side.reshape(1, leaf)
    couplings = coupling.reshape(src_count * tgt_count, 1, rank * rank)
    packed_rows = 4 * node_rows + 8

    basis_rows = 2 * rank + 8
    in_hbm = functools.partial(pltpu.with_memory_space_constraint, memory_space=pltpu.HBM)
    flag_shape = jax.ShapeDtypeStruct((stacked, rank * rank), jnp.bfloat16)
    packed, basis, near, flat, spread_flags, group_flags, values, cleared = pl.pallas_call(
        functools.partial(pack_kernel, node_rows=node_rows, rank=rank),
        out_shape=(
            jax.ShapeDtypeStruct((packed_rows, leaf), jnp.float32),
            jax.ShapeDtypeStruct((basis_rows, leaf), jnp.float32),
            jax.ShapeDtypeStruct(near_list.shape, jnp.int32),
            jax.ShapeDtypeStruct((device_count, rank * rank), jnp.float32),
            flag_shape,
            flag_shape,
            jax.ShapeDtypeStruct(values.shape, jnp.float32),
            jax.ShapeDtypeStruct((src_count, leaf, 128), jnp.float32),
        ),
        in_specs=[hbm_space] * 8,
        out_specs=(vmem_space,) * 8,
        scratch_shapes=[
            pltpu.VMEM(targets.shape, jnp.float32),
            pltpu.VMEM(couplings.shape, jnp.float32),
            pltpu.SemaphoreType.DMA((10,)),
        ],
        compiler_params=kernel_params,
        name="pack",
    )(
        in_hbm(source_nodes),
        in_hbm(node_weights),
        in_hbm(values),
        in_hbm(targets),
        in_hbm(row_basis),
        in_hbm(column_basis),
        in_hbm(near_list),
        in_hbm(couplings),
    )

    group = 2 if tgt_count % 2 == 0 else 1
    lines = tgt_count // group

    def from_line(value, shift):
        pairs = [
            (line * group + core, there * group + core)
            for line, there in partner_pairs(shift, lines)
            for core in range(group)
        ]
        return lax.ppermute(value, "tgt", pairs)

    def from_flip(value):
        return lax.ppermute(value, "tgt", [(tgt, tgt ^ 1) for tgt in range(tgt_count)])

    def from_source(value, shift):
        return lax.ppermute(value, "src", partner_pairs(shift, src_count))

    columns = [packed] + [from_line(packed, shift) for shift in range(1, lines)]
    if group == 2:
        columns = columns + [from_flip(value) for value in columns]
    bases = [basis] + [from_source(basis, shift) for shift in range(1, src_count)]

    sizes = dict(src_count=src_count, tgt_count=tgt_count, rank=rank, leaf=leaf)
    halves = leaf // 128
    stack = stack_rows(src_count, leaf)
    lines_held = -(-(halves + stacked // 128) // 8) * 8
    piece_rows = 2 * halves
    target_rows = max(8, src_count)
    message, tiles, row_bases, row_values, kept, _ = pl.pallas_call(
        functools.partial(first_kernel, node_rows=node_rows, **sizes),
        out_shape=(
            jax.ShapeDtypeStruct((device_count, 1, leaf + stacked), jnp.float32),
            jax.ShapeDtypeStruct((slots, leaf, leaf), jnp.float32),
            jax.ShapeDtypeStruct((stacked, leaf), jnp.float32),
            jax.ShapeDtypeStruct((stack, 128), jnp.float32),
            jax.ShapeDtypeStruct((device_count, rank * rank), jnp.float32),
            jax.ShapeDtypeStruct((src_count, leaf, 128), jnp.float32),
        ),
        in_specs=[smem_space, smem_space] + [vmem_space] * (4 + tgt_count + src_count),
        out_specs=(vmem_space,) * 6,
        input_output_aliases={2: 4, 5: 5},
        scratch_shapes=[
            pltpu.VMEM((tgt_count, packed_rows, leaf), jnp.float32),
            pltpu.VMEM((stacked, leaf), jnp.float32),
            pltpu.VMEM((3, target_rows, leaf), jnp.float32),
            pltpu.VMEM((halves, term_count * target_rows, 128), jnp.float32),
            pltpu.VMEM((src_count, leaf, term_count), jnp.bfloat16),
            pltpu.VMEM((halves, unique_terms * node_rows, 128), jnp.float32),
            pltpu.VMEM((tgt_count, node_rows, unique_terms, leaf), jnp.bfloat16),
            pltpu.SMEM((tgt_count,), jnp.int32),
            pltpu.VMEM((tgt_count, 128), jnp.float32),
        ],
        compiler_params=pltpu.CompilerParams(
            vmem_limit_bytes=32 * 1024 * 1024,
        ),
        name="first",
    )(near, near_count, flat, spread_flags, group_flags, cleared, *columns, *bases)

    received = lax.all_to_all(message, both_axes, 0, 0, tiled=True)

    message, once = pl.pallas_call(
        functools.partial(second_kernel, **sizes),
        out_shape=(
            jax.ShapeDtypeStruct(
                (device_count, stack // piece_rows + 1, piece_rows, 128), jnp.float32
            ),
            jax.ShapeDtypeStruct((1, leaf), jnp.float32),
        ),
        in_specs=[vmem_space, smem_space] + [vmem_space] * 8,
        out_specs=(vmem_space, vmem_space),
        scratch_shapes=[
            pltpu.VMEM((src_count, leaf, 128), jnp.float32),
            pltpu.VMEM((tgt_count * lines_held, 128), jnp.float32),
            pltpu.SMEM(near_list.shape, jnp.int32),
            pltpu.SemaphoreType.DMA,
        ],
        compiler_params=kernel_params,
        name="second",
    )(
        near,
        near_count,
        kept,
        spread_flags,
        group_flags,
        received,
        values,
        row_bases,
        row_values,
        tiles,
    )

    received = lax.all_to_all(message, both_axes, 0, 0, tiled=True)

    result = pl.pallas_call(
        functools.partial(third_kernel, src_count=src_count, tgt_count=tgt_count, leaf=leaf),
        out_shape=jax.ShapeDtypeStruct((1, leaf), jnp.float32),
        in_specs=[vmem_space] * 3,
        out_specs=vmem_space,
        compiler_params=kernel_params,
        name="third",
    )(received, values, once)
    return result.reshape(leaf)


def solution(mesh):
    return jax.shard_map(
        per_device,
        mesh=mesh,
        in_specs=(
            P(("tgt", "src")),
            P(None, ("tgt", "src")),
            P(None, None, ("tgt", "src")),
            P(None, ("tgt", "src")),
            P(None, ("tgt", "src")),
            P(("tgt", "src")),
            P(("tgt", "src"), None, None),
            P(("tgt", "src"), None, None),
            P("tgt", None, None, "src", None),
        ),
        out_specs=P(("tgt", "src")),
        check_vma=False,
    )
```
